128 devices in a mesh: req: 16 (over x, z), exp: 8 (over y, core).
Axes of the slice: x: 4, y: 4, z: 4, core: 2. Of those that a mesh axis runs over, the one named last changes fastest.
Arguments:
- tokens: bfloat16 [16384, 2048], P('req'), may hold values from -40 to 40
- routes: int32 [16384, 2], P('req'), may hold values from 0 to 7, all different within a row; in each aligned block of 1024 rows (0 to 1023, 1024 to 2047, ...) at most 320 rows name the same one
- lengths: int32 [64], P('req'), may hold values from 1 to 256, 8192 in all
- cached_prefix_length: int32 [64], P('req'), may hold values from 0 to 64, as said below
- prefix_cache_row: int32 [64], replicated, may hold values from 0 to 15, as said below
- adapter_per_request: int32 [64], P('req'), may hold values from 0 to 63
- adapter_storage_slot: int32 [64], replicated, may hold values from 0 to 63, each once
- router_weight: bfloat16 [2048, 8], replicated, may hold values from -0.125 to 0.125
- key_value_weight: bfloat16 [2048, 4096], P('req', 'exp'), may hold values from -0.125 to 0.125
- expert_query_weight: bfloat16 [2048, 8, 2048], P('req', None, 'exp'), may hold values from -0.125 to 0.125
- expert_output_weight: bfloat16 [8, 2048, 2048], P(None, 'exp', 'req'), may hold values from -0.125 to 0.125
- adapter_down_maps: bfloat16 [64, 2048, 16], P('req'), may hold values from -0.125 to 0.125
- adapter_up_maps: bfloat16 [64, 16, 4096], P('req', None, 'exp'), may hold values from -1.5 to 1.5
- prefix_cache_store: bfloat16 [64, 64, 4096], P('req', None, 'exp'), may hold values from -6 to 6
Outputs:
- attention_out: bfloat16 [16384, 2048], P('req', 'exp')
The draws below stay inside these ranges and needn't reach their ends.
Inputs may be any that keep to these rules, and one draw needn't show every extreme that they name: `routes`: in each aligned block of 1024 rows (one group) no expert is named by more than 320 rows, and one is named by exactly 320. The lengths sum to 8192 and some request has exactly 256. `cached_prefix_length`: exactly 32 requests have no cached prefix; some request has exactly 64. `prefix_cache_row`: request j of a group keeps its cache in slot j of its row; each row holds exactly one cache in each slot, and no row holds two caches of one group. `adapter_storage_slot`: each slot holds one adapter.
All inputs are finite; a program needn't handle non-finite values. No bound on the sum of `lengths` on one device may be relied on, other than what follows from the above.
Results may differ from the reference program's by a relative error of at most 0.017.
The reference program's roundings to bfloat16 on the way count: a program that leaves them out, or rounds other values in their place, can miss the bound.
Values may be sent and summed in bfloat16 or wider, within the bound.
No kernel may reach another device: no remote copies, remote signals or barrier semaphores. Data moves between devices by JAX's collectives and lax.ppermute only.
A program may use at most 128 MiB of HBM per device.

```python
import math
import jax
import jax.numpy as jnp
import numpy as np
from jax import lax

MODEL_DIM = 2048
KVH = 16
HD = 128
NE = 8
TOPK = 2
ADAPTER_COUNT = 64
ADAPTER_RANK = 16
CACHE = 64
REQ_GROUP = 4
TOK_REQ = 256
QW = 2048
KEY_VALUE_WIDTH = 4096
GROUP_TOKENS = 1024
CAP = 320
REQS = 64
TOKENS = 16384
N_REQ = 16
N_EXP = 8


def draw_tokens(key, part):
    first = jax.random.fold_in(key, 0)
    values = jax.random.normal(first, (TOKENS, MODEL_DIM), jnp.float32)
    values = jnp.clip(values, -6.0, 6.0)
    return values.astype(jnp.bfloat16)


def draw_cached_prefix_length(key, part):
    first, second = jax.random.split(jax.random.fold_in(key, 11))
    drawn = jax.random.randint(first, (REQS,), 1, CACHE + 1, dtype=jnp.int32)
    order = jax.random.permutation(second, REQS).astype(jnp.int32)
    position = jnp.zeros((REQS,), jnp.int32).at[order].set(jnp.arange(REQS, dtype=jnp.int32))
    drawn = jnp.where(position < REQS // 2, 0, drawn)
    drawn = jnp.where(position == REQS - 1, CACHE, drawn)
    return drawn.astype(jnp.int32)


def draw_prefix_cache_row(key, part):
    first, second = jax.random.split(jax.random.fold_in(key, 23))
    group_shift = jax.random.permutation(first, N_REQ).astype(jnp.int32)
    slot_shift = jax.random.permutation(second, N_REQ).astype(jnp.int32)[:REQ_GROUP]
    holder = (group_shift[:, None] + slot_shift[None, :]) % N_REQ
    return holder.reshape(REQS).astype(jnp.int32)


def place_ends(entries, stream_key, least, top_value):
    dims = entries.shape
    index_at = [jax.random.randint(jax.random.fold_in(stream_key, axis), (), 0, dims[axis]) for axis in range(len(dims))]
    entries = entries.at[tuple(index_at)].set(least)
    longest = dims.index(max(dims))
    index_at[longest] = (index_at[longest] + 1) % dims[longest]
    return entries.at[tuple(index_at)].set(top_value)


def steps_of(rng, dims, pieces, low, top_value):
    def one(dim, parts):
        draws = jax.random.uniform(jax.random.fold_in(jax.random.fold_in(rng, 6), dim), (parts,), jnp.float32, low / len(pieces), top_value / len(pieces))
        return jnp.repeat(jnp.exp(draws), dims[dim] // parts).reshape((-1,) + (1,) * (len(dims) - dim - 1))

    level = one(*pieces[0])
    for cut in pieces[1:]:
        level = level * one(*cut)
    return level


def split_up(number_of, total, most, lean):
    weights = [(1 << 20) // math.isqrt(grade ** lean) + 1 for grade in range(2, number_of + 1)]
    spare, holding = total - most - (number_of - 1), [1] * (number_of - 1)
    while spare > 0:
        candidates = [i for i in range(number_of - 1) if holding[i] < most]
        whole, budget = sum([weights[i] for i in candidates]), spare
        for i in candidates:
            addition = min(most - holding[i], max(1, budget * weights[i] // whole), spare)
            holding[i] = holding[i] + addition
            spare = spare - addition
    return np.array([most] + holding)


def uneven_parts(rng, amount, total, bound, lean):
    if amount == 2:
        one = jax.random.randint(rng, (), max(1, total - bound), min(bound, total - 1) + 1)
        return jnp.stack([one, total - one])
    tallies = jnp.asarray(split_up(amount, total, bound, lean), jnp.int32)
    pairs = (amount - 1) // 2
    giver, taker = tallies[1:1 + 2 * pairs:2], tallies[2:2 + 2 * pairs:2]
    margin = jnp.minimum(giver - 1, bound - taker)
    moved = jax.random.randint(jax.random.fold_in(rng, 1), (pairs,), 0, 1 << 20) % (margin + 1)
    tallies = tallies.at[1:1 + 2 * pairs:2].set(giver - moved).at[2:2 + 2 * pairs:2].set(taker + moved)
    return tallies[jax.random.permutation(jax.random.fold_in(rng, 2), amount)]


def assign_block(key, own, number, rows, amount, top, reach, lean):
    sequence = jax.random.permutation(key, amount)
    heavy_load, ordinary = shares(amount, rows * top, reach, lean, True), shares(amount, rows * top, reach, lean, False)
    places = jnp.arange(amount)

    def named(sizes, offset_by):
        used = int((sizes > 0).sum())
        fixed = max(1, used // 4)
        moved = fixed + (places - fixed + offset_by * (used - fixed)) % max(1, amount - fixed)
        return jnp.zeros((amount,), jnp.int32).at[sequence[jnp.where(places < fixed, places, moved)]].set(jnp.asarray(sizes, jnp.int32))

    sizes = jnp.where(number % 4 == 0, named(heavy_load, number // 4), named(ordinary, number - number // 4 - 1))
    mixed = jax.random.permutation(jax.random.fold_in(own, 3), amount)
    donor, sink = mixed[0:amount // 2 * 2:2], mixed[1:amount // 2 * 2:2]
    slack = jnp.minimum(sizes[donor] - 1, reach - sizes[sink]) // 2
    slack = jnp.where((donor == sequence[0]) | (sink == sequence[0]) | (sizes[sink] == 0), 0, jnp.maximum(slack, 0))
    moved = jax.random.randint(jax.random.fold_in(own, 4), (amount // 2,), 0, 1 << 20) % (slack + 1)
    sizes = sizes.at[donor].add(-moved).at[sink].add(moved)
    items = jnp.searchsorted(jnp.cumsum(sizes), jnp.arange(rows * top), side="right").astype(jnp.int32)
    listing = items.reshape(top, rows).T
    listing = listing[jax.random.permutation(jax.random.fold_in(own, 1), rows)]
    offset_by = jax.random.randint(jax.random.fold_in(own, 2), (rows, 1), 0, top)
    return jnp.take_along_axis(listing, (jnp.arange(top)[None, :] + offset_by) % top, axis=1)


def shares(number_of, total, bound, slope, full):
    portions = [(1 << 20) // math.isqrt(rank ** slope) + 1 for rank in range(1, number_of + 1)]
    largest = bound if full else min(bound, max(-(-total // number_of), total * portions[0] // sum(portions)))
    least = 1 if total - largest >= number_of - 1 else 0
    holding, spare = [largest] + [least] * (number_of - 1), total - largest - least * (number_of - 1)
    while spare > 0:
        candidates = [i for i in range(1, number_of) if holding[i] < largest] or [i for i in range(1, number_of) if holding[i] < bound]
        pool, remaining = sum([portions[i] for i in candidates]), spare
        for i in candidates:
            addition = min(bound - holding[i], max(1, remaining * portions[i] // pool), spare)
            holding[i] = holding[i] + addition
            spare = spare - addition
    return np.array(holding)


def centred(stream_key, shape, deviation, most, pieces=(), kind=jnp.bfloat16):
    values = jax.random.normal(stream_key, shape, jnp.float32) * deviation
    if len(pieces) > 0:
        values = steps_of(stream_key, shape, pieces, -0.22, 0.18) * values
    return jnp.clip(values, min=-most, max=most).astype(kind)


def setup_inputs(seed: int = 0) -> dict:
    arg_keys = jax.random.split(jax.random.key(seed), 15)
    tokens = draw_tokens(jax.random.fold_in(arg_keys[14], 71), 0)
    routes_keys = jax.random.split(jax.random.fold_in(arg_keys[1], 1), TOKENS // GROUP_TOKENS)
    routes_turns = jax.random.permutation(jax.random.fold_in(arg_keys[1], 3), TOKENS // GROUP_TOKENS)
    routes = jax.vmap(lambda own, number: assign_block(jax.random.fold_in(arg_keys[1], 2), own, number, GROUP_TOKENS, NE, TOPK, CAP, 2))(routes_keys, routes_turns).reshape((TOKENS, TOPK))
    lengths = uneven_parts(arg_keys[2], REQS, REQS * TOK_REQ // 2, TOK_REQ, 2).astype(jnp.int32)
    cached_prefix_length = draw_cached_prefix_length(jax.random.fold_in(arg_keys[14], 71), 0)
    prefix_cache_row = draw_prefix_cache_row(jax.random.fold_in(arg_keys[14], 71), 0)
    adapter_per_request = place_ends(jax.random.randint(arg_keys[5], (REQS,), 0, ADAPTER_COUNT), jax.random.fold_in(arg_keys[5], 1), 0, ADAPTER_COUNT - 1).astype(jnp.int32)
    adapter_storage_slot = jax.random.permutation(arg_keys[6], ADAPTER_COUNT).astype(jnp.int32)
    router_weight = centred(arg_keys[7], (MODEL_DIM, NE), MODEL_DIM ** -0.5, 0.125)
    key_value_weight = centred(arg_keys[8], (MODEL_DIM, KEY_VALUE_WIDTH), MODEL_DIM ** -0.5, 0.125, ((0, 16), (1, 8)))
    expert_query_weight = centred(arg_keys[9], (MODEL_DIM, NE, QW), MODEL_DIM ** -0.5, 0.125, ((0, 16), (2, 8)))
    expert_output_weight = centred(arg_keys[10], (NE, QW, MODEL_DIM), QW ** -0.5, 0.125, ((1, 8), (2, 16)))
    adapter_down_maps = centred(arg_keys[11], (ADAPTER_COUNT, MODEL_DIM, ADAPTER_RANK), MODEL_DIM ** -0.5, 0.125, ((0, 16),))
    adapter_up_maps = centred(arg_keys[12], (ADAPTER_COUNT, ADAPTER_RANK, KEY_VALUE_WIDTH), ADAPTER_RANK ** -0.5, 1.5, ((0, 16), (2, 8)))
    prefix_cache_store = centred(arg_keys[13], (REQS, CACHE, KEY_VALUE_WIDTH), 1.0, 6.0, ((0, 16), (2, 8)))
    return {"tokens": tokens, "routes": routes, "lengths": lengths, "cached_prefix_length": cached_prefix_length, "prefix_cache_row": prefix_cache_row, "adapter_per_request": adapter_per_request, "adapter_storage_slot": adapter_storage_slot, "router_weight": router_weight, "key_value_weight": key_value_weight, "expert_query_weight": expert_query_weight, "expert_output_weight": expert_output_weight, "adapter_down_maps": adapter_down_maps, "adapter_up_maps": adapter_up_maps, "prefix_cache_store": prefix_cache_store}


adapter_scale = 0.5


def compact(routes):
    route_flat = routes.reshape(-1)
    pair_count = route_flat.shape[0]
    one_hot = (route_flat[:, None] == jnp.arange(NE, dtype=jnp.int32)[None, :]).astype(jnp.int32)
    earlier = jnp.cumsum(one_hot, axis=0) - one_hot
    route_rank = jnp.sum(earlier * one_hot, axis=1).astype(jnp.int32)
    slot_table = jnp.zeros((NE, CAP), jnp.int32).at[route_flat, route_rank].set(jnp.arange(pair_count, dtype=jnp.int32))
    return route_flat, route_rank, slot_table


def attend(queries, all_keys, cached_prefix_length):
    per_request = queries.shape[1]
    key_span = all_keys.shape[1]
    cached = key_span - per_request
    scores = jnp.einsum('rtjhd,rshd->rhtjs', queries.astype(jnp.float32), all_keys[:, :, :, 0, :].astype(jnp.float32)) * (queries.shape[-1] ** -0.5)
    key_place = jnp.arange(key_span, dtype=jnp.int32)
    query_place = jnp.arange(per_request, dtype=jnp.int32)
    from_cache = key_place[None, :] < cached_prefix_length[:, None]
    from_prompt = (key_place[None, :] >= cached) & (key_place[None, :] - cached <= query_place[:, None])
    allowed = jnp.where(key_place[None, None, :] < cached, from_cache[:, None, :], from_prompt[None, :, :])
    allowed = allowed[:, None, :, None, :]
    row_max = jnp.max(jnp.where(allowed, scores, -jnp.inf), axis=-1, keepdims=True)
    weights = jnp.where(allowed, jnp.exp(scores - row_max), 0.0)
    probability = (weights / jnp.sum(weights, axis=-1, keepdims=True)).astype(jnp.bfloat16)
    return jnp.einsum('rhtjs,rshd->rtjhd', probability.astype(jnp.float32), all_keys[:, :, :, 1, :].astype(jnp.float32)).astype(jnp.bfloat16)


def reference(tokens, routes, lengths, cached_prefix_length, prefix_cache_row, adapter_per_request, adapter_storage_slot, router_weight, key_value_weight, expert_query_weight, expert_output_weight, adapter_down_maps, adapter_up_maps, prefix_cache_store):
    head_width = QW // N_EXP

    def one_group(inputs):
        group_tokens, group_routes, group_lengths, group_cache, group_rows, group_adapters = inputs
        key_value_base = jnp.dot(group_tokens, key_value_weight, preferred_element_type=jnp.float32)
        selected_slot = adapter_storage_slot[group_adapters]
        selected_down_map = adapter_down_maps[selected_slot].astype(jnp.float32)
        selected_up_map = adapter_up_maps[selected_slot].astype(jnp.float32)
        by_request = group_tokens.reshape(REQ_GROUP, TOK_REQ, MODEL_DIM).astype(jnp.float32)
        reduced_rank_state = jnp.einsum('rtd,rdq->rtq', by_request, selected_down_map).astype(jnp.bfloat16)
        adapter_term = jnp.einsum('mdg,mgy->mdy', reduced_rank_state.astype(jnp.float32), selected_up_map).reshape(GROUP_TOKENS, KEY_VALUE_WIDTH)
        fresh_key_value = (key_value_base + adapter_scale * adapter_term).astype(jnp.bfloat16)
        stored = prefix_cache_store[group_rows * REQ_GROUP + jnp.arange(REQ_GROUP, dtype=jnp.int32)]
        all_keys = jnp.concatenate([stored, fresh_key_value.reshape(REQ_GROUP, TOK_REQ, KEY_VALUE_WIDTH)], axis=1)
        all_keys = all_keys.reshape(REQ_GROUP, CACHE + TOK_REQ, KVH, 2, HD)
        route_flat, route_rank, slot_table = compact(group_routes)
        picked = group_tokens[slot_table // 2]
        query_blocks = jnp.stack([jnp.dot(picked[expert], expert_query_weight[:, expert, :], preferred_element_type=jnp.float32) for expert in range(NE)]).astype(jnp.bfloat16)
        queries = query_blocks[route_flat, route_rank].reshape(REQ_GROUP, TOK_REQ, TOPK, KVH, HD)
        attended = attend(queries, all_keys, group_cache)
        gathered = attended.reshape(TOPK * GROUP_TOKENS, QW)[slot_table]
        logits = jnp.dot(group_tokens, router_weight, preferred_element_type=jnp.float32)
        route_hot = (group_routes[:, :, None] == jnp.arange(NE, dtype=jnp.int32)[None, None, :]).astype(jnp.float32)
        chosen = jnp.sum(route_hot * logits[:, None, :], axis=-1)
        gate_values = jax.nn.sigmoid(chosen - chosen[:, ::-1])
        live_rows = (jnp.arange(TOK_REQ, dtype=jnp.int32)[None, :] < group_lengths[:, None]).reshape(GROUP_TOKENS).astype(jnp.float32)
        head_total = jnp.zeros((GROUP_TOKENS, MODEL_DIM), jnp.float32)
        for head_part in range(N_EXP):
            col_start = head_part * head_width
            out_blocks = jnp.stack([jnp.dot(gathered[expert, :, col_start:col_start + head_width], expert_output_weight[expert, col_start:col_start + head_width, :], preferred_element_type=jnp.float32) for expert in range(NE)])
            per_pair = out_blocks[route_flat, route_rank].reshape(GROUP_TOKENS, TOPK, MODEL_DIM)
            mixed_rows = jnp.sum(per_pair * gate_values[:, :, None], axis=1) * live_rows[:, None]
            rounded = lax.optimization_barrier(mixed_rows.astype(jnp.bfloat16))
            head_total = head_total + rounded.astype(jnp.float32)
        return head_total.astype(jnp.bfloat16)

    grouped = (tokens.reshape(N_REQ, GROUP_TOKENS, MODEL_DIM), routes.reshape(N_REQ, GROUP_TOKENS, TOPK), lengths.reshape(N_REQ, REQ_GROUP), cached_prefix_length.reshape(N_REQ, REQ_GROUP), prefix_cache_row.reshape(N_REQ, REQ_GROUP), adapter_per_request.reshape(N_REQ, REQ_GROUP))
    result = lax.map(one_group, grouped)
    return result.reshape(TOKENS, MODEL_DIM)
```

```python
import jax
import jax.numpy as jnp
from jax import lax
from jax.experimental import pallas as pl
from jax.experimental.pallas import tpu as pltpu
from jax.sharding import PartitionSpec as P

HD = 128
NE = 8
TOPK = 2
SIDE = 4
BF = jnp.bfloat16
F32 = jnp.float32
NEG = -1e30
adapter_scale = 0.5

ROW_Q, ROW_KV, ROW_UP, ROW_DN = 0, 512, 640, 704
SHARD_ROWS = 736
PLACES = []
for _piece, _off in ((0, 0), (1, -1), (2, 1)):
    for _i, _near in enumerate((0, -1, 1, 2)):
        PLACES.append((_piece, _i * SHARD_ROWS, _near, _off))
PLACES += [(3, 0, 0, 2), (3, SHARD_ROWS, -1, 2), (4, 0, 1, 2), (4, SHARD_ROWS, 2, 2)]


def torus(dx, dz):
    return [
        (i, ((i // SIDE + dx) % SIDE) * SIDE + (i % SIDE + dz) % SIDE) for i in range(SIDE * SIDE)
    ]


def send(value, along, step):
    return lax.ppermute(value, "req", torus(step, 0) if along == 0 else torus(0, step))


def ring(value, along):
    before = send(value, along, 1)
    after = send(value, along, -1)
    half = value.shape[0] // 2
    far_low = send(before[:half], along, 1)
    far_high = send(after[half:], along, -1)
    return before, after, far_low, far_high


def source(group, half, first, second):
    x, z = group // SIDE, group % SIDE
    dx, dz = (first, second) if half == 0 else (second, first)
    return ((x + dx + SIDE) % SIDE) * SIDE + (z + dz + SIDE) % SIDE


def pick_rows_kernel(index_ref, store_ref, out_ref, sem):
    copies = []
    for i in range(out_ref.shape[0]):
        copy = pltpu.make_async_copy(store_ref.at[index_ref[i]], out_ref.at[i], sem.at[i])
        copy.start()
        copies.append(copy)
    for copy in copies:
        copy.wait()


def pick_rows(index, store):
    count = index.shape[0]
    return pl.pallas_call(
        pick_rows_kernel,
        out_shape=jax.ShapeDtypeStruct((count,) + store.shape[1:], store.dtype),
        grid_spec=pltpu.PrefetchScalarGridSpec(
            num_scalar_prefetch=1,
            grid=(1,),
            in_specs=[pl.BlockSpec(memory_space=pl.ANY)],
            out_specs=pl.BlockSpec(memory_space=pl.ANY),
            scratch_shapes=[pltpu.SemaphoreType.DMA((count,))],
        ),
        name="pick_rows",
    )(index, store)


def pick_down_kernel(info_ref, *refs):
    pieces, (out_ref, sem) = refs[:10], refs[10:]
    group = info_ref[0]
    for j in range(4):
        slot = info_ref[1 + j]
        owner, inner = slot // 4, slot % 4
        for half in range(2):
            for piece, row, first, second in PLACES:
                here = (owner == source(group, half, first, second)) & (inner // 2 == half)

                @pl.when(here)
                def _(piece=piece, row=row, half=half, j=j, inner=inner):
                    start = pl.multiple_of(row + ROW_DN + (inner % 2) * 16, 16)
                    pltpu.make_async_copy(
                        pieces[half * 5 + piece].at[pl.ds(start, 16), :], out_ref.at[j], sem.at[j]
                    ).start()

    for j in range(4):
        pltpu.make_async_copy(
            pieces[0].at[pl.ds(0, 16), :], out_ref.at[j], sem.at[j]
        ).wait()


def pick_down(info, pieces):
    return pl.pallas_call(
        pick_down_kernel,
        out_shape=jax.ShapeDtypeStruct((4, 16, 256), BF),
        grid_spec=pltpu.PrefetchScalarGridSpec(
            num_scalar_prefetch=1,
            grid=(1,),
            in_specs=[pl.BlockSpec(memory_space=pl.ANY)] * 10,
            out_specs=pl.BlockSpec(memory_space=pl.ANY),
            scratch_shapes=[pltpu.SemaphoreType.DMA((4,))],
        ),
        name="pick_down",
    )(info, *pieces)


def mix_kernel(info_ref, x_ref, routes_ref, down_ref, recv_ref, *refs):
    pieces = refs[:10]
    out_ref = refs[10]
    wq, wkv, up, cache, kv, q, sem_q, sem_kv, sem_up, sem_cache = refs[11:]
    group = info_ref[0]
    for j in range(4):
        pltpu.make_async_copy(recv_ref.at[info_ref[5 + j]], cache.at[j], sem_cache.at[j]).start()
    sources = [
        [source(group, half, first, second) for _, _, first, second in PLACES] for half in range(2)
    ]

    def fetch(row, count, target, sem):
        for half in range(2):
            for at, (piece, base, _, _) in enumerate(PLACES):
                where = pl.multiple_of(sources[half][at] * count, count)
                pltpu.make_async_copy(
                    pieces[half * 5 + piece].at[pl.ds(base + row, count), :],
                    target(half).at[pl.ds(where, count), :],
                    sem(half),
                ).start()

    fetch(ROW_UP, 64, lambda half: up.at[half], lambda half: sem_up.at[half])
    fetch(ROW_KV, 128, lambda half: wkv.at[half], lambda half: sem_kv.at[half])
    for i in range(4):
        fetch(
            ROW_Q + i * 128,
            128,
            lambda half, i=i: wq.at[half * 4 + i],
            lambda half, i=i: sem_q.at[half * 4 + i],
        )
    for half in range(2):
        pltpu.make_async_copy(up.at[half], up.at[half], sem_up.at[half]).wait()
        pltpu.make_async_copy(wkv.at[half], wkv.at[half], sem_kv.at[half]).wait()

    def project_kv(j, carry):
        rows = pl.ds(pl.multiple_of(j * 256, 256), 256)
        x = x_ref[rows, :]
        slot = info_ref[1 + j]
        down = jnp.concatenate([down_ref[e, j] for e in range(NE)], axis=1)
        low = lax.dot_general(x, down, (((1,), (1,)), ((), ())), preferred_element_type=F32).astype(BF)
        for half in range(2):
            base = jnp.dot(x, wkv[half], preferred_element_type=F32)
            lift = up[half, pl.ds(pl.multiple_of(slot * 16, 16), 16), :]
            extra = jnp.dot(low, lift, preferred_element_type=F32)
            kv[half, rows, :] = (base + adapter_scale * extra).astype(BF)
        return carry

    lax.fori_loop(0, 4, project_kv, 0)

    q[...] = jnp.zeros_like(q)

    def project_q(step, carry):
        e = (step % 2) * 4 + step // 2
        pltpu.make_async_copy(wq.at[e], wq.at[e], sem_q.at[e]).wait()
        for j in range(4):
            rows = pl.ds(j * 256, 256)
            value = jnp.dot(x_ref[rows, :], wq[e], preferred_element_type=F32)
            for k in range(TOPK):
                mine = routes_ref[rows, k : k + 1] == e
                q[k, rows, :] = jnp.where(mine, value, q[k, rows, :])
        return carry

    lax.fori_loop(0, NE, project_q, 0)

    for j in range(4):
        pltpu.make_async_copy(recv_ref.at[0], cache.at[j], sem_cache.at[j]).wait()

    def attend(j, carry):
        rows = pl.ds(pl.multiple_of(j * 256, 256), 256)
        cached_length = info_ref[9 + j]
        place = lax.broadcasted_iota(jnp.int32, (512, 320), 1)
        query_at = lax.broadcasted_iota(jnp.int32, (512, 320), 0) % 256
        allowed = ((place < 64) & (place < cached_length)) | (
            (place >= 64) & (place - 64 <= query_at)
        )
        for h in range(2):
            cols = slice(h * HD, (h + 1) * HD)
            keys = jnp.concatenate(
                [cache[j, :, h * 256 : h * 256 + HD], kv[h, rows, 0:HD]], axis=0
            )
            values = jnp.concatenate(
                [cache[j, :, h * 256 + HD : h * 256 + 2 * HD], kv[h, rows, HD : 2 * HD]], axis=0
            )
            queries = jnp.concatenate([q[0, rows, cols], q[1, rows, cols]], axis=0).astype(BF)
            scores = lax.dot_general(
                queries, keys, (((1,), (1,)), ((), ())), preferred_element_type=F32
            ) * (HD**-0.5)
            scores = jnp.where(allowed, scores, NEG)
            weights = jnp.exp(scores - jnp.max(scores, axis=-1, keepdims=True))
            total = jnp.sum(weights, axis=-1, keepdims=True)
            probability = (weights * (1.0 / total)).astype(BF)
            attended = jnp.dot(probability, values, preferred_element_type=F32)
            first, second = attended[:256], attended[256:]
            for e in range(NE):
                chosen = jnp.where(
                    routes_ref[rows, 0:1] == e,
                    first,
                    jnp.where(routes_ref[rows, 1:2] == e, second, 0.0),
                )
                out_ref[e, rows, cols] = chosen.astype(BF)
        return carry

    lax.fori_loop(0, 4, attend, 0)


def mix(info, x, routes, down, recv, pieces):
    any_spec = pl.BlockSpec(memory_space=pl.ANY)
    whole = pl.BlockSpec(memory_space=pltpu.VMEM)
    return pl.pallas_call(
        mix_kernel,
        out_shape=jax.ShapeDtypeStruct((NE, 1024, 256), BF),
        in_specs=[pl.BlockSpec(memory_space=pltpu.SMEM), whole, whole, whole]
        + [any_spec] * 11,
        out_specs=whole,
        scratch_shapes=[
            pltpu.VMEM((NE, 2048, 256), BF),
            pltpu.VMEM((2, 2048, 256), BF),
            pltpu.VMEM((2, 1024, 256), BF),
            pltpu.VMEM((4, 64, 512), BF),
            pltpu.VMEM((2, 1024, 256), BF),
            pltpu.VMEM((TOPK, 1024, 256), F32),
            pltpu.SemaphoreType.DMA((NE,)),
            pltpu.SemaphoreType.DMA((2,)),
            pltpu.SemaphoreType.DMA((2,)),
            pltpu.SemaphoreType.DMA((4,)),
        ],
        compiler_params=pltpu.CompilerParams(vmem_limit_bytes=48 * 2**20),
        name="mix",
    )(info, x, routes, down, recv, *pieces)


def project_out_kernel(gates_ref, lhs_ref, w_ref, out_ref, wide):
    @pl.when(pl.program_id(0) == 0)
    def _():
        for e in range(NE):
            wide[e] = jnp.broadcast_to(gates_ref[:, e : e + 1], (1024, 128))

    def block(i, carry):
        rows = pl.ds(pl.multiple_of(i * 256, 256), 256)
        total = None
        for e in range(NE):
            weight = jnp.concatenate([w_ref[0, e], w_ref[1, e]], axis=1)
            value = jnp.dot(lhs_ref[e, rows, :], weight, preferred_element_type=F32)
            gate = wide[e, rows, :]
            value = value * jnp.concatenate([gate, gate], axis=1)
            total = value if total is None else total + value
        out_ref[rows, :] = total.astype(BF)
        return carry

    lax.fori_loop(0, 4, block, 0)


def project_out(gates, lhs, weight):
    return pl.pallas_call(
        project_out_kernel,
        out_shape=jax.ShapeDtypeStruct((1024, 2048), BF),
        grid=(8,),
        in_specs=[
            pl.BlockSpec((1024, NE), lambda n: (0, 0)),
            pl.BlockSpec((NE, 1024, 256), lambda n: (0, 0, 0)),
            pl.BlockSpec((2, NE, 256, 128), lambda n: (n, 0, 0, 0)),
        ],
        out_specs=pl.BlockSpec((1024, 256), lambda n: (0, n)),
        scratch_shapes=[pltpu.VMEM((NE, 1024, 128), F32)],
        compiler_params=pltpu.CompilerParams(vmem_limit_bytes=40 * 2**20),
        name="project_out",
    )(gates, lhs, weight)


def body(
    tokens,
    routes,
    lengths,
    cached_prefix_length,
    prefix_cache_row,
    adapter_per_request,
    adapter_storage_slot,
    router_weight,
    key_value_weight,
    expert_query_weight,
    expert_output_weight,
    adapter_down_maps,
    adapter_up_maps,
    prefix_cache_store,
):
    group = lax.axis_index("req")
    part = lax.axis_index("exp")
    out_weight = lax.all_gather(expert_output_weight, "req", axis=0, tiled=True).reshape(
        16, NE, 256, 128
    )

    query_rows = expert_query_weight.transpose(1, 0, 2).reshape(NE * 128, 256)
    down_rows = (
        lax.dynamic_slice_in_dim(adapter_down_maps, part * 256, 256, 1)
        .transpose(0, 2, 1)
        .reshape(64, 256)
    )
    up_rows = adapter_up_maps.reshape(64, 512)
    halves = []
    for half in range(2):
        cols = slice(half * 256, half * 256 + 256)
        halves.append(
            jnp.concatenate(
                [
                    query_rows[half * 512 : half * 512 + 512],
                    key_value_weight[:, cols],
                    up_rows[:, cols],
                    down_rows[half * 32 : half * 32 + 32],
                ],
                axis=0,
            )
        )
    near = [jnp.concatenate([halves[half], *ring(halves[half], half)], axis=0) for half in range(2)]
    pieces = []
    for half in range(2):
        pieces += [near[half], *ring(near[half], 1 - half)]

    rows_by_group = prefix_cache_row.reshape(16, 4)
    held = (rows_by_group == group).astype(jnp.int32)
    wanted_by = jnp.sum(held * jnp.arange(4, dtype=jnp.int32)[None, :], axis=1)
    outgoing = pick_rows(wanted_by, prefix_cache_store)
    received = lax.all_to_all(outgoing, "req", split_axis=0, concat_axis=0, tiled=True)

    adapter_hot = (
        adapter_per_request[:, None]
        == jnp.arange(adapter_storage_slot.shape[0], dtype=jnp.int32)[None, :]
    ).astype(jnp.int32)
    slots = jnp.sum(adapter_hot * adapter_storage_slot[None, :], axis=1)
    own_rows = lax.dynamic_slice_in_dim(prefix_cache_row, group * 4, 4, 0)
    info = jnp.concatenate([group[None].astype(jnp.int32), slots, own_rows, cached_prefix_length])

    logits = jnp.dot(tokens, router_weight, preferred_element_type=F32)
    expert = jnp.arange(NE, dtype=jnp.int32)
    route_hot = (routes[:, :, None] == expert[None, None, :]).astype(F32)
    chosen = jnp.sum(route_hot * logits[:, None, :], axis=-1)
    gate_values = jax.nn.sigmoid(chosen - chosen[:, ::-1])
    live = (jnp.arange(256, dtype=jnp.int32)[None, :] < lengths[:, None]).reshape(1024, 1)
    gates = jnp.sum(route_hot * gate_values[:, :, None], axis=1) * live.astype(F32)

    down_part = pick_down(info, pieces)
    down = lax.all_gather(down_part.reshape(1, 4, 16, 256), "exp", axis=0, tiled=True)
    lhs = mix(info, tokens, routes, down, received, pieces)
    partial_value = project_out(gates, lhs, out_weight)
    return lax.psum_scatter(partial_value, "exp", scatter_dimension=1, tiled=True)


def solution(mesh):
    return jax.shard_map(
        body,
        mesh=mesh,
        in_specs=(
            P("req", None),
            P("req", None),
            P("req"),
            P("req"),
            P(),
            P("req"),
            P(),
            P(),
            P("req", "exp"),
            P("req", None, "exp"),
            P(None, "exp", "req"),
            P("req", None, None),
            P("req", None, "exp"),
            P("req", None, "exp"),
        ),
        out_specs=P("req", "exp"),
        check_vma=False,
    )
```

```python
import jax
import jax.numpy as jnp
from jax import lax
from jax.experimental import pallas as pl
from jax.experimental.pallas import tpu as pltpu
from jax.sharding import PartitionSpec as P

HD = 128
NE = 8
TOPK = 2
SIDE = 4
BF = jnp.bfloat16
F32 = jnp.float32
NEG = -1e30
adapter_scale = 0.5

ROW_Q, ROW_KV, ROW_UP, ROW_DN = 0, 512, 640, 704
SHARD_ROWS = 736
OUT_ROWS = 512
PLACES = []
for _piece, _off in ((0, 0), (1, -1), (2, 1)):
    for _i, _near in enumerate((0, -1, 1, 2)):
        PLACES.append((_piece, _i, _near, _off))
PLACES += [(3, 0, 0, 2), (3, 1, -1, 2), (4, 0, 1, 2), (4, 1, 2, 2)]


def torus(dx, dz):
    return [
        (i, ((i // SIDE + dx) % SIDE) * SIDE + (i % SIDE + dz) % SIDE) for i in range(SIDE * SIDE)
    ]


def send(value, along, step):
    return lax.ppermute(value, "req", torus(step, 0) if along == 0 else torus(0, step))


def ring(value, along):
    before = send(value, along, 1)
    after = send(value, along, -1)
    half = value.shape[0] // 2
    far_low = send(before[:half], along, 1)
    far_high = send(after[half:], along, -1)
    return before, after, far_low, far_high


def source(group, half, first, second):
    x, z = group // SIDE, group % SIDE
    dx, dz = (first, second) if half == 0 else (second, first)
    return ((x + dx + SIDE) % SIDE) * SIDE + (z + dz + SIDE) % SIDE


def pick_rows_kernel(index_ref, store_ref, out_ref):
    def one(i, carry):
        out_ref[i] = store_ref[index_ref[i]]
        return carry

    lax.fori_loop(0, out_ref.shape[0], one, 0)


def pick_rows(index, store):
    whole = pl.BlockSpec(memory_space=pltpu.VMEM)
    return pl.pallas_call(
        pick_rows_kernel,
        out_shape=jax.ShapeDtypeStruct((index.shape[0],) + store.shape[1:], store.dtype),
        in_specs=[pl.BlockSpec(memory_space=pltpu.SMEM), whole],
        out_specs=whole,
        name="pick_rows",
    )(index, store)


def pick_down_kernel(info_ref, *refs):
    pieces, (out_ref, sem) = refs[:10], refs[10:]
    group = info_ref[0]
    for j in range(4):
        slot = info_ref[1 + j]
        owner, inner = slot // 4, slot % 4
        for half in range(2):
            for piece, shard, first, second in PLACES:
                here = (owner == source(group, half, first, second)) & (inner // 2 == half)

                @pl.when(here)
                def _(piece=piece, shard=shard, half=half, j=j, inner=inner):
                    start = pl.multiple_of(shard * SHARD_ROWS + ROW_DN + (inner % 2) * 16, 16)
                    pltpu.make_async_copy(
                        pieces[half * 5 + piece].at[pl.ds(start, 16), :], out_ref.at[j], sem.at[j]
                    ).start()

    for j in range(4):
        pltpu.make_async_copy(
            pieces[0].at[pl.ds(0, 16), :], out_ref.at[j], sem.at[j]
        ).wait()


def pick_down(info, pieces):
    return pl.pallas_call(
        pick_down_kernel,
        out_shape=jax.ShapeDtypeStruct((4, 16, 256), BF),
        grid_spec=pltpu.PrefetchScalarGridSpec(
            num_scalar_prefetch=1,
            grid=(1,),
            in_specs=[pl.BlockSpec(memory_space=pltpu.HBM)] * 10,
            out_specs=pl.BlockSpec(memory_space=pl.ANY),
            scratch_shapes=[pltpu.SemaphoreType.DMA((4,))],
        ),
        name="pick_down",
    )(info, *pieces)


def start_fetch(group, pieces, row, count, target, sem):
    for half in range(2):
        for piece, shard, first, second in PLACES:
            where = pl.multiple_of(source(group, half, first, second) * count, count)
            pltpu.make_async_copy(
                pieces[half * 5 + piece].at[pl.ds(shard * SHARD_ROWS + row, count), :],
                target(half).at[pl.ds(where, count), :],
                sem(half),
            ).start()


def query_kernel(info_ref, x_ref, routes_ref, *refs):
    pieces = refs[:10]
    out_ref, wq, q, sem_q = refs[10:]
    group = info_ref[0]
    for i in range(4):
        start_fetch(
            group,
            pieces,
            ROW_Q + i * 128,
            128,
            lambda half, i=i: wq.at[half * 4 + i],
            lambda half, i=i: sem_q.at[half * 4 + i],
        )
    q[...] = jnp.zeros_like(q)

    def project(step, carry):
        e = (step % 2) * 4 + step // 2
        pltpu.make_async_copy(wq.at[e], wq.at[e], sem_q.at[e]).wait()
        for j in range(4):
            rows = pl.ds(j * 256, 256)
            value = jnp.dot(x_ref[rows, :], wq[e], preferred_element_type=F32)
            for k in range(TOPK):
                mine = routes_ref[rows, k : k + 1] == e
                q[k, rows, :] = jnp.where(mine, value, q[k, rows, :])
        return carry

    lax.fori_loop(0, NE, project, 0)
    out_ref[...] = q[...].astype(BF)


HBM = pl.BlockSpec(memory_space=pltpu.HBM)
WHOLE = pl.BlockSpec(memory_space=pltpu.VMEM)
SCALARS = pl.BlockSpec(memory_space=pltpu.SMEM)


def project_query(info, x, routes, pieces):
    return pl.pallas_call(
        query_kernel,
        out_shape=jax.ShapeDtypeStruct((TOPK, 1024, 256), BF),
        in_specs=[SCALARS, WHOLE, WHOLE] + [HBM] * 10,
        out_specs=WHOLE,
        scratch_shapes=[
            pltpu.VMEM((NE, 2048, 256), BF),
            pltpu.VMEM((TOPK, 1024, 256), F32),
            pltpu.SemaphoreType.DMA((NE,)),
        ],
        compiler_params=pltpu.CompilerParams(vmem_limit_bytes=24 * 2**20),
        name="project_query",
    )(info, x, routes, *pieces)


def attend_kernel(info_ref, x_ref, routes_ref, down_ref, q_ref, recv_ref, *refs):
    pieces = refs[:10]
    out_ref, wkv, up, cache, kv, sem_kv, sem_up, sem_cache = refs[10:]
    group = info_ref[0]
    start_fetch(
        group, pieces, ROW_UP, 64, lambda half: up.at[half], lambda half: sem_up.at[half]
    )
    start_fetch(
        group, pieces, ROW_KV, 128, lambda half: wkv.at[half], lambda half: sem_kv.at[half]
    )
    for j in range(4):
        pltpu.make_async_copy(recv_ref.at[info_ref[5 + j]], cache.at[j], sem_cache.at[j]).start()
    for half in range(2):
        pltpu.make_async_copy(up.at[half], up.at[half], sem_up.at[half]).wait()
        pltpu.make_async_copy(wkv.at[half], wkv.at[half], sem_kv.at[half]).wait()

    def project_kv(j, carry):
        rows = pl.ds(pl.multiple_of(j * 256, 256), 256)
        x = x_ref[rows, :]
        slot = info_ref[1 + j]
        down = jnp.concatenate([down_ref[e, j] for e in range(NE)], axis=1)
        low = lax.dot_general(
            x, down, (((1,), (1,)), ((), ())), preferred_element_type=F32
        ).astype(BF)
        for half in range(2):
            base = jnp.dot(x, wkv[half], preferred_element_type=F32)
            lift = up[half, pl.ds(pl.multiple_of(slot * 16, 16), 16), :]
            extra = jnp.dot(low, lift, preferred_element_type=F32)
            kv[half, rows, :] = (base + adapter_scale * extra).astype(BF)
        return carry

    lax.fori_loop(0, 4, project_kv, 0)

    for j in range(4):
        pltpu.make_async_copy(recv_ref.at[0], cache.at[j], sem_cache.at[j]).wait()

    def attend(j, carry):
        rows = pl.ds(pl.multiple_of(j * 256, 256), 256)
        cached_length = info_ref[9 + j]
        place = lax.broadcasted_iota(jnp.int32, (512, 320), 1)
        query_at = lax.broadcasted_iota(jnp.int32, (512, 320), 0) % 256
        allowed = ((place < 64) & (place < cached_length)) | (
            (place >= 64) & (place - 64 <= query_at)
        )
        for h in range(2):
            cols = slice(h * HD, (h + 1) * HD)
            keys = jnp.concatenate(
                [cache[j, :, h * 256 : h * 256 + HD], kv[h, rows, 0:HD]], axis=0
            )
            values = jnp.concatenate(
                [cache[j, :, h * 256 + HD : h * 256 + 2 * HD], kv[h, rows, HD : 2 * HD]], axis=0
            )
            queries = jnp.concatenate([q_ref[0, rows, cols], q_ref[1, rows, cols]], axis=0)
            scores = lax.dot_general(
                queries, keys, (((1,), (1,)), ((), ())), preferred_element_type=F32
            ) * (HD**-0.5)
            scores = jnp.where(allowed, scores, NEG)
            weights = jnp.exp(scores - jnp.max(scores, axis=-1, keepdims=True))
            total = jnp.sum(weights, axis=-1, keepdims=True)
            probability = (weights * (1.0 / total)).astype(BF)
            attended = jnp.dot(probability, values, preferred_element_type=F32)
            first, second = attended[:256], attended[256:]
            for e in range(NE):
                chosen = jnp.where(
                    routes_ref[rows, 0:1] == e,
                    first,
                    jnp.where(routes_ref[rows, 1:2] == e, second, 0.0),
                )
                out_ref[e, rows, cols] = chosen.astype(BF)
        return carry

    lax.fori_loop(0, 4, attend, 0)


def attention(info, x, routes, down, q, recv, pieces):
    return pl.pallas_call(
        attend_kernel,
        out_shape=jax.ShapeDtypeStruct((NE, 1024, 256), BF),
        in_specs=[SCALARS] + [WHOLE] * 4 + [HBM] * 11,
        out_specs=WHOLE,
        scratch_shapes=[
            pltpu.VMEM((2, 2048, 256), BF),
            pltpu.VMEM((2, 1024, 256), BF),
            pltpu.VMEM((4, 64, 512), BF),
            pltpu.VMEM((2, 1024, 256), BF),
            pltpu.SemaphoreType.DMA((2,)),
            pltpu.SemaphoreType.DMA((2,)),
            pltpu.SemaphoreType.DMA((4,)),
        ],
        compiler_params=pltpu.CompilerParams(vmem_limit_bytes=24 * 2**20),
        name="attention",
    )(info, x, routes, down, q, recv, *pieces)


def project_out_kernel(place_ref, gates_ref, lhs_ref, *refs):
    pieces = refs[:10]
    out_ref, w, wide, sem = refs[10:]
    group, first_block, side = place_ref[0], place_ref[1], place_ref[2]
    for half in range(2):
        for piece, shard, first, second in PLACES:
            owner = source(group, half, first, second)

            @pl.when((owner % 4) // 2 == side)
            def _(half=half, piece=piece, shard=shard, owner=owner):
                pltpu.make_async_copy(
                    pieces[half * 5 + piece].at[pl.ds(shard * OUT_ROWS, OUT_ROWS), :],
                    w.at[owner // 4, half, owner % 2],
                    sem.at[owner // 4],
                ).start()

    for e in range(NE):
        wide[e] = jnp.broadcast_to(gates_ref[:, e : e + 1], (1024, 128))

    def block(step, carry):
        at = (first_block + step) % 4
        pltpu.make_async_copy(w.at[at], w.at[at], sem.at[at]).wait()
        for i in range(4):
            rows = pl.ds(i * 256, 256)
            total = None
            for e in range(NE):
                half, pair, lane = e // 4, (e % 4) // 2, e % 2
                place = (pl.ds(pair * 256, 256), pl.ds(lane * 128, 128))
                weight = jnp.concatenate(
                    [w[at, half, 0, place[0], place[1]], w[at, half, 1, place[0], place[1]]], axis=1
                )
                value = jnp.dot(lhs_ref[e, rows, :], weight, preferred_element_type=F32)
                gate = wide[e, rows, :]
                value = value * jnp.concatenate([gate, gate], axis=1)
                total = value if total is None else total + value
            out_ref[step, rows, :] = total.astype(BF)
        return carry

    lax.fori_loop(0, 4, block, 0)


def project_out(place, gates, lhs, pieces):
    return pl.pallas_call(
        project_out_kernel,
        out_shape=jax.ShapeDtypeStruct((4, 1024, 256), BF),
        in_specs=[SCALARS, WHOLE, WHOLE] + [HBM] * 10,
        out_specs=WHOLE,
        scratch_shapes=[
            pltpu.VMEM((4, 2, 2, OUT_ROWS, 256), BF),
            pltpu.VMEM((NE, 1024, 128), F32),
            pltpu.SemaphoreType.DMA((4,)),
        ],
        compiler_params=pltpu.CompilerParams(vmem_limit_bytes=24 * 2**20),
        name="project_out",
    )(place, gates, lhs, *pieces)


def exchange(value, step):
    if step == 0:
        return lax.ppermute(value, "exp", [(i, i ^ 1) for i in range(8)])
    return lax.ppermute(value, "exp", [(i, (i + 2 * step) % 8) for i in range(8)])


def rounded_sum(*values):
    total = values[0].astype(F32)
    for value in values[1:]:
        total = total + value.astype(F32)
    return total.astype(BF)


def body(
    tokens,
    routes,
    lengths,
    cached_prefix_length,
    prefix_cache_row,
    adapter_per_request,
    adapter_storage_slot,
    router_weight,
    key_value_weight,
    expert_query_weight,
    expert_output_weight,
    adapter_down_maps,
    adapter_up_maps,
    prefix_cache_store,
):
    group = lax.axis_index("req")
    part = lax.axis_index("exp")
    query_rows = expert_query_weight.transpose(1, 0, 2).reshape(NE * 128, 256)
    down_rows = (
        lax.dynamic_slice_in_dim(adapter_down_maps, part * 256, 256, 1)
        .transpose(0, 2, 1)
        .reshape(64, 256)
    )
    up_rows = adapter_up_maps.reshape(64, 512)
    out_rows = (
        expert_output_weight.reshape(4, 2, 256, 128).transpose(0, 2, 1, 3).reshape(1024, 256)
    )
    near_mix, near_out = [], []
    for half in range(2):
        cols = slice(half * 256, half * 256 + 256)
        own = jnp.concatenate(
            [
                query_rows[half * 512 : half * 512 + 512],
                key_value_weight[:, cols],
                up_rows[:, cols],
                down_rows[half * 32 : half * 32 + 32],
                out_rows[half * 512 : half * 512 + 512],
            ],
            axis=0,
        )
        before, after, far_low, far_high = ring(own, half)
        cut = SHARD_ROWS - far_low.shape[0]
        near_mix.append(
            jnp.concatenate(
                [own[:SHARD_ROWS], before[:SHARD_ROWS], after[:SHARD_ROWS], far_low, far_high[:cut]],
                axis=0,
            )
        )
        near_out.append(
            jnp.concatenate(
                [own[SHARD_ROWS:], before[SHARD_ROWS:], after[SHARD_ROWS:], far_high[cut:]], axis=0
            )
        )
    pieces, waits = [], []
    for half in range(2):
        rest = ring(near_mix[half], 1 - half)
        pieces += [near_mix[half], *rest]
        waits += rest[:2]
    near_out = lax.optimization_barrier(tuple(near_out + waits))[:2]
    out_pieces = []
    for half in range(2):
        out_pieces += [near_out[half], *ring(near_out[half], 1 - half)]

    rows_by_group = prefix_cache_row.reshape(16, 4)
    held = (rows_by_group == group).astype(jnp.int32)
    wanted_by = jnp.sum(held * jnp.arange(4, dtype=jnp.int32)[None, :], axis=1)
    outgoing = pick_rows(wanted_by, prefix_cache_store)
    received = lax.all_to_all(outgoing, "req", split_axis=0, concat_axis=0, tiled=True)

    adapter_hot = (
        adapter_per_request[:, None]
        == jnp.arange(adapter_storage_slot.shape[0], dtype=jnp.int32)[None, :]
    ).astype(jnp.int32)
    slots = jnp.sum(adapter_hot * adapter_storage_slot[None, :], axis=1)
    own_rows = lax.dynamic_slice_in_dim(prefix_cache_row, group * 4, 4, 0)
    info = jnp.concatenate([group[None].astype(jnp.int32), slots, own_rows, cached_prefix_length])

    logits = jnp.dot(tokens, router_weight, preferred_element_type=F32)
    expert = jnp.arange(NE, dtype=jnp.int32)
    route_hot = (routes[:, :, None] == expert[None, None, :]).astype(F32)
    chosen = jnp.sum(route_hot * logits[:, None, :], axis=-1)
    gate_values = jax.nn.sigmoid(chosen - chosen[:, ::-1])
    live = (jnp.arange(256, dtype=jnp.int32)[None, :] < lengths[:, None]).reshape(1024, 1)
    gates = jnp.sum(route_hot * gate_values[:, :, None], axis=1) * live.astype(F32)

    down_part = pick_down(info, pieces)
    down = lax.all_to_all(
        jnp.broadcast_to(down_part[None], (NE, 4, 16, 256)), "exp", 0, 0, tiled=True
    )
    q = project_query(info, tokens, routes, pieces)
    lhs = attention(info, tokens, routes, down, q, received, pieces)

    y, core = part // 2, part % 2
    theirs_at = jnp.stack([group, y, 1 - core]).astype(jnp.int32)
    mine_at = jnp.stack([group, y, core]).astype(jnp.int32)
    theirs = project_out(theirs_at, gates, lhs, out_pieces)
    swapped = exchange(theirs, 0)
    mine = project_out(mine_at, gates, lhs, out_pieces)
    both = rounded_sum(mine, swapped)
    low = exchange(both[2, :512], 1)
    high = exchange(both[2, 512:], -1)
    ahead = jnp.concatenate([rounded_sum(both[1, :512], low), both[1, 512:]], axis=0)
    behind = jnp.concatenate([both[3, :512], rounded_sum(both[3, 512:], high)], axis=0)
    return rounded_sum(both[0], exchange(ahead, 1), exchange(behind, -1))


def solution(mesh):
    return jax.shard_map(
        body,
        mesh=mesh,
        in_specs=(
            P("req", None),
            P("req", None),
            P("req"),
            P("req"),
            P(),
            P("req"),
            P(),
            P(),
            P("req", "exp"),
            P("req", None, "exp"),
            P(None, "exp", "req"),
            P("req", None, None),
            P("req", None, "exp"),
            P("req", None, "exp"),
        ),
        out_specs=P("req", "exp"),
        check_vma=False,
    )
```

```python
import functools

import jax
import jax.numpy as jnp
from jax import lax
from jax.experimental import pallas as pl
from jax.experimental.pallas import tpu as pltpu
from jax.sharding import PartitionSpec as P

HD = 128
NE = 8
TOPK = 2
SIDE = 4
BF = jnp.bfloat16
F32 = jnp.float32
NEG = -1e30
adapter_scale = 0.5

ROW_KV = 512
SHARD_ROWS = 640
OUT_ROWS = 512
ROW_UP, ROW_DN, SENT_ROWS = 64, 128, 160
PLACES = []
for _piece, _off in ((0, 0), (1, -1), (2, 1)):
    for _i, _near in enumerate((0, -1, 1, 2)):
        PLACES.append((_piece, _i, _near, _off))
PLACES += [(3, 0, 0, 2), (3, 1, -1, 2), (4, 0, 1, 2), (4, 1, 2, 2)]


def torus(dx, dz):
    return [
        (i, ((i // SIDE + dx) % SIDE) * SIDE + (i % SIDE + dz) % SIDE) for i in range(SIDE * SIDE)
    ]


def send(value, along, step):
    return lax.ppermute(value, "req", torus(step, 0) if along == 0 else torus(0, step))


def first_step(value, along):
    return send(value, along, 1), send(value, along, -1)


def second_step(before, after, along):
    half = before.shape[0] // 2
    return send(before[:half], along, 1), send(after[half:], along, -1)


def source(group, half, first, second):
    x, z = group // SIDE, group % SIDE
    dx, dz = (first, second) if half == 0 else (second, first)
    return ((x + dx + SIDE) % SIDE) * SIDE + (z + dz + SIDE) % SIDE


def cost(us):
    return pl.CostEstimate(flops=int(us * 1.15e9), bytes_accessed=2**20, transcendentals=0)


ANY = pl.BlockSpec(memory_space=pl.ANY)
WHOLE = pl.BlockSpec(memory_space=pltpu.VMEM)
SCALARS = pl.BlockSpec(memory_space=pltpu.SMEM)


def pack_kernel(index_ref, store_ref, up_ref, down_ref, out_ref):
    def one(i, carry):
        out_ref[i, 0:ROW_UP, :] = store_ref[index_ref[i]]
        out_ref[i, ROW_UP:ROW_DN, :] = up_ref[...]
        for side in range(2):
            out_ref[i, ROW_DN:SENT_ROWS, side * 256 : side * 256 + 256] = down_ref[
                side * 32 : side * 32 + 32, :
            ]
        return carry

    lax.fori_loop(0, out_ref.shape[0], one, 0)


def pack(index, store, up, down):
    return pl.pallas_call(
        pack_kernel,
        out_shape=jax.ShapeDtypeStruct((16, SENT_ROWS, 512), BF),
        in_specs=[SCALARS] + [WHOLE] * 3,
        out_specs=WHOLE,
        cost_estimate=cost(3),
        name="pack",
    )(index, store, up, down)


def pick_down_kernel(info_ref, recv_ref, out_ref, sem):
    for j in range(4):
        slot = info_ref[1 + j]
        owner, inner = slot // 4, slot % 4
        start = pl.multiple_of(ROW_DN + (inner % 2) * 16, 16)
        for side in range(2):

            @pl.when(inner // 2 == side)
            def _(side=side, j=j, owner=owner, start=start):
                pltpu.make_async_copy(
                    recv_ref.at[owner, pl.ds(start, 16), pl.ds(side * 256, 256)],
                    out_ref.at[j],
                    sem.at[j],
                ).start()

    for j in range(4):
        pltpu.make_async_copy(out_ref.at[j], out_ref.at[j], sem.at[j]).wait()


def pick_down(info, recv):
    return pl.pallas_call(
        pick_down_kernel,
        out_shape=jax.ShapeDtypeStruct((4, 16, 256), BF),
        in_specs=[SCALARS, ANY],
        out_specs=WHOLE,
        scratch_shapes=[pltpu.SemaphoreType.DMA((4,))],
        cost_estimate=cost(2),
        name="pick_down",
    )(info, recv)


STAGES = [
    [(0, shard, first, second) for piece, shard, first, second in PLACES if piece == 0],
    [(piece - 1, shard, first, second) for piece, shard, first, second in PLACES if 0 < piece < 3],
    [(piece - 3, shard, first, second) for piece, shard, first, second in PLACES if piece >= 3],
]


def stage_kernel(stage, info_ref, x_ref, routes_ref, *refs):
    shards = STAGES[stage]
    count = 1 if stage == 0 else 2
    pieces, refs = refs[: 2 * count], refs[2 * count :]
    if stage > 0:
        q_in, kv_in = refs[:2]
        refs = refs[2:]
    q_out, kv_out = refs
    group = info_ref[0]

    def block(j, carry):
        rows = pl.ds(pl.multiple_of(j * 256, 256), 256)
        routes = [routes_ref[rows, k : k + 1] for k in range(TOPK)]
        chosen = [jnp.zeros((256, 256), F32)] * TOPK
        for half in range(2):
            x = jnp.concatenate(
                [
                    x_ref[
                        rows,
                        pl.ds(pl.multiple_of(source(group, half, first, second) * 128, 128), 128),
                    ]
                    for _, _, first, second in shards
                ],
                axis=1,
            )

            def product(row):
                weight = jnp.concatenate(
                    [
                        pieces[half * count + piece][pl.ds(shard * SHARD_ROWS + row, 128), :]
                        for piece, shard, _, _ in shards
                    ],
                    axis=0,
                )
                return jnp.dot(x, weight, preferred_element_type=F32)

            for i in range(4):
                value = product(i * 128)
                for k in range(TOPK):
                    chosen[k] = jnp.where(routes[k] == half * 4 + i, value, chosen[k])
            value = product(ROW_KV)
            if stage > 0:
                value = value + kv_in[half, rows, :]
            kv_out[half, rows, :] = value
        for k in range(TOPK):
            value = chosen[k]
            if stage > 0:
                value = value + q_in[k, rows, :]
            q_out[k, rows, :] = value.astype(q_out.dtype)
        return carry

    lax.fori_loop(0, 4, block, 0)


def project_stage(stage, info, x, routes, pieces, sums):
    count = len(pieces)
    kind = BF if stage == 2 else F32
    return pl.pallas_call(
        functools.partial(stage_kernel, stage),
        out_shape=(
            jax.ShapeDtypeStruct((TOPK, 1024, 256), kind),
            jax.ShapeDtypeStruct((2, 1024, 256), F32),
        ),
        in_specs=[SCALARS] + [WHOLE] * (2 + count + len(sums)),
        out_specs=(WHOLE, WHOLE),
        compiler_params=pltpu.CompilerParams(vmem_limit_bytes=16 * 2**20),
        cost_estimate=cost((5, 10, 5)[stage]),
        name="project_stage_" + str(stage),
    )(info, x, routes, *pieces, *sums)


def attend_kernel(
    part, info_ref, x_ref, routes_ref, down_ref, q_ref, base_ref, recv_ref, out_ref, up, cache, sem
):
    for i in range(2):
        j = part * 2 + i
        slot = info_ref[1 + j]
        start = pl.multiple_of(ROW_UP + (slot % 4) * 16, 16)
        pltpu.make_async_copy(
            recv_ref.at[slot // 4, pl.ds(start, 16), :], up.at[i], sem.at[0, i]
        ).start()
        pltpu.make_async_copy(
            recv_ref.at[info_ref[5 + j], pl.ds(0, 64), :], cache.at[i], sem.at[1, i]
        ).start()
    for i in range(2):
        pltpu.make_async_copy(up.at[i], up.at[i], sem.at[0, i]).wait()
        pltpu.make_async_copy(cache.at[i], cache.at[i], sem.at[1, i]).wait()

    def attend(i, carry):
        j = part * 2 + i
        rows = pl.ds(pl.multiple_of(j * 256, 256), 256)
        out_rows = pl.ds(pl.multiple_of(i * 256, 256), 256)
        down = jnp.concatenate([down_ref[e, j] for e in range(NE)], axis=1)
        low = lax.dot_general(
            x_ref[rows, :], down, (((1,), (1,)), ((), ())), preferred_element_type=F32
        ).astype(BF)
        cached_length = info_ref[9 + j]
        place = lax.broadcasted_iota(jnp.int32, (256, 320), 1)
        query_at = lax.broadcasted_iota(jnp.int32, (256, 320), 0)
        allowed = (place < cached_length) | ((place >= 64) & (place - 64 <= query_at))
        for h in range(2):
            cols = slice(h * HD, (h + 1) * HD)
            extra = jnp.dot(low, up[i, :, h * 256 : h * 256 + 256], preferred_element_type=F32)
            fresh = (base_ref[h, rows, :] + adapter_scale * extra).astype(BF)
            keys = jnp.concatenate(
                [cache[i, :, h * 256 : h * 256 + HD], fresh[:, 0:HD]], axis=0
            )
            values = jnp.concatenate(
                [cache[i, :, h * 256 + HD : h * 256 + 2 * HD], fresh[:, HD : 2 * HD]], axis=0
            )
            attended = []
            for k in range(TOPK):
                scores = lax.dot_general(
                    q_ref[k, rows, cols], keys, (((1,), (1,)), ((), ())), preferred_element_type=F32
                ) * (HD**-0.5)
                scores = jnp.where(allowed, scores, NEG)
                weights = jnp.exp(scores - jnp.max(scores, axis=-1, keepdims=True))
                total = jnp.sum(weights, axis=-1, keepdims=True)
                probability = (weights * (1.0 / total)).astype(BF)
                attended.append(jnp.dot(probability, values, preferred_element_type=F32))
            for e in range(NE):
                chosen = jnp.where(
                    routes_ref[rows, 0:1] == e,
                    attended[0],
                    jnp.where(routes_ref[rows, 1:2] == e, attended[1], 0.0),
                )
                out_ref[e, out_rows, cols] = chosen.astype(BF)
        return carry

    lax.fori_loop(0, 2, attend, 0)


def attention(part, info, x, routes, down, q, base, recv):
    return pl.pallas_call(
        functools.partial(attend_kernel, part),
        out_shape=jax.ShapeDtypeStruct((NE, 512, 256), BF),
        in_specs=[SCALARS] + [WHOLE] * 5 + [ANY],
        out_specs=WHOLE,
        scratch_shapes=[
            pltpu.VMEM((2, 16, 512), BF),
            pltpu.VMEM((2, 64, 512), BF),
            pltpu.SemaphoreType.DMA((2, 2)),
        ],
        compiler_params=pltpu.CompilerParams(vmem_limit_bytes=16 * 2**20),
        cost_estimate=cost(9),
        name="attention_" + str(part),
    )(info, x, routes, down, q, base, recv)


def project_out_kernel(blocks, place_ref, wide_ref, low_ref, high_ref, *refs):
    pieces = refs[:10]
    out_ref, w, sem = refs[10:]
    group, y, core = place_ref[0], place_ref[1], place_ref[2]
    for b, (mine, ahead) in enumerate(blocks):
        wanted_x = (y + ahead) % 4
        side = core if mine else 1 - core
        for half in range(2):
            for piece, shard, first, second in PLACES:
                owner = source(group, half, first, second)

                @pl.when((owner // 4 == wanted_x) & ((owner % 4) // 2 == side))
                def _(b=b, half=half, piece=piece, shard=shard, owner=owner):
                    pltpu.make_async_copy(
                        pieces[half * 5 + piece].at[pl.ds(shard * OUT_ROWS, OUT_ROWS), :],
                        w.at[b, half, owner % 2],
                        sem.at[b],
                    ).start()

    def tile(b, lhs_ref, part, i):
        rows = pl.ds(pl.multiple_of(i * 256, 256), 256)
        gate_rows = pl.ds(pl.multiple_of(part * 512 + i * 256, 256), 256)
        total = None
        for e in range(NE):
            half, pair, lane = e // 4, (e % 4) // 2, e % 2
            place = (pl.ds(pair * 256, 256), pl.ds(lane * 128, 128))
            weight = jnp.concatenate(
                [w[b, half, 0, place[0], place[1]], w[b, half, 1, place[0], place[1]]], axis=1
            )
            value = jnp.dot(lhs_ref[e, rows, :], weight, preferred_element_type=F32)
            gate = wide_ref[e, gate_rows, :]
            value = value * jnp.concatenate([gate, gate], axis=1)
            total = value if total is None else total + value
        out_ref[b, gate_rows, :] = total.astype(BF)

    def block(b, carry):
        pltpu.make_async_copy(w.at[b], w.at[b], sem.at[b]).wait()
        for part, lhs_ref in enumerate((low_ref, high_ref)):

            def step(i, inner, lhs_ref=lhs_ref, part=part):
                tile(b, lhs_ref, part, i)
                return inner

            lax.fori_loop(0, 2, step, 0)
        return carry

    lax.fori_loop(0, len(blocks), block, 0)


def project_out(blocks, place, wide, lhs, pieces):
    return pl.pallas_call(
        functools.partial(project_out_kernel, blocks),
        out_shape=jax.ShapeDtypeStruct((len(blocks), 1024, 256), BF),
        in_specs=[SCALARS, WHOLE, WHOLE, WHOLE] + [ANY] * 10,
        out_specs=WHOLE,
        scratch_shapes=[
            pltpu.VMEM((len(blocks), 2, 2, OUT_ROWS, 256), BF),
            pltpu.SemaphoreType.DMA((len(blocks),)),
        ],
        compiler_params=pltpu.CompilerParams(vmem_limit_bytes=16 * 2**20),
        cost_estimate=cost(2.2 * len(blocks)),
        name="project_out_" + str(len(blocks)),
    )(place, wide, *lhs, *pieces)


def exchange(value, step):
    if step == 0:
        return lax.ppermute(value, "exp", [(i, i ^ 1) for i in range(8)])
    return lax.ppermute(value, "exp", [(i, (i + 2 * step) % 8) for i in range(8)])


def rounded_sum(*values):
    total = values[0].astype(F32)
    for value in values[1:]:
        total = total + value.astype(F32)
    return total.astype(BF)


def body(
    tokens,
    routes,
    lengths,
    cached_prefix_length,
    prefix_cache_row,
    adapter_per_request,
    adapter_storage_slot,
    router_weight,
    key_value_weight,
    expert_query_weight,
    expert_output_weight,
    adapter_down_maps,
    adapter_up_maps,
    prefix_cache_store,
):
    group = lax.axis_index("req")
    part = lax.axis_index("exp")
    rows_by_group = prefix_cache_row.reshape(16, 4)
    held = (rows_by_group == group).astype(jnp.int32)
    wanted_by = jnp.sum(held * jnp.arange(4, dtype=jnp.int32)[None, :], axis=1)
    down_rows = (
        lax.dynamic_slice_in_dim(adapter_down_maps, part * 256, 256, 1)
        .transpose(0, 2, 1)
        .reshape(64, 256)
    )
    outgoing = pack(wanted_by, prefix_cache_store, adapter_up_maps.reshape(64, 512), down_rows)

    query_rows = expert_query_weight.transpose(1, 0, 2).reshape(NE * 128, 256)
    out_rows = (
        expert_output_weight.reshape(4, 2, 256, 128).transpose(0, 2, 1, 3).reshape(1024, 256)
    )
    own = [
        jnp.concatenate(
            [
                query_rows[half * 512 : half * 512 + 512],
                key_value_weight[:, half * 256 : half * 256 + 256],
                out_rows[half * 512 : half * 512 + 512],
            ],
            axis=0,
        )
        for half in range(2)
    ]
    *own, outgoing = lax.optimization_barrier((*own, outgoing))
    received = lax.all_to_all(outgoing, "req", 0, 0, tiled=True)
    near_mix, near_out = [], []
    for half in range(2):
        before, after = first_step(own[half], half)
        far_low, far_high = second_step(before, after, half)
        cut = SHARD_ROWS - far_low.shape[0]
        near_mix.append(
            jnp.concatenate(
                [
                    own[half][:SHARD_ROWS],
                    before[:SHARD_ROWS],
                    after[:SHARD_ROWS],
                    far_low,
                    far_high[:cut],
                ],
                axis=0,
            )
        )
        near_out.append(
            jnp.concatenate(
                [
                    own[half][SHARD_ROWS:],
                    before[SHARD_ROWS:],
                    after[SHARD_ROWS:],
                    far_high[cut:],
                ],
                axis=0,
            )
        )

    adapter_hot = (
        adapter_per_request[:, None]
        == jnp.arange(adapter_storage_slot.shape[0], dtype=jnp.int32)[None, :]
    ).astype(jnp.int32)
    slots = jnp.sum(adapter_hot * adapter_storage_slot[None, :], axis=1)
    own_rows = lax.dynamic_slice_in_dim(prefix_cache_row, group * 4, 4, 0)
    info = jnp.concatenate([group[None].astype(jnp.int32), slots, own_rows, cached_prefix_length])

    logits = jnp.dot(tokens, router_weight, preferred_element_type=F32)
    expert = jnp.arange(NE, dtype=jnp.int32)
    route_hot = (routes[:, :, None] == expert[None, None, :]).astype(F32)
    chosen = jnp.sum(route_hot * logits[:, None, :], axis=-1)
    gate_values = jax.nn.sigmoid(chosen - chosen[:, ::-1])
    live = (jnp.arange(256, dtype=jnp.int32)[None, :] < lengths[:, None]).reshape(1024, 1)
    gates = jnp.sum(route_hot * gate_values[:, :, None], axis=1) * live.astype(F32)
    wide = jnp.broadcast_to(gates.T[:, :, None], (NE, 1024, 128))

    beside = [*first_step(near_mix[0], 1), *first_step(near_mix[1], 0)]
    down_part = pick_down(info, received)
    sums = project_stage(0, info, tokens, routes, near_mix, ())
    *beside, down_part, wide, q, base = lax.optimization_barrier(
        (*beside, down_part, wide, *sums)
    )
    down = lax.all_to_all(
        jnp.broadcast_to(down_part[None], (NE, 4, 16, 256)), "exp", 0, 0, tiled=True
    )
    last = [*second_step(*beside[:2], 1), *second_step(*beside[2:], 0)]
    sums = project_stage(1, info, tokens, routes, beside, (q, base))
    *rest, q, base, down = lax.optimization_barrier((*last, *near_out, *sums, down))
    last, near_out = rest[:4], rest[4:]
    out_beside = [*first_step(near_out[0], 1), *first_step(near_out[1], 0)]
    q, base = project_stage(2, info, tokens, routes, last, (q, base))
    lhs = [attention(0, info, tokens, routes, down, q, base, received)]
    *out_beside, lhs[0] = lax.optimization_barrier((*out_beside, lhs[0]))
    out_last = [*second_step(*out_beside[:2], 1), *second_step(*out_beside[2:], 0)]
    lhs.append(attention(1, info, tokens, routes, down, q, base, received))
    out_pieces = []
    for half in range(2):
        two = slice(half * 2, half * 2 + 2)
        out_pieces += [near_out[half], *out_beside[two], *out_last[two]]

    place = jnp.stack([group, part // 2, part % 2]).astype(jnp.int32)
    far = project_out(((False, 2), (True, 2)), place, wide, lhs, out_pieces)
    far_swapped = exchange(far[0], 0)
    place_next = lax.optimization_barrier((place, far))[0]
    theirs = project_out(((False, 1), (False, 3), (False, 0)), place_next, wide, lhs, out_pieces)
    swapped = exchange(theirs, 0)
    both_far = rounded_sum(far[1], far_swapped)
    low = exchange(both_far[:512], 1)
    high = exchange(both_far[512:], -1)
    place_last = lax.optimization_barrier((place, theirs, both_far))[0]
    mine = project_out(((True, 1), (True, 3), (True, 0)), place_last, wide, lhs, out_pieces)
    ahead = jnp.concatenate(
        [rounded_sum(mine[0, :512], swapped[0, :512], low), rounded_sum(mine[0, 512:], swapped[0, 512:])],
        axis=0,
    )
    behind = jnp.concatenate(
        [rounded_sum(mine[1, :512], swapped[1, :512]), rounded_sum(mine[1, 512:], swapped[1, 512:], high)],
        axis=0,
    )
    return rounded_sum(mine[2], swapped[2], exchange(ahead, 1), exchange(behind, -1))


def solution(mesh):
    return jax.shard_map(
        body,
        mesh=mesh,
        in_specs=(
            P("req", None),
            P("req", None),
            P("req"),
            P("req"),
            P(),
            P("req"),
            P(),
            P(),
            P("req", "exp"),
            P("req", None, "exp"),
            P(None, "exp", "req"),
            P("req", None, None),
            P("req", None, "exp"),
            P("req", None, "exp"),
        ),
        out_specs=P("req", "exp"),
        check_vma=False,
    )
```

```python
import functools

import jax
import jax.numpy as jnp
from jax import lax
from jax.experimental import pallas as pl
from jax.experimental.pallas import tpu as pltpu
from jax.sharding import PartitionSpec as P

HD = 128
NE = 8
TOPK = 2
SIDE = 4
BF = jnp.bfloat16
F32 = jnp.float32
NEG = -1e30
adapter_scale = 0.5

ROW_KV = 512
SHARD_ROWS = 640
OUT_ROWS = 512
ROW_UP, ROW_DN, SENT_ROWS = 64, 128, 160
PLACES = []
for _i, _off in enumerate((0, -1, 1, 2)):
    PLACES += [(2 * _i, 0, 0, _off), (2 * _i, 1, -1, _off)]
    PLACES += [(2 * _i + 1, 0, 1, _off), (2 * _i + 1, 1, 2, _off)]
STAGES = [range(0, 2), range(2, 6), range(6, 8)]


def torus(dx, dz):
    return [
        (i, ((i // SIDE + dx) % SIDE) * SIDE + (i % SIDE + dz) % SIDE) for i in range(SIDE * SIDE)
    ]


def send(value, along, step):
    return lax.ppermute(value, "req", torus(step, 0) if along == 0 else torus(0, step))


def outward(low, high, along):
    return send(low, along, 1), send(high, along, -1)


def inward(low, high, along):
    return send(high, along, 1), send(low, along, -1)


def source(group, half, first, second):
    x, z = group // SIDE, group % SIDE
    dx, dz = (first, second) if half == 0 else (second, first)
    return ((x + dx + SIDE) % SIDE) * SIDE + (z + dz + SIDE) % SIDE


def cost(us):
    return pl.CostEstimate(flops=int(us * 1.15e9), bytes_accessed=2**20, transcendentals=0)


ANY = pl.BlockSpec(memory_space=pl.ANY)
WHOLE = pl.BlockSpec(memory_space=pltpu.VMEM)
SCALARS = pl.BlockSpec(memory_space=pltpu.SMEM)


def pack_kernel(index_ref, store_ref, up_ref, down_ref, out_ref):
    def one(i, carry):
        out_ref[i, 0:ROW_UP, :] = store_ref[index_ref[i]]
        out_ref[i, ROW_UP:ROW_DN, :] = up_ref[...]
        for side in range(2):
            out_ref[i, ROW_DN:SENT_ROWS, side * 256 : side * 256 + 256] = down_ref[
                side * 32 : side * 32 + 32, :
            ]
        return carry

    lax.fori_loop(0, out_ref.shape[0], one, 0)


def pack(index, store, up, down):
    return pl.pallas_call(
        pack_kernel,
        out_shape=jax.ShapeDtypeStruct((16, SENT_ROWS, 512), BF),
        in_specs=[SCALARS] + [WHOLE] * 3,
        out_specs=WHOLE,
        cost_estimate=cost(3),
        name="pack",
    )(index, store, up, down)


def pick_down_kernel(info_ref, recv_ref, out_ref, sem):
    for j in range(4):
        slot = info_ref[1 + j]
        owner, inner = slot // 4, slot % 4
        start = pl.multiple_of(ROW_DN + (inner % 2) * 16, 16)
        for side in range(2):

            @pl.when(inner // 2 == side)
            def _(side=side, j=j, owner=owner, start=start):
                pltpu.make_async_copy(
                    recv_ref.at[owner, pl.ds(start, 16), pl.ds(side * 256, 256)],
                    out_ref.at[j],
                    sem.at[j],
                ).start()

    for j in range(4):
        pltpu.make_async_copy(out_ref.at[j], out_ref.at[j], sem.at[j]).wait()


def pick_down(info, recv):
    return pl.pallas_call(
        pick_down_kernel,
        out_shape=jax.ShapeDtypeStruct((4, 16, 256), BF),
        in_specs=[SCALARS, ANY],
        out_specs=WHOLE,
        scratch_shapes=[pltpu.SemaphoreType.DMA((4,))],
        cost_estimate=cost(2),
        name="pick_down",
    )(info, recv)


def stage_kernel(stage, info_ref, x_ref, routes_ref, *refs):
    names = STAGES[stage]
    count = len(names)
    shards = [place for place in PLACES if place[0] in names]
    pieces, refs = refs[: 2 * count], refs[2 * count :]
    if stage == 0:
        gates_ref, q_out, kv_out, wide_ref = refs
        for e in range(NE):
            wide_ref[e] = jnp.broadcast_to(gates_ref[:, e : e + 1], (256, 128))
    else:
        q_in, kv_in, q_out, kv_out = refs
    group = info_ref[0]
    chosen = [jnp.zeros((256, 256), F32)] * TOPK
    for half in range(2):
        x = jnp.concatenate(
            [
                x_ref[:, pl.ds(pl.multiple_of(source(group, half, first, second) * 128, 128), 128)]
                for _, _, first, second in shards
            ],
            axis=1,
        )

        def product(row, half=half, x=x):
            weight = jnp.concatenate(
                [
                    pieces[half * count + piece - names[0]][
                        pl.ds(shard * SHARD_ROWS + row, 128), :
                    ]
                    for piece, shard, _, _ in shards
                ],
                axis=0,
            )
            return jnp.dot(x, weight, preferred_element_type=F32)

        for i in range(4):
            value = product(i * 128)
            for k in range(TOPK):
                mine = routes_ref[:, k : k + 1] == half * 4 + i
                chosen[k] = jnp.where(mine, value, chosen[k])
        value = product(ROW_KV)
        kv_out[half] = value if stage == 0 else value + kv_in[half]
    for k in range(TOPK):
        value = chosen[k] if stage == 0 else chosen[k] + q_in[k]
        q_out[k] = value.astype(q_out.dtype)


def row_block(*lead):
    return pl.BlockSpec((*lead, 256, 256), lambda j: (0,) * len(lead) + (j, 0))


def project_stage(stage, info, x, routes, pieces, rest):
    kind = BF if stage == 2 else F32
    shapes = [
        jax.ShapeDtypeStruct((TOPK, 1024, 256), kind),
        jax.ShapeDtypeStruct((2, 1024, 256), F32),
    ]
    out_specs = [row_block(2), row_block(2)]
    if stage == 0:
        rest_specs = [pl.BlockSpec((256, NE), lambda j: (j, 0))]
        shapes.append(jax.ShapeDtypeStruct((NE, 1024, 128), F32))
        out_specs.append(pl.BlockSpec((NE, 256, 128), lambda j: (0, j, 0)))
    else:
        rest_specs = [row_block(2), row_block(2)]
    return pl.pallas_call(
        functools.partial(stage_kernel, stage),
        out_shape=shapes,
        grid=(4,),
        in_specs=[
            SCALARS,
            pl.BlockSpec((256, 2048), lambda j: (j, 0)),
            pl.BlockSpec((256, TOPK), lambda j: (j, 0)),
        ]
        + [WHOLE] * len(pieces)
        + rest_specs,
        out_specs=out_specs,
        compiler_params=pltpu.CompilerParams(vmem_limit_bytes=20 * 2**20),
        cost_estimate=cost((5, 10, 5)[stage]),
        name="project_stage_" + str(stage),
    )(info, x, routes, *pieces, *rest)


def attend_kernel(
    part, info_ref, x_ref, routes_ref, down_ref, q_ref, base_ref, recv_ref, out_ref, up, cache, sem
):
    j = part * 2 + pl.program_id(0)
    slot = info_ref[1 + j]
    start = pl.multiple_of(ROW_UP + (slot % 4) * 16, 16)
    copies = [
        pltpu.make_async_copy(recv_ref.at[slot // 4, pl.ds(start, 16), :], up, sem.at[0]),
        pltpu.make_async_copy(recv_ref.at[info_ref[5 + j], pl.ds(0, 64), :], cache, sem.at[1]),
    ]
    for copy in copies:
        copy.start()
    down = jnp.concatenate([down_ref[e, j] for e in range(NE)], axis=1)
    low = lax.dot_general(
        x_ref[...], down, (((1,), (1,)), ((), ())), preferred_element_type=F32
    ).astype(BF)
    for copy in copies:
        copy.wait()
    cached_length = info_ref[9 + j]
    place = lax.broadcasted_iota(jnp.int32, (256, 320), 1)
    query_at = lax.broadcasted_iota(jnp.int32, (256, 320), 0)
    allowed = (place < cached_length) | ((place >= 64) & (place - 64 <= query_at))
    for h in range(2):
        cols = slice(h * HD, (h + 1) * HD)
        extra = jnp.dot(low, up[:, h * 256 : h * 256 + 256], preferred_element_type=F32)
        fresh = (base_ref[h] + adapter_scale * extra).astype(BF)
        keys = jnp.concatenate(
            [cache[:, h * 256 : h * 256 + HD], fresh[:, 0:HD]], axis=0
        )
        values = jnp.concatenate(
            [cache[:, h * 256 + HD : h * 256 + 2 * HD], fresh[:, HD : 2 * HD]], axis=0
        )
        attended = []
        for k in range(TOPK):
            scores = lax.dot_general(
                q_ref[k, :, cols], keys, (((1,), (1,)), ((), ())), preferred_element_type=F32
            ) * (HD**-0.5)
            scores = jnp.where(allowed, scores, NEG)
            weights = jnp.exp(scores - jnp.max(scores, axis=-1, keepdims=True))
            total = jnp.sum(weights, axis=-1, keepdims=True)
            probability = (weights * (1.0 / total)).astype(BF)
            attended.append(jnp.dot(probability, values, preferred_element_type=F32))
        for e in range(NE):
            chosen = jnp.where(
                routes_ref[:, 0:1] == e,
                attended[0],
                jnp.where(routes_ref[:, 1:2] == e, attended[1], 0.0),
            )
            out_ref[e, :, cols] = chosen.astype(BF)


def attention(part, info, x, routes, down, q, base, recv):
    return pl.pallas_call(
        functools.partial(attend_kernel, part),
        out_shape=jax.ShapeDtypeStruct((NE, 512, 256), BF),
        grid=(2,),
        in_specs=[
            SCALARS,
            pl.BlockSpec((256, 2048), lambda i: (part * 2 + i, 0)),
            pl.BlockSpec((256, TOPK), lambda i: (part * 2 + i, 0)),
            WHOLE,
            pl.BlockSpec((TOPK, 256, 256), lambda i: (0, part * 2 + i, 0)),
            pl.BlockSpec((2, 256, 256), lambda i: (0, part * 2 + i, 0)),
            ANY,
        ],
        out_specs=pl.BlockSpec((NE, 256, 256), lambda i: (0, i, 0)),
        scratch_shapes=[
            pltpu.VMEM((16, 512), BF),
            pltpu.VMEM((64, 512), BF),
            pltpu.SemaphoreType.DMA((2,)),
        ],
        compiler_params=pltpu.CompilerParams(vmem_limit_bytes=20 * 2**20),
        cost_estimate=cost(9),
        name="attention_" + str(part),
    )(info, x, routes, down, q, base, recv)


def project_out_kernel(blocks, place_ref, wide_ref, low_ref, high_ref, *refs):
    pieces = refs[:16]
    out_ref, w, sem = refs[16:]
    group, y, core = place_ref[0], place_ref[1], place_ref[2]
    for b, (mine, ahead) in enumerate(blocks):
        wanted_x = (y + ahead) % 4
        side = core if mine else 1 - core
        for half in range(2):
            for piece, shard, first, second in PLACES:
                owner = source(group, half, first, second)

                @pl.when((owner // 4 == wanted_x) & ((owner % 4) // 2 == side))
                def _(b=b, half=half, piece=piece, shard=shard, owner=owner):
                    pltpu.make_async_copy(
                        pieces[half * 8 + piece].at[pl.ds(shard * OUT_ROWS, OUT_ROWS), :],
                        w.at[b, half, owner % 2],
                        sem.at[b],
                    ).start()

    def tile(b, lhs_ref, part, i):
        rows = pl.ds(pl.multiple_of(i * 256, 256), 256)
        gate_rows = pl.ds(pl.multiple_of(part * 512 + i * 256, 256), 256)
        total = None
        for e in range(NE):
            half, pair, lane = e // 4, (e % 4) // 2, e % 2
            place = (pl.ds(pair * 256, 256), pl.ds(lane * 128, 128))
            weight = jnp.concatenate(
                [w[b, half, 0, place[0], place[1]], w[b, half, 1, place[0], place[1]]], axis=1
            )
            value = jnp.dot(lhs_ref[e, rows, :], weight, preferred_element_type=F32)
            gate = wide_ref[e, gate_rows, :]
            value = value * jnp.concatenate([gate, gate], axis=1)
            total = value if total is None else total + value
        out_ref[b, gate_rows, :] = total.astype(BF)

    def block(b, carry):
        pltpu.make_async_copy(w.at[b], w.at[b], sem.at[b]).wait()
        for part, lhs_ref in enumerate((low_ref, high_ref)):

            def step(i, inner, lhs_ref=lhs_ref, part=part):
                tile(b, lhs_ref, part, i)
                return inner

            lax.fori_loop(0, 2, step, 0)
        return carry

    lax.fori_loop(0, len(blocks), block, 0)


def project_out(blocks, place, wide, lhs, pieces):
    return pl.pallas_call(
        functools.partial(project_out_kernel, blocks),
        out_shape=jax.ShapeDtypeStruct((len(blocks), 1024, 256), BF),
        in_specs=[SCALARS, WHOLE, WHOLE, WHOLE] + [ANY] * 16,
        out_specs=WHOLE,
        scratch_shapes=[
            pltpu.VMEM((len(blocks), 2, 2, OUT_ROWS, 256), BF),
            pltpu.SemaphoreType.DMA((len(blocks),)),
        ],
        compiler_params=pltpu.CompilerParams(vmem_limit_bytes=16 * 2**20),
        cost_estimate=cost(2.2 * len(blocks)),
        name="project_out_" + str(len(blocks)),
    )(place, wide, *lhs, *pieces)


def exchange(value, step):
    if step == 0:
        return lax.ppermute(value, "exp", [(i, i ^ 1) for i in range(8)])
    return lax.ppermute(value, "exp", [(i, (i + 2 * step) % 8) for i in range(8)])


def rounded_sum(*values):
    total = values[0].astype(F32)
    for value in values[1:]:
        total = total + value.astype(F32)
    return total.astype(BF)


def body(
    tokens,
    routes,
    lengths,
    cached_prefix_length,
    prefix_cache_row,
    adapter_per_request,
    adapter_storage_slot,
    router_weight,
    key_value_weight,
    expert_query_weight,
    expert_output_weight,
    adapter_down_maps,
    adapter_up_maps,
    prefix_cache_store,
):
    group = lax.axis_index("req")
    part = lax.axis_index("exp")
    rows_by_group = prefix_cache_row.reshape(16, 4)
    held = (rows_by_group == group).astype(jnp.int32)
    wanted_by = jnp.sum(held * jnp.arange(4, dtype=jnp.int32)[None, :], axis=1)
    down_rows = (
        lax.dynamic_slice_in_dim(adapter_down_maps, part * 256, 256, 1)
        .transpose(0, 2, 1)
        .reshape(64, 256)
    )
    outgoing = pack(wanted_by, prefix_cache_store, adapter_up_maps.reshape(64, 512), down_rows)

    query_rows = expert_query_weight.transpose(1, 0, 2).reshape(NE * 128, 256)
    out_rows = (
        expert_output_weight.reshape(4, 2, 256, 128).transpose(0, 2, 1, 3).reshape(1024, 256)
    )
    own_mix, own_out = [], []
    for half in range(2):
        own_mix.append(
            jnp.concatenate(
                [
                    query_rows[half * 512 : half * 512 + 512],
                    key_value_weight[:, half * 256 : half * 256 + 256],
                ],
                axis=0,
            )
        )
        own_out.append(out_rows[half * 512 : half * 512 + 512])
    *own_mix, outgoing = lax.optimization_barrier((*own_mix, outgoing))
    received = lax.all_to_all(outgoing, "req", 0, 0, tiled=True)
    mix_low, mix_high, out_low, out_high = [], [], [], []
    for half in range(2):
        mix_before, out_after = outward(own_mix[half], own_out[half], half)
        out_before, mix_after = inward(own_mix[half], own_out[half], half)
        mix_far, out_far = outward(mix_before, out_after, half)
        mix_low.append(jnp.concatenate([own_mix[half], mix_before], axis=0))
        mix_high.append(jnp.concatenate([mix_after, mix_far], axis=0))
        out_low.append(jnp.concatenate([own_out[half], out_before], axis=0))
        out_high.append(jnp.concatenate([out_after, out_far], axis=0))

    adapter_hot = (
        adapter_per_request[:, None]
        == jnp.arange(adapter_storage_slot.shape[0], dtype=jnp.int32)[None, :]
    ).astype(jnp.int32)
    slots = jnp.sum(adapter_hot * adapter_storage_slot[None, :], axis=1)
    own_rows = lax.dynamic_slice_in_dim(prefix_cache_row, group * 4, 4, 0)
    info = jnp.concatenate([group[None].astype(jnp.int32), slots, own_rows, cached_prefix_length])

    logits = jnp.dot(tokens, router_weight, preferred_element_type=F32)
    expert = jnp.arange(NE, dtype=jnp.int32)
    route_hot = (routes[:, :, None] == expert[None, None, :]).astype(F32)
    chosen = jnp.sum(route_hot * logits[:, None, :], axis=-1)
    gate_values = jax.nn.sigmoid(chosen - chosen[:, ::-1])
    live = (jnp.arange(256, dtype=jnp.int32)[None, :] < lengths[:, None]).reshape(1024, 1)
    gates = jnp.sum(route_hot * gate_values[:, :, None], axis=1) * live.astype(F32)

    ahead_of = [outward(mix_low[half], mix_high[half], 1 - half) for half in range(2)]
    beside = [inward(mix_low[half], mix_high[half], 1 - half) for half in range(2)]
    down_part = pick_down(info, received)
    gates, down_part = lax.optimization_barrier((gates, down_part))
    down = lax.all_to_all(
        jnp.broadcast_to(down_part[None], (NE, 4, 16, 256)), "exp", 0, 0, tiled=True
    )
    near = [mix_low[0], mix_high[0], mix_low[1], mix_high[1]]
    q, base, wide = project_stage(0, info, tokens, routes, near, (gates,))
    *onward, q = lax.optimization_barrier((*ahead_of[0], *ahead_of[1], q))
    far = [*outward(*onward[:2], 1), *outward(*onward[2:], 0)]
    middle = []
    for half in range(2):
        middle += [onward[2 * half], beside[half][0], beside[half][1], onward[2 * half + 1]]
    q, base = project_stage(1, info, tokens, routes, middle, (q, base))
    rest = lax.optimization_barrier((*far, *out_low, *out_high))
    far, out_low, out_high = rest[:4], rest[4:6], rest[6:8]
    out_ahead = [outward(out_low[half], out_high[half], 1 - half) for half in range(2)]
    out_beside = [inward(out_low[half], out_high[half], 1 - half) for half in range(2)]
    q, base = project_stage(2, info, tokens, routes, far, (q, base))
    lhs = [attention(0, info, tokens, routes, down, q, base, received)]
    *onward, lhs[0] = lax.optimization_barrier((*out_ahead[0], *out_ahead[1], lhs[0]))
    out_far = [*outward(*onward[:2], 1), *outward(*onward[2:], 0)]
    lhs.append(attention(1, info, tokens, routes, down, q, base, received))
    out_pieces = []
    for half in range(2):
        out_pieces += [out_low[half], out_high[half]]
        out_pieces += [onward[2 * half], out_beside[half][0], out_beside[half][1]]
        out_pieces += [onward[2 * half + 1], out_far[2 * half], out_far[2 * half + 1]]

    place = jnp.stack([group, part // 2, part % 2]).astype(jnp.int32)
    far = project_out(((False, 2), (True, 2)), place, wide, lhs, out_pieces)
    far_swapped = exchange(far[0], 0)
    place = lax.optimization_barrier((place, far))[0]
    theirs = project_out(((False, 1), (False, 3)), place, wide, lhs, out_pieces)
    swapped = exchange(theirs, 0)
    both_far = rounded_sum(far[1], far_swapped)
    low = exchange(both_far[:512], 1)
    high = exchange(both_far[512:], -1)
    place = lax.optimization_barrier((place, theirs, both_far))[0]
    mine = project_out(((True, 1), (True, 3)), place, wide, lhs, out_pieces)
    ahead = jnp.concatenate(
        [rounded_sum(mine[0, :512], swapped[0, :512], low), rounded_sum(mine[0, 512:], swapped[0, 512:])],
        axis=0,
    )
    behind = jnp.concatenate(
        [rounded_sum(mine[1, :512], swapped[1, :512]), rounded_sum(mine[1, 512:], swapped[1, 512:], high)],
        axis=0,
    )
    from_behind, from_ahead = exchange(ahead, 1), exchange(behind, -1)
    place = lax.optimization_barrier((place, ahead, behind))[0]
    own = project_out(((False, 0), (True, 0)), place, wide, lhs, out_pieces)
    return rounded_sum(own[1], exchange(own[0], 0), from_behind, from_ahead)


def solution(mesh):
    return jax.shard_map(
        body,
        mesh=mesh,
        in_specs=(
            P("req", None),
            P("req", None),
            P("req"),
            P("req"),
            P(),
            P("req"),
            P(),
            P(),
            P("req", "exp"),
            P("req", None, "exp"),
            P(None, "exp", "req"),
            P("req", None, None),
            P("req", None, "exp"),
            P("req", None, "exp"),
        ),
        out_specs=P("req", "exp"),
        check_vma=False,
    )
```

```python
import functools

import jax
import jax.numpy as jnp
from jax import lax
from jax.experimental import pallas as pl
from jax.experimental.pallas import tpu as pltpu
from jax.sharding import PartitionSpec as P

HD = 128
NE = 8
TOPK = 2
SIDE = 4
BF = jnp.bfloat16
F32 = jnp.float32
NEG = -1e30
adapter_scale = 0.5

ROW_KV = 512
SHARD_ROWS = 640
ROW_UP, ROW_DN, SENT_ROWS = 64, 128, 160
PLACES = []
for _piece, _off in ((0, 0), (1, -1), (2, 1)):
    for _i, _near in enumerate((0, -1, 1, 2)):
        PLACES.append((_piece, _i, _near, _off))
EARLY = list(PLACES)
LATE = [(0, 0, 0, 2), (0, 1, -1, 2), (1, 0, 1, 2), (1, 1, 2, 2)]


def torus(dx, dz):
    return [
        (i, ((i // SIDE + dx) % SIDE) * SIDE + (i % SIDE + dz) % SIDE) for i in range(SIDE * SIDE)
    ]


def send(value, along, step):
    return lax.ppermute(value, "req", torus(step, 0) if along == 0 else torus(0, step))


def first_step(value, along):
    return send(value, along, 1), send(value, along, -1)


def second_step(before, after, along):
    half = before.shape[0] // 2
    return send(before[:half], along, 1), send(after[half:], along, -1)


def source(group, half, first, second):
    x, z = group // SIDE, group % SIDE
    dx, dz = (first, second) if half == 0 else (second, first)
    return ((x + dx + SIDE) % SIDE) * SIDE + (z + dz + SIDE) % SIDE


def cost(us):
    return pl.CostEstimate(flops=int(us * 1.15e9), bytes_accessed=2**20, transcendentals=0)


ANY = pl.BlockSpec(memory_space=pl.ANY)
HBM = pl.BlockSpec(memory_space=pltpu.HBM)
WHOLE = pl.BlockSpec(memory_space=pltpu.VMEM)
SCALARS = pl.BlockSpec(memory_space=pltpu.SMEM)


def pack_kernel(index_ref, store_ref, up_ref, down_ref, out_ref):
    def one(i, carry):
        out_ref[i, 0:ROW_UP, :] = store_ref[index_ref[i]]
        out_ref[i, ROW_UP:ROW_DN, :] = up_ref[...]
        for side in range(2):
            out_ref[i, ROW_DN:SENT_ROWS, side * 256 : side * 256 + 256] = down_ref[
                side * 32 : side * 32 + 32, :
            ]
        return carry

    lax.fori_loop(0, out_ref.shape[0], one, 0)


def pack(index, store, up, down):
    return pl.pallas_call(
        pack_kernel,
        out_shape=jax.ShapeDtypeStruct((16, SENT_ROWS, 512), BF),
        in_specs=[SCALARS] + [WHOLE] * 3,
        out_specs=WHOLE,
        cost_estimate=cost(3),
        name="pack",
    )(index, store, up, down)


def pick_down_kernel(info_ref, recv_ref, out_ref, sem):
    for j in range(4):
        slot = info_ref[1 + j]
        owner, inner = slot // 4, slot % 4
        start = pl.multiple_of(ROW_DN + (inner % 2) * 16, 16)
        for side in range(2):

            @pl.when(inner // 2 == side)
            def _(side=side, j=j, owner=owner, start=start):
                pltpu.make_async_copy(
                    recv_ref.at[owner, pl.ds(start, 16), pl.ds(side * 256, 256)],
                    out_ref.at[j],
                    sem.at[j],
                ).start()

    for j in range(4):
        pltpu.make_async_copy(out_ref.at[j], out_ref.at[j], sem.at[j]).wait()


def pick_down(info, recv):
    return pl.pallas_call(
        pick_down_kernel,
        out_shape=jax.ShapeDtypeStruct((4, 16, 256), BF),
        in_specs=[SCALARS, ANY],
        out_specs=WHOLE,
        scratch_shapes=[pltpu.SemaphoreType.DMA((4,))],
        cost_estimate=cost(2),
        name="pick_down",
    )(info, recv)


def products(group, x_ref, routes_ref, pieces, shards, half):
    count = len(pieces) // 2
    x = jnp.concatenate(
        [
            x_ref[:, pl.ds(pl.multiple_of(source(group, half, first, second) * 128, 128), 128)]
            for _, _, first, second in shards
        ],
        axis=1,
    )

    def product(row):
        weight = jnp.concatenate(
            [
                pieces[half * count + piece][pl.ds(shard * SHARD_ROWS + row, 128), :]
                for piece, shard, _, _ in shards
            ],
            axis=0,
        )
        return jnp.dot(x, weight, preferred_element_type=F32)

    chosen = [jnp.zeros((256, 256), F32)] * TOPK
    for i in range(4):
        value = product(i * 128)
        for k in range(TOPK):
            chosen[k] = jnp.where(routes_ref[:, k : k + 1] == half * 4 + i, value, chosen[k])
    return chosen, product(ROW_KV)


def early_kernel(info_ref, gates_ref, routes_ref, x_hbm, *refs):
    pieces = refs[:6]
    wide_ref, sums_hbm, x, sums, sem = refs[6:]
    group = info_ref[0]
    loads = [
        pltpu.make_async_copy(x_hbm.at[pl.ds(j * 256, 256), :], x.at[j], sem.at[j])
        for j in range(4)
    ]
    for load in loads:
        load.start()
    for e in range(NE):
        wide_ref[e] = jnp.broadcast_to(gates_ref[:, e : e + 1], (1024, 128))

    def block(j, carry):
        pltpu.make_async_copy(x.at[j], x.at[j], sem.at[j]).wait()
        rows = routes_ref.at[pl.ds(pl.multiple_of(j * 256, 256), 256), :]
        first, base = products(group, x.at[j], rows, pieces, EARLY, 0)
        sums[j, 2] = base
        second, base = products(group, x.at[j], rows, pieces, EARLY, 1)
        sums[j, 3] = base
        for k in range(TOPK):
            sums[j, k] = first[k] + second[k]
        pltpu.make_async_copy(sums.at[j], sums_hbm.at[j], sem.at[4 + j]).start()
        return carry

    lax.fori_loop(0, 4, block, 0)
    for j in range(4):
        pltpu.make_async_copy(sums.at[j], sums_hbm.at[j], sem.at[4 + j]).wait()


def project_early(info, gates, routes, x, pieces):
    return pl.pallas_call(
        early_kernel,
        out_shape=(
            jax.ShapeDtypeStruct((NE, 1024, 128), F32),
            jax.ShapeDtypeStruct((4, 4, 256, 256), F32),
        ),
        in_specs=[SCALARS, WHOLE, WHOLE, HBM] + [WHOLE] * 6,
        out_specs=(WHOLE, HBM),
        scratch_shapes=[
            pltpu.VMEM((4, 256, 2048), BF),
            pltpu.VMEM((4, 4, 256, 256), F32),
            pltpu.SemaphoreType.DMA((8,)),
        ],
        compiler_params=pltpu.CompilerParams(vmem_limit_bytes=24 * 2**20),
        cost_estimate=cost(15),
        name="project_early",
    )(info, gates, routes, x, *pieces)


def attend_kernel(info_ref, routes_ref, down_ref, x_hbm, sums_hbm, recv_hbm, *refs):
    pieces = refs[:4]
    out_ref, x, sums, up, cache, sem = refs[4:]
    group = info_ref[0]
    for j in range(4):
        slot = info_ref[1 + j]
        start = pl.multiple_of(ROW_UP + (slot % 4) * 16, 16)
        pltpu.make_async_copy(x_hbm.at[pl.ds(j * 256, 256), :], x.at[j], sem.at[0, j]).start()
        pltpu.make_async_copy(sums_hbm.at[j], sums.at[j], sem.at[1, j]).start()
        pltpu.make_async_copy(
            recv_hbm.at[slot // 4, pl.ds(start, 16), :], up.at[j], sem.at[2, j]
        ).start()
        pltpu.make_async_copy(
            recv_hbm.at[info_ref[5 + j], pl.ds(0, 64), :], cache.at[j], sem.at[3, j]
        ).start()

    def attend(j, carry):
        for i, ref in enumerate((x, sums, up, cache)):
            pltpu.make_async_copy(ref.at[j], ref.at[j], sem.at[i, j]).wait()
        rows = pl.ds(pl.multiple_of(j * 256, 256), 256)
        routes = routes_ref.at[rows, :]
        for half in range(2):
            chosen, base = products(group, x.at[j], routes, pieces, LATE, half)
            sums[j, 2 + half] += base
            for k in range(TOPK):
                sums[j, k] += chosen[k]
        down = jnp.concatenate([down_ref[e, j] for e in range(NE)], axis=1)
        low = lax.dot_general(
            x[j], down, (((1,), (1,)), ((), ())), preferred_element_type=F32
        ).astype(BF)
        cached_length = info_ref[9 + j]
        place = lax.broadcasted_iota(jnp.int32, (256, 320), 1)
        query_at = lax.broadcasted_iota(jnp.int32, (256, 320), 0)
        allowed = (place < cached_length) | ((place >= 64) & (place - 64 <= query_at))
        for h in range(2):
            cols = slice(h * HD, (h + 1) * HD)
            extra = jnp.dot(low, up[j, :, h * 256 : h * 256 + 256], preferred_element_type=F32)
            fresh = (sums[j, 2 + h] + adapter_scale * extra).astype(BF)
            keys = jnp.concatenate(
                [cache[j, :, h * 256 : h * 256 + HD], fresh[:, 0:HD]], axis=0
            )
            values = jnp.concatenate(
                [cache[j, :, h * 256 + HD : h * 256 + 2 * HD], fresh[:, HD : 2 * HD]], axis=0
            )
            attended = []
            for k in range(TOPK):
                scores = lax.dot_general(
                    sums[j, k, :, cols].astype(BF),
                    keys,
                    (((1,), (1,)), ((), ())),
                    preferred_element_type=F32,
                ) * (HD**-0.5)
                scores = jnp.where(allowed, scores, NEG)
                weights = jnp.exp(scores - jnp.max(scores, axis=-1, keepdims=True))
                total = jnp.sum(weights, axis=-1, keepdims=True)
                probability = (weights * (1.0 / total)).astype(BF)
                attended.append(jnp.dot(probability, values, preferred_element_type=F32))
            for e in range(NE):
                chosen = jnp.where(
                    routes[:, 0:1] == e,
                    attended[0],
                    jnp.where(routes[:, 1:2] == e, attended[1], 0.0),
                )
                out_ref[e, rows, cols] = chosen.astype(BF)
        return carry

    lax.fori_loop(0, 4, attend, 0)


def attention(info, routes, down, x, sums, recv, pieces):
    return pl.pallas_call(
        attend_kernel,
        out_shape=jax.ShapeDtypeStruct((NE, 1024, 256), BF),
        in_specs=[SCALARS, WHOLE, WHOLE, HBM, HBM, ANY] + [WHOLE] * 4,
        out_specs=WHOLE,
        scratch_shapes=[
            pltpu.VMEM((4, 256, 2048), BF),
            pltpu.VMEM((4, 4, 256, 256), F32),
            pltpu.VMEM((4, 16, 512), BF),
            pltpu.VMEM((4, 64, 512), BF),
            pltpu.SemaphoreType.DMA((4, 4)),
        ],
        compiler_params=pltpu.CompilerParams(vmem_limit_bytes=24 * 2**20),
        cost_estimate=cost(22),
        name="attention",
    )(info, routes, down, x, sums, recv, *pieces)


def project_out_kernel(blocks, place_ref, wide_ref, lhs_ref, w_hbm, out_ref, w, sem):
    y, core = place_ref[0], place_ref[1]
    for b, (mine, ahead) in enumerate(blocks):
        side = core if mine else 1 - core
        start = ((y + ahead) % 4 * 2 + side) * 2
        pltpu.make_async_copy(w_hbm.at[pl.ds(start, 2)], w.at[b], sem.at[b]).start()

    def block(b, carry):
        pltpu.make_async_copy(w.at[b], w.at[b], sem.at[b]).wait()

        def tile(i, inner):
            rows = pl.ds(pl.multiple_of(i * 256, 256), 256)
            total = None
            for e in range(NE):
                weight = jnp.concatenate([w[b, 0, e], w[b, 1, e]], axis=1)
                value = jnp.dot(lhs_ref[e, rows, :], weight, preferred_element_type=F32)
                gate = wide_ref[e, rows, :]
                value = value * jnp.concatenate([gate, gate], axis=1)
                total = value if total is None else total + value
            out_ref[b, rows, :] = total.astype(BF)
            return inner

        return lax.fori_loop(0, 4, tile, carry)

    lax.fori_loop(0, len(blocks), block, 0)


def project_out(blocks, place, wide, lhs, weight):
    return pl.pallas_call(
        functools.partial(project_out_kernel, blocks),
        out_shape=jax.ShapeDtypeStruct((len(blocks), 1024, 256), BF),
        in_specs=[SCALARS, WHOLE, WHOLE, HBM],
        out_specs=WHOLE,
        scratch_shapes=[
            pltpu.VMEM((len(blocks), 2, NE, 256, 128), BF),
            pltpu.SemaphoreType.DMA((len(blocks),)),
        ],
        compiler_params=pltpu.CompilerParams(vmem_limit_bytes=16 * 2**20),
        cost_estimate=cost(2.5 * len(blocks)),
        name="project_out_" + str(len(blocks)),
    )(place, wide, lhs, weight)


def exchange(value, step):
    if step == 0:
        return lax.ppermute(value, "exp", [(i, i ^ 1) for i in range(8)])
    return lax.ppermute(value, "exp", [(i, (i + 2 * step) % 8) for i in range(8)])


def rounded_sum(*values):
    total = values[0].astype(F32)
    for value in values[1:]:
        total = total + value.astype(F32)
    return total.astype(BF)


def body(
    tokens,
    routes,
    lengths,
    cached_prefix_length,
    prefix_cache_row,
    adapter_per_request,
    adapter_storage_slot,
    router_weight,
    key_value_weight,
    expert_query_weight,
    expert_output_weight,
    adapter_down_maps,
    adapter_up_maps,
    prefix_cache_store,
):
    group = lax.axis_index("req")
    part = lax.axis_index("exp")
    out_weight = lax.all_gather(expert_output_weight, "req", axis=0, tiled=True).reshape(
        16, NE, 256, 128
    )
    rows_by_group = prefix_cache_row.reshape(16, 4)
    held = (rows_by_group == group).astype(jnp.int32)
    wanted_by = jnp.sum(held * jnp.arange(4, dtype=jnp.int32)[None, :], axis=1)
    down_rows = (
        lax.dynamic_slice_in_dim(adapter_down_maps, part * 256, 256, 1)
        .transpose(0, 2, 1)
        .reshape(64, 256)
    )
    outgoing = pack(wanted_by, prefix_cache_store, adapter_up_maps.reshape(64, 512), down_rows)

    query_rows = expert_query_weight.transpose(1, 0, 2).reshape(NE * 128, 256)
    own = [
        jnp.concatenate(
            [
                query_rows[half * 512 : half * 512 + 512],
                key_value_weight[:, half * 256 : half * 256 + 256],
            ],
            axis=0,
        )
        for half in range(2)
    ]
    *own, outgoing = lax.optimization_barrier((*own, outgoing))
    received = lax.all_to_all(outgoing, "req", 0, 0, tiled=True)
    near = []
    for half in range(2):
        before, after = first_step(own[half], half)
        far = second_step(before, after, half)
        near.append(jnp.concatenate([own[half], before, after, *far], axis=0))

    adapter_hot = (
        adapter_per_request[:, None]
        == jnp.arange(adapter_storage_slot.shape[0], dtype=jnp.int32)[None, :]
    ).astype(jnp.int32)
    slots = jnp.sum(adapter_hot * adapter_storage_slot[None, :], axis=1)
    own_rows = lax.dynamic_slice_in_dim(prefix_cache_row, group * 4, 4, 0)
    info = jnp.concatenate([group[None].astype(jnp.int32), slots, own_rows, cached_prefix_length])

    logits = jnp.dot(tokens, router_weight, preferred_element_type=F32)
    expert = jnp.arange(NE, dtype=jnp.int32)
    route_hot = (routes[:, :, None] == expert[None, None, :]).astype(F32)
    chosen = jnp.sum(route_hot * logits[:, None, :], axis=-1)
    gate_values = jax.nn.sigmoid(chosen - chosen[:, ::-1])
    live = (jnp.arange(256, dtype=jnp.int32)[None, :] < lengths[:, None]).reshape(1024, 1)
    gates = jnp.sum(route_hot * gate_values[:, :, None], axis=1) * live.astype(F32)
    wide = jnp.broadcast_to(gates.T[:, :, None], (NE, 1024, 128))

    beside = [*first_step(near[0], 1), *first_step(near[1], 0)]
    down_part = pick_down(info, received)
    down = lax.all_to_all(
        jnp.broadcast_to(down_part[None], (NE, 4, 16, 256)), "exp", 0, 0, tiled=True
    )
    *beside, down = lax.optimization_barrier((*beside, down))
    late = [*second_step(*beside[:2], 1), *second_step(*beside[2:], 0)]
    wide, sums = project_early(
        info, gates, routes, tokens, [near[0], *beside[:2], near[1], *beside[2:]]
    )
    lhs = attention(info, routes, down, tokens, sums, received, late)

    place = jnp.stack([part // 2, part % 2]).astype(jnp.int32)
    far = project_out(((False, 2), (True, 2)), place, wide, lhs, out_weight)
    far_swapped = exchange(far[0], 0)
    place = lax.optimization_barrier((place, far))[0]
    theirs = project_out(((False, 1), (False, 3), (False, 0)), place, wide, lhs, out_weight)
    swapped = exchange(theirs, 0)
    both_far = rounded_sum(far[1], far_swapped)
    low = exchange(both_far[:512], 1)
    high = exchange(both_far[512:], -1)
    place = lax.optimization_barrier((place, theirs, both_far))[0]
    mine = project_out(((True, 1), (True, 3)), place, wide, lhs, out_weight)
    ahead = jnp.concatenate(
        [rounded_sum(mine[0, :512], swapped[0, :512], low), rounded_sum(mine[0, 512:], swapped[0, 512:])],
        axis=0,
    )
    behind = jnp.concatenate(
        [rounded_sum(mine[1, :512], swapped[1, :512]), rounded_sum(mine[1, 512:], swapped[1, 512:], high)],
        axis=0,
    )
    from_behind, from_ahead = exchange(ahead, 1), exchange(behind, -1)
    place = lax.optimization_barrier((place, ahead, behind))[0]
    own_block = project_out(((True, 0),), place, wide, lhs, out_weight)
    return rounded_sum(own_block[0], swapped[2], from_behind, from_ahead)


def solution(mesh):
    return jax.shard_map(
        body,
        mesh=mesh,
        in_specs=(
            P("req", None),
            P("req", None),
            P("req"),
            P("req"),
            P(),
            P("req"),
            P(),
            P(),
            P("req", "exp"),
            P("req", None, "exp"),
            P(None, "exp", "req"),
            P("req", None, None),
            P("req", None, "exp"),
            P("req", None, "exp"),
        ),
        out_specs=P("req", "exp"),
        check_vma=False,
    )
```

```python
import functools

import jax
import jax.numpy as jnp
from jax import lax
from jax.experimental import pallas as pl
from jax.experimental.pallas import tpu as pltpu
from jax.sharding import PartitionSpec as P

HD = 128
NE = 8
TOPK = 2
SIDE = 4
BF = jnp.bfloat16
F32 = jnp.float32
NEG = -1e30
adapter_scale = 0.5

ROW_KV = 512
SHARD_ROWS = 640
OUT_ROWS = 512
ROW_UP, ROW_DN, SENT_ROWS = 64, 128, 160
PLACES = []
for _piece, _off in ((0, 0), (1, -1), (2, 1)):
    for _i, _near in enumerate((0, -1, 1, 2)):
        PLACES.append((_piece, _i, _near, _off))
EARLY = list(PLACES)
LATE = [(0, 0, 0, 2), (0, 1, -1, 2), (1, 0, 1, 2), (1, 1, 2, 2)]
PLACES += [(3 + piece, shard, first, second) for piece, shard, first, second in LATE]


def torus(dx, dz):
    return [
        (i, ((i // SIDE + dx) % SIDE) * SIDE + (i % SIDE + dz) % SIDE) for i in range(SIDE * SIDE)
    ]


def send(value, along, step):
    return lax.ppermute(value, "req", torus(step, 0) if along == 0 else torus(0, step))


def first_step(value, along):
    return send(value, along, 1), send(value, along, -1)


def second_step(before, after, along):
    half = before.shape[0] // 2
    return send(before[:half], along, 1), send(after[half:], along, -1)


def source(group, half, first, second):
    x, z = group // SIDE, group % SIDE
    dx, dz = (first, second) if half == 0 else (second, first)
    return ((x + dx + SIDE) % SIDE) * SIDE + (z + dz + SIDE) % SIDE


def cost(us):
    return pl.CostEstimate(flops=int(us * 1.15e9), bytes_accessed=2**20, transcendentals=0)


ANY = pl.BlockSpec(memory_space=pl.ANY)
WHOLE = pl.BlockSpec(memory_space=pltpu.VMEM)
SCALARS = pl.BlockSpec(memory_space=pltpu.SMEM)


def pack_kernel(index_ref, store_ref, up_ref, down_ref, out_ref):
    def one(i, carry):
        out_ref[i, 0:ROW_UP, :] = store_ref[index_ref[i]]
        out_ref[i, ROW_UP:ROW_DN, :] = up_ref[...]
        for side in range(2):
            out_ref[i, ROW_DN:SENT_ROWS, side * 256 : side * 256 + 256] = down_ref[
                side * 32 : side * 32 + 32, :
            ]
        return carry

    lax.fori_loop(0, out_ref.shape[0], one, 0)


def pack(index, store, up, down):
    return pl.pallas_call(
        pack_kernel,
        out_shape=jax.ShapeDtypeStruct((16, SENT_ROWS, 512), BF),
        in_specs=[SCALARS] + [WHOLE] * 3,
        out_specs=WHOLE,
        cost_estimate=cost(3),
        name="pack",
    )(index, store, up, down)


def pick_down_kernel(info_ref, recv_ref, out_ref, sem):
    for j in range(4):
        slot = info_ref[1 + j]
        owner, inner = slot // 4, slot % 4
        start = pl.multiple_of(ROW_DN + (inner % 2) * 16, 16)
        for side in range(2):

            @pl.when(inner // 2 == side)
            def _(side=side, j=j, owner=owner, start=start):
                pltpu.make_async_copy(
                    recv_ref.at[owner, pl.ds(start, 16), pl.ds(side * 256, 256)],
                    out_ref.at[j],
                    sem.at[j],
                ).start()

    for j in range(4):
        pltpu.make_async_copy(out_ref.at[j], out_ref.at[j], sem.at[j]).wait()


def pick_down(info, recv):
    return pl.pallas_call(
        pick_down_kernel,
        out_shape=jax.ShapeDtypeStruct((4, 16, 256), BF),
        in_specs=[SCALARS, ANY],
        out_specs=WHOLE,
        scratch_shapes=[pltpu.SemaphoreType.DMA((4,))],
        cost_estimate=cost(2),
        name="pick_down",
    )(info, recv)


def products(group, x_ref, routes_ref, pieces, shards, half):
    count = len(pieces) // 2
    x = jnp.concatenate(
        [
            x_ref[:, pl.ds(pl.multiple_of(source(group, half, first, second) * 128, 128), 128)]
            for _, _, first, second in shards
        ],
        axis=1,
    )

    def product(row):
        weight = jnp.concatenate(
            [
                pieces[half * count + piece][pl.ds(shard * SHARD_ROWS + row, 128), :]
                for piece, shard, _, _ in shards
            ],
            axis=0,
        )
        return jnp.dot(x, weight, preferred_element_type=F32)

    chosen = [jnp.zeros((256, 256), F32)] * TOPK
    for i in range(4):
        value = product(i * 128)
        for k in range(TOPK):
            chosen[k] = jnp.where(routes_ref[:, k : k + 1] == half * 4 + i, value, chosen[k])
    return chosen, product(ROW_KV)


def early_kernel(info_ref, gates_ref, routes_ref, x_ref, *refs):
    pieces = refs[:6]
    wide_ref, sums_ref = refs[6:]
    group = info_ref[0]
    for e in range(NE):
        wide_ref[e] = jnp.broadcast_to(gates_ref[:, e : e + 1], (1024, 128))

    def block(j, carry):
        rows = pl.ds(pl.multiple_of(j * 256, 256), 256)
        x, routes = x_ref.at[rows, :], routes_ref.at[rows, :]
        first, base = products(group, x, routes, pieces, EARLY, 0)
        sums_ref[j, 2] = base
        second, base = products(group, x, routes, pieces, EARLY, 1)
        sums_ref[j, 3] = base
        for k in range(TOPK):
            sums_ref[j, k] = first[k] + second[k]
        return carry

    lax.fori_loop(0, 4, block, 0)


def project_early(info, gates, routes, x, pieces):
    return pl.pallas_call(
        early_kernel,
        out_shape=(
            jax.ShapeDtypeStruct((NE, 1024, 128), F32),
            jax.ShapeDtypeStruct((4, 4, 256, 256), F32),
        ),
        in_specs=[SCALARS] + [WHOLE] * 9,
        out_specs=(WHOLE, WHOLE),
        compiler_params=pltpu.CompilerParams(vmem_limit_bytes=10 * 2**20),
        cost_estimate=cost(15),
        name="project_early",
    )(info, gates, routes, x, *pieces)


def attend_kernel(info_ref, routes_ref, down_ref, x_ref, sums_ref, recv_hbm, *refs):
    pieces = refs[:4]
    out_ref, sums, up, cache, sem = refs[4:]
    group = info_ref[0]
    for j in range(4):
        slot = info_ref[1 + j]
        start = pl.multiple_of(ROW_UP + (slot % 4) * 16, 16)
        pltpu.make_async_copy(
            recv_hbm.at[slot // 4, pl.ds(start, 16), :], up.at[j], sem.at[0, j]
        ).start()
        pltpu.make_async_copy(
            recv_hbm.at[info_ref[5 + j], pl.ds(0, 64), :], cache.at[j], sem.at[1, j]
        ).start()

    def attend(j, carry):
        for i, ref in enumerate((up, cache)):
            pltpu.make_async_copy(ref.at[j], ref.at[j], sem.at[i, j]).wait()
        rows = pl.ds(pl.multiple_of(j * 256, 256), 256)
        x, routes = x_ref.at[rows, :], routes_ref.at[rows, :]
        for half in range(2):
            chosen, base = products(group, x, routes, pieces, LATE, half)
            sums[2 + half] = sums_ref[j, 2 + half] + base
            for k in range(TOPK):
                before = sums_ref[j, k] if half == 0 else sums[k]
                sums[k] = before + chosen[k]
        down = jnp.concatenate([down_ref[e, j] for e in range(NE)], axis=1)
        low = lax.dot_general(
            x[...], down, (((1,), (1,)), ((), ())), preferred_element_type=F32
        ).astype(BF)
        cached_length = info_ref[9 + j]
        place = lax.broadcasted_iota(jnp.int32, (256, 320), 1)
        query_at = lax.broadcasted_iota(jnp.int32, (256, 320), 0)
        allowed = (place < cached_length) | ((place >= 64) & (place - 64 <= query_at))
        for h in range(2):
            cols = slice(h * HD, (h + 1) * HD)
            extra = jnp.dot(low, up[j, :, h * 256 : h * 256 + 256], preferred_element_type=F32)
            fresh = (sums[2 + h] + adapter_scale * extra).astype(BF)
            keys = jnp.concatenate(
                [cache[j, :, h * 256 : h * 256 + HD], fresh[:, 0:HD]], axis=0
            )
            values = jnp.concatenate(
                [cache[j, :, h * 256 + HD : h * 256 + 2 * HD], fresh[:, HD : 2 * HD]], axis=0
            )
            attended = []
            for k in range(TOPK):
                scores = lax.dot_general(
                    sums[k, :, cols].astype(BF),
                    keys,
                    (((1,), (1,)), ((), ())),
                    preferred_element_type=F32,
                ) * (HD**-0.5)
                scores = jnp.where(allowed, scores, NEG)
                weights = jnp.exp(scores - jnp.max(scores, axis=-1, keepdims=True))
                total = jnp.sum(weights, axis=-1, keepdims=True)
                probability = (weights * (1.0 / total)).astype(BF)
                attended.append(jnp.dot(probability, values, preferred_element_type=F32))
            for e in range(NE):
                chosen = jnp.where(
                    routes[:, 0:1] == e,
                    attended[0],
                    jnp.where(routes[:, 1:2] == e, attended[1], 0.0),
                )
                out_ref[e, rows, cols] = chosen.astype(BF)
        return carry

    lax.fori_loop(0, 4, attend, 0)


def attention(info, routes, down, x, sums, recv, pieces):
    return pl.pallas_call(
        attend_kernel,
        out_shape=jax.ShapeDtypeStruct((NE, 1024, 256), BF),
        in_specs=[SCALARS] + [WHOLE] * 4 + [ANY] + [WHOLE] * 4,
        out_specs=WHOLE,
        scratch_shapes=[
            pltpu.VMEM((4, 256, 256), F32),
            pltpu.VMEM((4, 16, 512), BF),
            pltpu.VMEM((4, 64, 512), BF),
            pltpu.SemaphoreType.DMA((2, 4)),
        ],
        compiler_params=pltpu.CompilerParams(vmem_limit_bytes=10 * 2**20),
        cost_estimate=cost(22),
        name="attention",
    )(info, routes, down, x, sums, recv, *pieces)


def project_out_kernel(blocks, place_ref, wide_ref, lhs_ref, *refs):
    pieces = refs[:10]
    out_ref, w, sem = refs[10:]
    group, y, core = place_ref[0], place_ref[1], place_ref[2]
    for b, (mine, ahead) in enumerate(blocks):
        wanted_x = (y + ahead) % 4
        side = core if mine else 1 - core
        for half in range(2):
            for piece, shard, first, second in PLACES:
                owner = source(group, half, first, second)

                @pl.when((owner // 4 == wanted_x) & ((owner % 4) // 2 == side))
                def _(b=b, half=half, piece=piece, shard=shard, owner=owner):
                    pltpu.make_async_copy(
                        pieces[half * 5 + piece].at[pl.ds(shard * OUT_ROWS, OUT_ROWS), :],
                        w.at[b, half, owner % 2],
                        sem.at[b],
                    ).start()

    def block(b, carry):
        pltpu.make_async_copy(w.at[b], w.at[b], sem.at[b]).wait()

        def tile(i, inner):
            rows = pl.ds(pl.multiple_of(i * 256, 256), 256)
            total = None
            for e in range(NE):
                half, pair, lane = e // 4, (e % 4) // 2, e % 2
                place = (pl.ds(pair * 256, 256), pl.ds(lane * 128, 128))
                weight = jnp.concatenate(
                    [w[b, half, 0, place[0], place[1]], w[b, half, 1, place[0], place[1]]], axis=1
                )
                value = jnp.dot(lhs_ref[e, rows, :], weight, preferred_element_type=F32)
                gate = wide_ref[e, rows, :]
                value = value * jnp.concatenate([gate, gate], axis=1)
                total = value if total is None else total + value
            out_ref[b, rows, :] = total.astype(BF)
            return inner

        return lax.fori_loop(0, 4, tile, carry)

    lax.fori_loop(0, len(blocks), block, 0)


def project_out(blocks, place, wide, lhs, pieces):
    return pl.pallas_call(
        functools.partial(project_out_kernel, blocks),
        out_shape=jax.ShapeDtypeStruct((len(blocks), 1024, 256), BF),
        in_specs=[SCALARS, WHOLE, WHOLE] + [ANY] * 10,
        out_specs=WHOLE,
        scratch_shapes=[
            pltpu.VMEM((len(blocks), 2, 2, OUT_ROWS, 256), BF),
            pltpu.SemaphoreType.DMA((len(blocks),)),
        ],
        compiler_params=pltpu.CompilerParams(vmem_limit_bytes=8 * 2**20),
        cost_estimate=cost(2.5 * len(blocks)),
        name="project_out_" + str(len(blocks)),
    )(place, wide, lhs, *pieces)


def exchange(value, step):
    if step == 0:
        return lax.ppermute(value, "exp", [(i, i ^ 1) for i in range(8)])
    return lax.ppermute(value, "exp", [(i, (i + 2 * step) % 8) for i in range(8)])


def rounded_sum(*values):
    total = values[0].astype(F32)
    for value in values[1:]:
        total = total + value.astype(F32)
    return total.astype(BF)


def body(
    tokens,
    routes,
    lengths,
    cached_prefix_length,
    prefix_cache_row,
    adapter_per_request,
    adapter_storage_slot,
    router_weight,
    key_value_weight,
    expert_query_weight,
    expert_output_weight,
    adapter_down_maps,
    adapter_up_maps,
    prefix_cache_store,
):
    group = lax.axis_index("req")
    part = lax.axis_index("exp")
    rows_by_group = prefix_cache_row.reshape(16, 4)
    held = (rows_by_group == group).astype(jnp.int32)
    wanted_by = jnp.sum(held * jnp.arange(4, dtype=jnp.int32)[None, :], axis=1)
    down_rows = (
        lax.dynamic_slice_in_dim(adapter_down_maps, part * 256, 256, 1)
        .transpose(0, 2, 1)
        .reshape(64, 256)
    )
    outgoing = pack(wanted_by, prefix_cache_store, adapter_up_maps.reshape(64, 512), down_rows)

    query_rows = expert_query_weight.transpose(1, 0, 2).reshape(NE * 128, 256)
    out_rows = (
        expert_output_weight.reshape(4, 2, 256, 128).transpose(0, 2, 1, 3).reshape(1024, 256)
    )
    own = [
        jnp.concatenate(
            [
                query_rows[half * 512 : half * 512 + 512],
                key_value_weight[:, half * 256 : half * 256 + 256],
                out_rows[half * 512 : half * 512 + 512],
            ],
            axis=0,
        )
        for half in range(2)
    ]
    neighbours = [*first_step(own[0], 0), *first_step(own[1], 1)]
    *neighbours, outgoing = lax.optimization_barrier((*neighbours, outgoing))
    received = lax.all_to_all(outgoing, "req", 0, 0, tiled=True)
    near, near_out = [], []
    for half in range(2):
        before, after = neighbours[2 * half : 2 * half + 2]
        far_low, far_high = second_step(before, after, half)
        cut = SHARD_ROWS - far_low.shape[0]
        near.append(
            jnp.concatenate(
                [
                    own[half][:SHARD_ROWS],
                    before[:SHARD_ROWS],
                    after[:SHARD_ROWS],
                    far_low,
                    far_high[:cut],
                ],
                axis=0,
            )
        )
        near_out.append(
            jnp.concatenate(
                [
                    own[half][SHARD_ROWS:],
                    before[SHARD_ROWS:],
                    after[SHARD_ROWS:],
                    far_high[cut:],
                ],
                axis=0,
            )
        )

    adapter_hot = (
        adapter_per_request[:, None]
        == jnp.arange(adapter_storage_slot.shape[0], dtype=jnp.int32)[None, :]
    ).astype(jnp.int32)
    slots = jnp.sum(adapter_hot * adapter_storage_slot[None, :], axis=1)
    own_rows = lax.dynamic_slice_in_dim(prefix_cache_row, group * 4, 4, 0)
    info = jnp.concatenate([group[None].astype(jnp.int32), slots, own_rows, cached_prefix_length])

    logits = jnp.dot(tokens, router_weight, preferred_element_type=F32)
    expert = jnp.arange(NE, dtype=jnp.int32)
    route_hot = (routes[:, :, None] == expert[None, None, :]).astype(F32)
    chosen = jnp.sum(route_hot * logits[:, None, :], axis=-1)
    gate_values = jax.nn.sigmoid(chosen - chosen[:, ::-1])
    live = (jnp.arange(256, dtype=jnp.int32)[None, :] < lengths[:, None]).reshape(1024, 1)
    gates = jnp.sum(route_hot * gate_values[:, :, None], axis=1) * live.astype(F32)
    wide = jnp.broadcast_to(gates.T[:, :, None], (NE, 1024, 128))

    beside = [*first_step(near[0], 1), *first_step(near[1], 0)]
    down_part = pick_down(info, received)
    down = lax.all_to_all(
        jnp.broadcast_to(down_part[None], (NE, 4, 16, 256)), "exp", 0, 0, tiled=True
    )
    *beside, down = lax.optimization_barrier((*beside, down))
    late = [*second_step(*beside[:2], 1), *second_step(*beside[2:], 0)]
    wide, sums = project_early(
        info, gates, routes, tokens, [near[0], *beside[:2], near[1], *beside[2:]]
    )
    *late, near_out[0], near_out[1] = lax.optimization_barrier((*late, *near_out))
    out_beside = [*first_step(near_out[0], 1), *first_step(near_out[1], 0)]
    lhs = attention(info, routes, down, tokens, sums, received, late)
    *out_beside, lhs = lax.optimization_barrier((*out_beside, lhs))
    out_late = [*second_step(*out_beside[:2], 1), *second_step(*out_beside[2:], 0)]
    out_pieces = []
    for half in range(2):
        two = slice(half * 2, half * 2 + 2)
        out_pieces += [near_out[half], *out_beside[two], *out_late[two]]

    place = jnp.stack([group, part // 2, part % 2]).astype(jnp.int32)
    far = project_out(((False, 2), (True, 2)), place, wide, lhs, out_pieces)
    far_swapped = exchange(far[0], 0)
    place = lax.optimization_barrier((place, far))[0]
    theirs = project_out(((False, 1), (False, 3), (False, 0)), place, wide, lhs, out_pieces)
    swapped = exchange(theirs, 0)
    both_far = rounded_sum(far[1], far_swapped)
    low = exchange(both_far[:512], 1)
    high = exchange(both_far[512:], -1)
    place = lax.optimization_barrier((place, theirs, both_far))[0]
    mine = project_out(((True, 1), (True, 3)), place, wide, lhs, out_pieces)
    ahead = jnp.concatenate(
        [rounded_sum(mine[0, :512], swapped[0, :512], low), rounded_sum(mine[0, 512:], swapped[0, 512:])],
        axis=0,
    )
    behind = jnp.concatenate(
        [rounded_sum(mine[1, :512], swapped[1, :512]), rounded_sum(mine[1, 512:], swapped[1, 512:], high)],
        axis=0,
    )
    from_behind, from_ahead = exchange(ahead, 1), exchange(behind, -1)
    place = lax.optimization_barrier((place, ahead, behind))[0]
    own_block = project_out(((True, 0),), place, wide, lhs, out_pieces)
    return rounded_sum(own_block[0], swapped[2], from_behind, from_ahead)


def solution(mesh):
    return jax.shard_map(
        body,
        mesh=mesh,
        in_specs=(
            P("req", None),
            P("req", None),
            P("req"),
            P("req"),
            P(),
            P("req"),
            P(),
            P(),
            P("req", "exp"),
            P("req", None, "exp"),
            P(None, "exp", "req"),
            P("req", None, None),
            P("req", None, "exp"),
            P("req", None, "exp"),
        ),
        out_specs=P("req", "exp"),
        check_vma=False,
    )
```

```python
import functools

import jax
import jax.numpy as jnp
from jax import lax
from jax.experimental import pallas as pl
from jax.experimental.pallas import tpu as pltpu
from jax.sharding import PartitionSpec as P

HD = 128
NE = 8
TOPK = 2
SIDE = 4
BF = jnp.bfloat16
F32 = jnp.float32
NEG = -1e30
adapter_scale = 0.5

ROW_KV, ROW_UP = 512, 640
SHARD_ROWS = 704
OUT_ROWS = 512
ROW_DN, SENT_ROWS = 64, 96
PLACES = []
for _piece, _off in ((0, 0), (1, -1), (2, 1)):
    for _i, _near in enumerate((0, -1, 1, 2)):
        PLACES.append((_piece, _i, _near, _off))
EARLY = list(PLACES)
LATE = [(0, 0, 0, 2), (0, 1, -1, 2), (1, 0, 1, 2), (1, 1, 2, 2)]
PLACES += [(3 + piece, shard, first, second) for piece, shard, first, second in LATE]


def torus(dx, dz):
    return [
        (i, ((i // SIDE + dx) % SIDE) * SIDE + (i % SIDE + dz) % SIDE) for i in range(SIDE * SIDE)
    ]


def send(value, along, step):
    return lax.ppermute(value, "req", torus(step, 0) if along == 0 else torus(0, step))


def first_step(value, along):
    return send(value, along, 1), send(value, along, -1)


def source(group, half, first, second):
    x, z = group // SIDE, group % SIDE
    dx, dz = (first, second) if half == 0 else (second, first)
    return ((x + dx + SIDE) % SIDE) * SIDE + (z + dz + SIDE) % SIDE


def cost(us):
    return pl.CostEstimate(flops=int(us * 1.15e9), bytes_accessed=2**20, transcendentals=0)


ANY = pl.BlockSpec(memory_space=pl.ANY)
WHOLE = pl.BlockSpec(memory_space=pltpu.VMEM)
SCALARS = pl.BlockSpec(memory_space=pltpu.SMEM)


def pack_kernel(index_ref, store_ref, down_ref, out_ref):
    def one(i, carry):
        out_ref[i, 0:ROW_DN, :] = store_ref[index_ref[i]]
        for side in range(2):
            out_ref[i, ROW_DN:SENT_ROWS, side * 256 : side * 256 + 256] = down_ref[
                side * 32 : side * 32 + 32, :
            ]
        return carry

    lax.fori_loop(0, out_ref.shape[0], one, 0)


def pack(index, store, down):
    return pl.pallas_call(
        pack_kernel,
        out_shape=jax.ShapeDtypeStruct((16, SENT_ROWS, 512), BF),
        in_specs=[SCALARS] + [WHOLE] * 2,
        out_specs=WHOLE,
        cost_estimate=cost(3),
        name="pack",
    )(index, store, down)


def pick_down_kernel(info_ref, recv_ref, out_ref, sem):
    for j in range(4):
        slot = info_ref[1 + j]
        owner, inner = slot // 4, slot % 4
        start = pl.multiple_of(ROW_DN + (inner % 2) * 16, 16)
        for side in range(2):

            @pl.when(inner // 2 == side)
            def _(side=side, j=j, owner=owner, start=start):
                pltpu.make_async_copy(
                    recv_ref.at[owner, pl.ds(start, 16), pl.ds(side * 256, 256)],
                    out_ref.at[j],
                    sem.at[j],
                ).start()

    for j in range(4):
        pltpu.make_async_copy(out_ref.at[j], out_ref.at[j], sem.at[j]).wait()


def pick_down(info, recv):
    return pl.pallas_call(
        pick_down_kernel,
        out_shape=jax.ShapeDtypeStruct((4, 16, 256), BF),
        in_specs=[SCALARS, ANY],
        out_specs=WHOLE,
        scratch_shapes=[pltpu.SemaphoreType.DMA((4,))],
        cost_estimate=cost(2),
        name="pick_down",
    )(info, recv)


def products(group, x_ref, routes_ref, pieces, shards, half):
    count = len(pieces) // 2
    x = jnp.concatenate(
        [
            x_ref[:, pl.ds(pl.multiple_of(source(group, half, first, second) * 128, 128), 128)]
            for _, _, first, second in shards
        ],
        axis=1,
    )

    def product(row):
        weight = jnp.concatenate(
            [
                pieces[half * count + piece][pl.ds(shard * SHARD_ROWS + row, 128), :]
                for piece, shard, _, _ in shards
            ],
            axis=0,
        )
        return jnp.dot(x, weight, preferred_element_type=F32)

    chosen = [jnp.zeros((256, 256), F32)] * TOPK
    for i in range(4):
        value = product(i * 128)
        for k in range(TOPK):
            chosen[k] = jnp.where(routes_ref[:, k : k + 1] == half * 4 + i, value, chosen[k])
    return chosen, product(ROW_KV)


def pick_up(info_ref, pieces, shards, up_ref):
    count = len(pieces) // 2
    for half in range(2):
        for piece, shard, first, second in shards:
            owner = source(info_ref[0], half, first, second)
            for j in range(4):
                slot = info_ref[1 + j]

                @pl.when(slot // 4 == owner)
                def _(half=half, piece=piece, shard=shard, j=j, slot=slot):
                    start = pl.multiple_of(shard * SHARD_ROWS + ROW_UP + slot % 4 * 16, 16)
                    up_ref[j, half] = pieces[half * count + piece][pl.ds(start, 16), :]


def early_kernel(info_ref, routes_ref, x_ref, *refs):
    pieces = refs[:6]
    up_ref, sums_ref = refs[6:]
    group = info_ref[0]
    up_ref[...] = jnp.zeros_like(up_ref)
    pick_up(info_ref, pieces, EARLY, up_ref)

    def block(j, carry):
        rows = pl.ds(pl.multiple_of(j * 256, 256), 256)
        x, routes = x_ref.at[rows, :], routes_ref.at[rows, :]
        first, base = products(group, x, routes, pieces, EARLY, 0)
        sums_ref[j, 2] = base
        second, base = products(group, x, routes, pieces, EARLY, 1)
        sums_ref[j, 3] = base
        for k in range(TOPK):
            sums_ref[j, k] = first[k] + second[k]
        return carry

    lax.fori_loop(0, 4, block, 0)


def project_early(info, routes, x, pieces):
    return pl.pallas_call(
        early_kernel,
        out_shape=(
            jax.ShapeDtypeStruct((4, 2, 16, 256), BF),
            jax.ShapeDtypeStruct((4, 4, 256, 256), F32),
        ),
        in_specs=[SCALARS] + [WHOLE] * 8,
        out_specs=(WHOLE, WHOLE),
        compiler_params=pltpu.CompilerParams(vmem_limit_bytes=20 * 2**20),
        cost_estimate=cost(15),
        name="project_early",
    )(info, routes, x, *pieces)


def attend_kernel(info_ref, routes_ref, down_ref, x_ref, up_ref, sums_ref, recv_hbm, *refs):
    pieces = refs[:4]
    out_ref, sums, up, cache, sem = refs[4:]
    group = info_ref[0]
    for j in range(4):
        pltpu.make_async_copy(
            recv_hbm.at[info_ref[5 + j], pl.ds(0, 64), :], cache.at[j], sem.at[j]
        ).start()
    up[...] = up_ref[...]
    pick_up(info_ref, pieces, LATE, up)

    def attend(j, carry):
        pltpu.make_async_copy(cache.at[j], cache.at[j], sem.at[j]).wait()
        rows = pl.ds(pl.multiple_of(j * 256, 256), 256)
        x, routes = x_ref.at[rows, :], routes_ref.at[rows, :]
        for half in range(2):
            chosen, base = products(group, x, routes, pieces, LATE, half)
            sums[2 + half] = sums_ref[j, 2 + half] + base
            for k in range(TOPK):
                before = sums_ref[j, k] if half == 0 else sums[k]
                sums[k] = before + chosen[k]
        down = jnp.concatenate([down_ref[e, j] for e in range(NE)], axis=1)
        low = lax.dot_general(
            x[...], down, (((1,), (1,)), ((), ())), preferred_element_type=F32
        ).astype(BF)
        cached_length = info_ref[9 + j]
        place = lax.broadcasted_iota(jnp.int32, (256, 320), 1)
        query_at = lax.broadcasted_iota(jnp.int32, (256, 320), 0)
        allowed = (place < cached_length) | ((place >= 64) & (place - 64 <= query_at))
        for h in range(2):
            cols = slice(h * HD, (h + 1) * HD)
            extra = jnp.dot(low, up[j, h], preferred_element_type=F32)
            fresh = (sums[2 + h] + adapter_scale * extra).astype(BF)
            keys = jnp.concatenate(
                [cache[j, :, h * 256 : h * 256 + HD], fresh[:, 0:HD]], axis=0
            )
            values = jnp.concatenate(
                [cache[j, :, h * 256 + HD : h * 256 + 2 * HD], fresh[:, HD : 2 * HD]], axis=0
            )
            attended = []
            for k in range(TOPK):
                scores = lax.dot_general(
                    sums[k, :, cols].astype(BF),
                    keys,
                    (((1,), (1,)), ((), ())),
                    preferred_element_type=F32,
                ) * (HD**-0.5)
                scores = jnp.where(allowed, scores, NEG)
                weights = jnp.exp(scores - jnp.max(scores, axis=-1, keepdims=True))
                total = jnp.sum(weights, axis=-1, keepdims=True)
                probability = (weights * (1.0 / total)).astype(BF)
                attended.append(jnp.dot(probability, values, preferred_element_type=F32))
            for e in range(NE):
                chosen = jnp.where(
                    routes[:, 0:1] == e,
                    attended[0],
                    jnp.where(routes[:, 1:2] == e, attended[1], 0.0),
                )
                out_ref[e, rows, cols] = chosen.astype(BF)
        return carry

    lax.fori_loop(0, 4, attend, 0)


def attention(info, routes, down, x, up, sums, recv, pieces):
    return pl.pallas_call(
        attend_kernel,
        out_shape=jax.ShapeDtypeStruct((NE, 1024, 256), BF),
        in_specs=[SCALARS] + [WHOLE] * 5 + [ANY] + [WHOLE] * 4,
        out_specs=WHOLE,
        scratch_shapes=[
            pltpu.VMEM((4, 256, 256), F32),
            pltpu.VMEM((4, 2, 16, 256), BF),
            pltpu.VMEM((4, 64, 512), BF),
            pltpu.SemaphoreType.DMA((4,)),
        ],
        compiler_params=pltpu.CompilerParams(vmem_limit_bytes=20 * 2**20),
        cost_estimate=cost(22),
        name="attention",
    )(info, routes, down, x, up, sums, recv, *pieces)


def project_out_kernel(blocks, place_ref, gates_ref, lhs_ref, *refs):
    pieces = refs[:10]
    *outs, w, sem = refs[10:]
    group, y, core = place_ref[0], place_ref[1], place_ref[2]
    for b, (mine, ahead) in enumerate(blocks):
        wanted_x = (y + ahead) % 4
        side = core if mine else 1 - core
        for half in range(2):
            for piece, shard, first, second in PLACES:
                owner = source(group, half, first, second)

                @pl.when((owner // 4 == wanted_x) & ((owner % 4) // 2 == side))
                def _(b=b, half=half, piece=piece, shard=shard, owner=owner):
                    pltpu.make_async_copy(
                        pieces[half * 5 + piece].at[pl.ds(shard * OUT_ROWS, OUT_ROWS), :],
                        w.at[b, half, owner % 2],
                        sem.at[b],
                    ).start()

    def block(b, out_ref):
        pltpu.make_async_copy(w.at[b], w.at[b], sem.at[b]).wait()

        def tile(i, carry):
            rows = pl.ds(pl.multiple_of(i * 256, 256), 256)
            total = None
            for e in range(NE):
                half, pair, lane = e // 4, (e % 4) // 2, e % 2
                place = (pl.ds(pair * 256, 256), pl.ds(lane * 128, 128))
                weight = jnp.concatenate(
                    [w[b, half, 0, place[0], place[1]], w[b, half, 1, place[0], place[1]]], axis=1
                )
                value = jnp.dot(lhs_ref[e, rows, :], weight, preferred_element_type=F32)
                value = value * gates_ref[rows, e : e + 1]
                total = value if total is None else total + value
            out_ref[rows, :] = total.astype(BF)
            return carry

        lax.fori_loop(0, 4, tile, 0)

    if len(outs) > 1:
        for b, out_ref in enumerate(outs):
            block(b, out_ref)
    else:

        def step(b, carry):
            block(b, outs[0].at[b])
            return carry

        lax.fori_loop(0, len(blocks), step, 0)


def project_out(blocks, place, gates, lhs, pieces, apart=False):
    if apart:
        shapes = [jax.ShapeDtypeStruct((1024, 256), BF)] * len(blocks)
    else:
        shapes = [jax.ShapeDtypeStruct((len(blocks), 1024, 256), BF)]
    return pl.pallas_call(
        functools.partial(project_out_kernel, blocks),
        out_shape=shapes,
        in_specs=[SCALARS, WHOLE, WHOLE] + [ANY] * 10,
        out_specs=[WHOLE] * len(shapes),
        scratch_shapes=[
            pltpu.VMEM((len(blocks), 2, 2, OUT_ROWS, 256), BF),
            pltpu.SemaphoreType.DMA((len(blocks),)),
        ],
        compiler_params=pltpu.CompilerParams(vmem_limit_bytes=8 * 2**20),
        cost_estimate=cost(2.2 * len(blocks)),
        name="project_out_" + str(len(blocks)),
    )(place, gates, lhs, *pieces)


def small_call(kernel, shapes, us, *operands):
    return pl.pallas_call(
        kernel,
        out_shape=[jax.ShapeDtypeStruct(shape, BF) for shape in shapes],
        in_specs=[WHOLE] * len(operands),
        out_specs=[WHOLE] * len(shapes),
        compiler_params=pltpu.CompilerParams(vmem_limit_bytes=8 * 2**20),
        cost_estimate=cost(us),
        name=kernel.__name__,
    )(*operands)


def forward_kernel(*refs):
    for i in range(4):
        source_ref, out_ref = refs[i], refs[4 + i]
        half = out_ref.shape[0]
        out_ref[...] = source_ref[pl.ds(i % 2 * half, half), :]


def forwarded(values):
    half = values[0].shape[0] // 2
    return small_call(forward_kernel, [(half, 256)] * 4, 2, *values)


def onward(values, along):
    low0, high0, low1, high1 = forwarded(values)
    return [
        send(low0, along, 1),
        send(high0, along, -1),
        send(low1, 1 - along, 1),
        send(high1, 1 - along, -1),
    ]


def far_sum_kernel(mine_ref, theirs_ref, low_ref, high_ref):
    for i, out_ref in enumerate((low_ref, high_ref)):
        rows = pl.ds(i * 512, 512)
        out_ref[...] = (mine_ref[rows, :].astype(F32) + theirs_ref[rows, :].astype(F32)).astype(BF)


def near_sum_kernel(mine_ref, theirs_ref, low_ref, high_ref, ahead_ref, behind_ref):
    for i, out_ref in enumerate((ahead_ref, behind_ref)):
        extra_ref = (low_ref, high_ref)[i]
        for half in range(2):
            rows = pl.ds(half * 512, 512)
            total = mine_ref[i, rows, :].astype(F32) + theirs_ref[i, rows, :].astype(F32)
            if half == i:
                total = total + extra_ref[...].astype(F32)
            out_ref[rows, :] = total.astype(BF)


def exchange(value, step):
    if step == 0:
        return lax.ppermute(value, "exp", [(i, i ^ 1) for i in range(8)])
    return lax.ppermute(value, "exp", [(i, (i + 2 * step) % 8) for i in range(8)])


def rounded_sum(*values):
    total = values[0].astype(F32)
    for value in values[1:]:
        total = total + value.astype(F32)
    return total.astype(BF)


def body(
    tokens,
    routes,
    lengths,
    cached_prefix_length,
    prefix_cache_row,
    adapter_per_request,
    adapter_storage_slot,
    router_weight,
    key_value_weight,
    expert_query_weight,
    expert_output_weight,
    adapter_down_maps,
    adapter_up_maps,
    prefix_cache_store,
):
    group = lax.axis_index("req")
    part = lax.axis_index("exp")
    rows_by_group = prefix_cache_row.reshape(16, 4)
    held = (rows_by_group == group).astype(jnp.int32)
    wanted_by = jnp.sum(held * jnp.arange(4, dtype=jnp.int32)[None, :], axis=1)
    down_rows = (
        lax.dynamic_slice_in_dim(adapter_down_maps, part * 256, 256, 1)
        .transpose(0, 2, 1)
        .reshape(64, 256)
    )
    outgoing = pack(wanted_by, prefix_cache_store, down_rows)
    up_rows = adapter_up_maps.reshape(64, 512)

    query_rows = expert_query_weight.transpose(1, 0, 2).reshape(NE * 128, 256)
    out_rows = (
        expert_output_weight.reshape(4, 2, 256, 128).transpose(0, 2, 1, 3).reshape(1024, 256)
    )
    own = [
        jnp.concatenate(
            [
                query_rows[half * 512 : half * 512 + 512],
                key_value_weight[:, half * 256 : half * 256 + 256],
                up_rows[:, half * 256 : half * 256 + 256],
                out_rows[half * 512 : half * 512 + 512],
            ],
            axis=0,
        )
        for half in range(2)
    ]
    neighbours = [*first_step(own[0], 0), *first_step(own[1], 1)]
    *neighbours, outgoing = lax.optimization_barrier((*neighbours, outgoing))
    received = lax.all_to_all(outgoing, "req", 0, 0, tiled=True)
    passed = onward(neighbours, 0)
    near, near_out = [], []
    for half in range(2):
        before, after = neighbours[2 * half : 2 * half + 2]
        far_low, far_high = passed[2 * half : 2 * half + 2]
        cut = SHARD_ROWS - far_low.shape[0]
        near.append(
            jnp.concatenate(
                [
                    own[half][:SHARD_ROWS],
                    before[:SHARD_ROWS],
                    after[:SHARD_ROWS],
                    far_low,
                    far_high[:cut],
                ],
                axis=0,
            )
        )
        near_out.append(
            jnp.concatenate(
                [
                    own[half][SHARD_ROWS:],
                    before[SHARD_ROWS:],
                    after[SHARD_ROWS:],
                    far_high[cut:],
                ],
                axis=0,
            )
        )

    adapter_hot = (
        adapter_per_request[:, None]
        == jnp.arange(adapter_storage_slot.shape[0], dtype=jnp.int32)[None, :]
    ).astype(jnp.int32)
    slots = jnp.sum(adapter_hot * adapter_storage_slot[None, :], axis=1)
    own_rows = lax.dynamic_slice_in_dim(prefix_cache_row, group * 4, 4, 0)
    info = jnp.concatenate([group[None].astype(jnp.int32), slots, own_rows, cached_prefix_length])

    logits = jnp.dot(tokens, router_weight, preferred_element_type=F32)
    expert = jnp.arange(NE, dtype=jnp.int32)
    route_hot = (routes[:, :, None] == expert[None, None, :]).astype(F32)
    chosen = jnp.sum(route_hot * logits[:, None, :], axis=-1)
    gate_values = jax.nn.sigmoid(chosen - chosen[:, ::-1])
    live = (jnp.arange(256, dtype=jnp.int32)[None, :] < lengths[:, None]).reshape(1024, 1)
    gates = jnp.sum(route_hot * gate_values[:, :, None], axis=1) * live.astype(F32)

    beside = [*first_step(near[0], 1), *first_step(near[1], 0)]
    down_part = pick_down(info, received)
    down = lax.all_to_all(
        jnp.broadcast_to(down_part[None], (NE, 4, 16, 256)), "exp", 0, 0, tiled=True
    )
    *beside, down, gates = lax.optimization_barrier((*beside, down, gates))
    late = onward(beside, 1)
    up, sums = project_early(info, routes, tokens, [near[0], *beside[:2], near[1], *beside[2:]])
    *late, near_out[0], near_out[1] = lax.optimization_barrier((*late, *near_out))
    out_beside = [*first_step(near_out[0], 1), *first_step(near_out[1], 0)]
    lhs = attention(info, routes, down, tokens, up, sums, received, late)
    *out_beside, lhs = lax.optimization_barrier((*out_beside, lhs))
    out_late = onward(out_beside, 1)
    out_pieces = []
    for half in range(2):
        two = slice(half * 2, half * 2 + 2)
        out_pieces += [near_out[half], *out_beside[two], *out_late[two]]

    place = jnp.stack([group, part // 2, part % 2]).astype(jnp.int32)
    operands = (gates, lhs, out_pieces)
    far, far_mine = project_out(((False, 2), (True, 2)), place, *operands, apart=True)
    far_swapped = exchange(far, 0)
    place = lax.optimization_barrier((place, far_mine))[0]
    (theirs,) = project_out(((False, 1), (False, 3), (False, 0)), place, *operands)
    swapped = exchange(theirs, 0)
    low, high = small_call(far_sum_kernel, [(512, 256)] * 2, 1, far_mine, far_swapped)
    place = lax.optimization_barrier((place, theirs, low))[0]
    low, high = exchange(low, 1), exchange(high, -1)
    (mine,) = project_out(((True, 1), (True, 3)), place, *operands)
    ahead, behind = small_call(near_sum_kernel, [(1024, 256)] * 2, 2, mine, swapped, low, high)
    from_behind, from_ahead = exchange(ahead, 1), exchange(behind, -1)
    place = lax.optimization_barrier((place, ahead))[0]
    (own_block,) = project_out(((True, 0),), place, *operands)
    return rounded_sum(own_block[0], swapped[2], from_behind, from_ahead)


def solution(mesh):
    return jax.shard_map(
        body,
        mesh=mesh,
        in_specs=(
            P("req", None),
            P("req", None),
            P("req"),
            P("req"),
            P(),
            P("req"),
            P(),
            P(),
            P("req", "exp"),
            P("req", None, "exp"),
            P(None, "exp", "req"),
            P("req", None, None),
            P("req", None, "exp"),
            P("req", None, "exp"),
        ),
        out_specs=P("req", "exp"),
        check_vma=False,
    )
```

```python
import functools

import jax
import jax.numpy as jnp
from jax import lax
from jax.experimental import pallas as pl
from jax.experimental.pallas import tpu as pltpu
from jax.sharding import PartitionSpec as P

HD = 128
NE = 8
TOPK = 2
SIDE = 4
BF = jnp.bfloat16
F32 = jnp.float32
NEG = -1e30
adapter_scale = 0.5

ROW_KV, ROW_UP = 512, 640
SHARD_ROWS = 704
OUT_ROWS = 512
ROW_DN, SENT_ROWS = 64, 96
PLACES = []
for _piece, _off in ((0, 0), (1, -1), (2, 1)):
    for _i, _near in enumerate((0, -1, 1, 2)):
        PLACES.append((_piece, _i, _near, _off))
EARLY = list(PLACES)
LATE = [(0, 0, 0, 2), (0, 1, -1, 2), (1, 0, 1, 2), (1, 1, 2, 2)]
PLACES += [(3 + piece, shard, first, second) for piece, shard, first, second in LATE]


def torus(dx, dz):
    return [
        (i, ((i // SIDE + dx) % SIDE) * SIDE + (i % SIDE + dz) % SIDE) for i in range(SIDE * SIDE)
    ]


def send(value, along, step):
    return lax.ppermute(value, "req", torus(step, 0) if along == 0 else torus(0, step))


def first_step(value, along):
    return send(value, along, 1), send(value, along, -1)


def source(group, half, first, second):
    x, z = group // SIDE, group % SIDE
    dx, dz = (first, second) if half == 0 else (second, first)
    return ((x + dx + SIDE) % SIDE) * SIDE + (z + dz + SIDE) % SIDE


def cost(us):
    return pl.CostEstimate(flops=int(us * 1.15e9), bytes_accessed=2**20, transcendentals=0)


ANY = pl.BlockSpec(memory_space=pl.ANY)
WHOLE = pl.BlockSpec(memory_space=pltpu.VMEM)
SCALARS = pl.BlockSpec(memory_space=pltpu.SMEM)


def pack_kernel(index_ref, store_ref, down_ref, out_ref):
    def one(i, carry):
        out_ref[i, 0:ROW_DN, :] = store_ref[index_ref[i]]
        for side in range(2):
            out_ref[i, ROW_DN:SENT_ROWS, side * 256 : side * 256 + 256] = down_ref[
                side * 32 : side * 32 + 32, :
            ]
        return carry

    lax.fori_loop(0, out_ref.shape[0], one, 0)


def pack(index, store, down):
    return pl.pallas_call(
        pack_kernel,
        out_shape=jax.ShapeDtypeStruct((16, SENT_ROWS, 512), BF),
        in_specs=[SCALARS] + [WHOLE] * 2,
        out_specs=WHOLE,
        cost_estimate=cost(3),
        name="pack",
    )(index, store, down)


def pick_down_kernel(info_ref, recv_ref, out_ref, sem):
    for j in range(4):
        slot = info_ref[1 + j]
        owner, inner = slot // 4, slot % 4
        start = pl.multiple_of(ROW_DN + (inner % 2) * 16, 16)
        for side in range(2):

            @pl.when(inner // 2 == side)
            def _(side=side, j=j, owner=owner, start=start):
                pltpu.make_async_copy(
                    recv_ref.at[owner, pl.ds(start, 16), pl.ds(side * 256, 256)],
                    out_ref.at[j],
                    sem.at[j],
                ).start()

    for j in range(4):
        pltpu.make_async_copy(out_ref.at[j], out_ref.at[j], sem.at[j]).wait()


def pick_down(info, recv):
    return pl.pallas_call(
        pick_down_kernel,
        out_shape=jax.ShapeDtypeStruct((4, 16, 256), BF),
        in_specs=[SCALARS, ANY],
        out_specs=WHOLE,
        scratch_shapes=[pltpu.SemaphoreType.DMA((4,))],
        cost_estimate=cost(2),
        name="pick_down",
    )(info, recv)


def products(group, x_ref, routes_ref, pieces, shards, half):
    count = len(pieces) // 2
    x = jnp.concatenate(
        [
            x_ref[:, pl.ds(pl.multiple_of(source(group, half, first, second) * 128, 128), 128)]
            for _, _, first, second in shards
        ],
        axis=1,
    )

    def product(row):
        weight = jnp.concatenate(
            [
                pieces[half * count + piece][pl.ds(shard * SHARD_ROWS + row, 128), :]
                for piece, shard, _, _ in shards
            ],
            axis=0,
        )
        return jnp.dot(x, weight, preferred_element_type=F32)

    chosen = [jnp.zeros((256, 256), F32)] * TOPK
    for i in range(4):
        value = product(i * 128)
        for k in range(TOPK):
            chosen[k] = jnp.where(routes_ref[:, k : k + 1] == half * 4 + i, value, chosen[k])
    return chosen, product(ROW_KV)


def pick_up(info_ref, pieces, shards, up_ref):
    count = len(pieces) // 2
    for half in range(2):
        for piece, shard, first, second in shards:
            owner = source(info_ref[0], half, first, second)
            for j in range(4):
                slot = info_ref[1 + j]

                @pl.when(slot // 4 == owner)
                def _(half=half, piece=piece, shard=shard, j=j, slot=slot):
                    start = pl.multiple_of(shard * SHARD_ROWS + ROW_UP + slot % 4 * 16, 16)
                    up_ref[j, half] = pieces[half * count + piece][pl.ds(start, 16), :]


def early_kernel(info_ref, routes_ref, x_ref, *refs):
    pieces = refs[:6]
    up_ref, sums_ref = refs[6:]
    group = info_ref[0]
    up_ref[...] = jnp.zeros_like(up_ref)
    pick_up(info_ref, pieces, EARLY, up_ref)

    def block(j, carry):
        rows = pl.ds(pl.multiple_of(j * 256, 256), 256)
        x, routes = x_ref.at[rows, :], routes_ref.at[rows, :]
        first, base = products(group, x, routes, pieces, EARLY, 0)
        sums_ref[j, 2] = base
        second, base = products(group, x, routes, pieces, EARLY, 1)
        sums_ref[j, 3] = base
        for k in range(TOPK):
            sums_ref[j, k] = first[k] + second[k]
        return carry

    lax.fori_loop(0, 4, block, 0)


def project_early(info, routes, x, pieces):
    return pl.pallas_call(
        early_kernel,
        out_shape=(
            jax.ShapeDtypeStruct((4, 2, 16, 256), BF),
            jax.ShapeDtypeStruct((4, 4, 256, 256), F32),
        ),
        in_specs=[SCALARS] + [WHOLE] * 8,
        out_specs=(WHOLE, WHOLE),
        compiler_params=pltpu.CompilerParams(vmem_limit_bytes=20 * 2**20),
        cost_estimate=cost(15),
        name="project_early",
    )(info, routes, x, *pieces)


def attend_kernel(info_ref, routes_ref, down_ref, x_ref, up_ref, sums_ref, recv_hbm, *refs):
    pieces = refs[:4]
    out_ref, sums, up, cache, sem = refs[4:]
    group = info_ref[0]
    for j in range(4):
        pltpu.make_async_copy(
            recv_hbm.at[info_ref[5 + j], pl.ds(0, 64), :], cache.at[j], sem.at[j]
        ).start()
    up[...] = up_ref[...]
    pick_up(info_ref, pieces, LATE, up)

    def attend(j, carry):
        pltpu.make_async_copy(cache.at[j], cache.at[j], sem.at[j]).wait()
        rows = pl.ds(pl.multiple_of(j * 256, 256), 256)
        x, routes = x_ref.at[rows, :], routes_ref.at[rows, :]
        for half in range(2):
            chosen, base = products(group, x, routes, pieces, LATE, half)
            sums[2 + half] = sums_ref[j, 2 + half] + base
            for k in range(TOPK):
                before = sums_ref[j, k] if half == 0 else sums[k]
                sums[k] = before + chosen[k]
        down = jnp.concatenate([down_ref[e, j] for e in range(NE)], axis=1)
        low = lax.dot_general(
            x[...], down, (((1,), (1,)), ((), ())), preferred_element_type=F32
        ).astype(BF)
        cached_length = info_ref[9 + j]
        place = lax.broadcasted_iota(jnp.int32, (256, 320), 1)
        query_at = lax.broadcasted_iota(jnp.int32, (256, 320), 0)
        allowed = (place < cached_length) | ((place >= 64) & (place - 64 <= query_at))
        for h in range(2):
            cols = slice(h * HD, (h + 1) * HD)
            extra = jnp.dot(low, up[j, h], preferred_element_type=F32)
            fresh = (sums[2 + h] + adapter_scale * extra).astype(BF)
            keys = jnp.concatenate(
                [cache[j, :, h * 256 : h * 256 + HD], fresh[:, 0:HD]], axis=0
            )
            values = jnp.concatenate(
                [cache[j, :, h * 256 + HD : h * 256 + 2 * HD], fresh[:, HD : 2 * HD]], axis=0
            )
            attended = []
            for k in range(TOPK):
                scores = lax.dot_general(
                    sums[k, :, cols].astype(BF),
                    keys,
                    (((1,), (1,)), ((), ())),
                    preferred_element_type=F32,
                ) * (HD**-0.5)
                scores = jnp.where(allowed, scores, NEG)
                weights = jnp.exp(scores - jnp.max(scores, axis=-1, keepdims=True))
                total = jnp.sum(weights, axis=-1, keepdims=True)
                probability = (weights * (1.0 / total)).astype(BF)
                attended.append(jnp.dot(probability, values, preferred_element_type=F32))
            for e in range(NE):
                chosen = jnp.where(
                    routes[:, 0:1] == e,
                    attended[0],
                    jnp.where(routes[:, 1:2] == e, attended[1], 0.0),
                )
                out_ref[e, rows, cols] = chosen.astype(BF)
        return carry

    lax.fori_loop(0, 4, attend, 0)


def attention(info, routes, down, x, up, sums, recv, pieces):
    return pl.pallas_call(
        attend_kernel,
        out_shape=jax.ShapeDtypeStruct((NE, 1024, 256), BF),
        in_specs=[SCALARS] + [WHOLE] * 5 + [ANY] + [WHOLE] * 4,
        out_specs=WHOLE,
        scratch_shapes=[
            pltpu.VMEM((4, 256, 256), F32),
            pltpu.VMEM((4, 2, 16, 256), BF),
            pltpu.VMEM((4, 64, 512), BF),
            pltpu.SemaphoreType.DMA((4,)),
        ],
        compiler_params=pltpu.CompilerParams(vmem_limit_bytes=20 * 2**20),
        cost_estimate=cost(22),
        name="attention",
    )(info, routes, down, x, up, sums, recv, *pieces)


def project_out_kernel(blocks, place_ref, gates_ref, lhs_ref, *refs):
    pieces = refs[:10]
    *outs, w, sem = refs[10:]
    group, y, core = place_ref[0], place_ref[1], place_ref[2]
    for b, (mine, ahead) in enumerate(blocks):
        wanted_x = (y + ahead) % 4
        side = core if mine else 1 - core
        for half in range(2):
            for piece, shard, first, second in PLACES:
                owner = source(group, half, first, second)

                @pl.when((owner // 4 == wanted_x) & ((owner % 4) // 2 == side))
                def _(b=b, half=half, piece=piece, shard=shard, owner=owner):
                    pltpu.make_async_copy(
                        pieces[half * 5 + piece].at[pl.ds(shard * OUT_ROWS, OUT_ROWS), :],
                        w.at[b, half, owner % 2],
                        sem.at[b],
                    ).start()

    def block(b, out_ref):
        pltpu.make_async_copy(w.at[b], w.at[b], sem.at[b]).wait()

        def tile(i, carry):
            rows = pl.ds(pl.multiple_of(i * 256, 256), 256)
            total = None
            for e in range(NE):
                half, pair, lane = e // 4, (e % 4) // 2, e % 2
                place = (pl.ds(pair * 256, 256), pl.ds(lane * 128, 128))
                weight = jnp.concatenate(
                    [w[b, half, 0, place[0], place[1]], w[b, half, 1, place[0], place[1]]], axis=1
                )
                value = jnp.dot(lhs_ref[e, rows, :], weight, preferred_element_type=F32)
                value = value * gates_ref[rows, e : e + 1]
                total = value if total is None else total + value
            out_ref[rows, :] = total.astype(BF)
            return carry

        lax.fori_loop(0, 4, tile, 0)

    if len(outs) > 1:
        for b, out_ref in enumerate(outs):
            block(b, out_ref)
    else:

        def step(b, carry):
            block(b, outs[0].at[b])
            return carry

        lax.fori_loop(0, len(blocks), step, 0)


def project_out(blocks, place, gates, lhs, pieces, apart=False):
    if apart:
        shapes = [jax.ShapeDtypeStruct((1024, 256), BF)] * len(blocks)
    else:
        shapes = [jax.ShapeDtypeStruct((len(blocks), 1024, 256), BF)]
    return pl.pallas_call(
        functools.partial(project_out_kernel, blocks),
        out_shape=shapes,
        in_specs=[SCALARS, WHOLE, WHOLE] + [ANY] * 10,
        out_specs=[WHOLE] * len(shapes),
        scratch_shapes=[
            pltpu.VMEM((len(blocks), 2, 2, OUT_ROWS, 256), BF),
            pltpu.SemaphoreType.DMA((len(blocks),)),
        ],
        compiler_params=pltpu.CompilerParams(vmem_limit_bytes=8 * 2**20),
        cost_estimate=cost(2.2 * len(blocks)),
        name="project_out_" + str(len(blocks)),
    )(place, gates, lhs, *pieces)


def small_call(kernel, shapes, us, *operands):
    return pl.pallas_call(
        kernel,
        out_shape=[jax.ShapeDtypeStruct(shape, BF) for shape in shapes],
        in_specs=[WHOLE] * len(operands),
        out_specs=[WHOLE] * len(shapes),
        compiler_params=pltpu.CompilerParams(vmem_limit_bytes=8 * 2**20),
        cost_estimate=cost(us),
        name=kernel.__name__,
    )(*operands)


def forward_kernel(*refs):
    for i in range(4):
        source_ref, out_ref = refs[i], refs[4 + i]
        half = out_ref.shape[0]
        out_ref[...] = source_ref[pl.ds(i % 2 * half, half), :]


def forwarded(values):
    half = values[0].shape[0] // 2
    return small_call(forward_kernel, [(half, 256)] * 4, 2, *values)


def onward(values, along):
    low0, high0, low1, high1 = forwarded(values)
    return [
        send(low0, along, 1),
        send(high0, along, -1),
        send(low1, 1 - along, 1),
        send(high1, 1 - along, -1),
    ]


def far_sum_kernel(mine_ref, theirs_ref, low_ref, high_ref):
    for i, out_ref in enumerate((low_ref, high_ref)):
        rows = pl.ds(i * 512, 512)
        out_ref[...] = (mine_ref[rows, :].astype(F32) + theirs_ref[rows, :].astype(F32)).astype(BF)


def near_sum_kernel(mine_ref, theirs_ref, low_ref, high_ref, ahead_ref, behind_ref):
    for i, out_ref in enumerate((ahead_ref, behind_ref)):
        extra_ref = (low_ref, high_ref)[i]
        for half in range(2):
            rows = pl.ds(half * 512, 512)
            total = mine_ref[i, rows, :].astype(F32) + theirs_ref[i, rows, :].astype(F32)
            if half == i:
                total = total + extra_ref[...].astype(F32)
            out_ref[rows, :] = total.astype(BF)


def exchange(value, step):
    if step == 0:
        return lax.ppermute(value, "exp", [(i, i ^ 1) for i in range(8)])
    return lax.ppermute(value, "exp", [(i, (i + 2 * step) % 8) for i in range(8)])


def rounded_sum(*values):
    total = values[0].astype(F32)
    for value in values[1:]:
        total = total + value.astype(F32)
    return total.astype(BF)


def body(
    tokens,
    routes,
    lengths,
    cached_prefix_length,
    prefix_cache_row,
    adapter_per_request,
    adapter_storage_slot,
    router_weight,
    key_value_weight,
    expert_query_weight,
    expert_output_weight,
    adapter_down_maps,
    adapter_up_maps,
    prefix_cache_store,
):
    group = lax.axis_index("req")
    part = lax.axis_index("exp")
    rows_by_group = prefix_cache_row.reshape(16, 4)
    held = (rows_by_group == group).astype(jnp.int32)
    wanted_by = jnp.sum(held * jnp.arange(4, dtype=jnp.int32)[None, :], axis=1)
    down_rows = (
        lax.dynamic_slice_in_dim(adapter_down_maps, part * 256, 256, 1)
        .transpose(0, 2, 1)
        .reshape(64, 256)
    )
    outgoing = pack(wanted_by, prefix_cache_store, down_rows)
    up_rows = adapter_up_maps.reshape(64, 512)

    query_rows = expert_query_weight.transpose(1, 0, 2).reshape(NE * 128, 256)
    out_rows = (
        expert_output_weight.reshape(4, 2, 256, 128).transpose(0, 2, 1, 3).reshape(1024, 256)
    )
    own = [
        jnp.concatenate(
            [
                query_rows[half * 512 : half * 512 + 512],
                key_value_weight[:, half * 256 : half * 256 + 256],
                up_rows[:, half * 256 : half * 256 + 256],
                out_rows[half * 512 : half * 512 + 512],
            ],
            axis=0,
        )
        for half in range(2)
    ]
    adapter_hot = (
        adapter_per_request[:, None]
        == jnp.arange(adapter_storage_slot.shape[0], dtype=jnp.int32)[None, :]
    ).astype(jnp.int32)
    slots = jnp.sum(adapter_hot * adapter_storage_slot[None, :], axis=1)
    own_rows = lax.dynamic_slice_in_dim(prefix_cache_row, group * 4, 4, 0)
    info = jnp.concatenate([group[None].astype(jnp.int32), slots, own_rows, cached_prefix_length])
    place = jnp.stack([group, lax.div(part, 2), lax.rem(part, 2)]).astype(jnp.int32)
    neighbours = [*first_step(own[0], 0), *first_step(own[1], 1)]
    received = lax.all_to_all(outgoing, "req", 0, 0, tiled=True)
    *neighbours, info, place, _ = lax.optimization_barrier((*neighbours, info, place, outgoing))
    passed = onward(neighbours, 0)
    near, near_out = [], []
    for half in range(2):
        before, after = neighbours[2 * half : 2 * half + 2]
        far_low, far_high = passed[2 * half : 2 * half + 2]
        cut = SHARD_ROWS - far_low.shape[0]
        near.append(
            jnp.concatenate(
                [
                    own[half][:SHARD_ROWS],
                    before[:SHARD_ROWS],
                    after[:SHARD_ROWS],
                    far_low,
                    far_high[:cut],
                ],
                axis=0,
            )
        )
        near_out.append(
            jnp.concatenate(
                [
                    own[half][SHARD_ROWS:],
                    before[SHARD_ROWS:],
                    after[SHARD_ROWS:],
                    far_high[cut:],
                ],
                axis=0,
            )
        )

    logits = jnp.dot(tokens, router_weight, preferred_element_type=F32)
    expert = jnp.arange(NE, dtype=jnp.int32)
    route_hot = (routes[:, :, None] == expert[None, None, :]).astype(F32)
    chosen = jnp.sum(route_hot * logits[:, None, :], axis=-1)
    gate_values = jax.nn.sigmoid(chosen - chosen[:, ::-1])
    live = (jnp.arange(256, dtype=jnp.int32)[None, :] < lengths[:, None]).reshape(1024, 1)
    gates = jnp.sum(route_hot * gate_values[:, :, None], axis=1) * live.astype(F32)

    beside = [*first_step(near[0], 1), *first_step(near[1], 0)]
    down_part = pick_down(info, received)
    down = lax.all_to_all(
        jnp.broadcast_to(down_part[None], (NE, 4, 16, 256)), "exp", 0, 0, tiled=True
    )
    *beside, down, gates = lax.optimization_barrier((*beside, down, gates))
    late = onward(beside, 1)
    up, sums = project_early(info, routes, tokens, [near[0], *beside[:2], near[1], *beside[2:]])
    *late, near_out[0], near_out[1] = lax.optimization_barrier((*late, *near_out))
    out_beside = [*first_step(near_out[0], 1), *first_step(near_out[1], 0)]
    lhs = attention(info, routes, down, tokens, up, sums, received, late)
    *out_beside, lhs = lax.optimization_barrier((*out_beside, lhs))
    out_late = onward(out_beside, 1)
    out_pieces = []
    for half in range(2):
        two = slice(half * 2, half * 2 + 2)
        out_pieces += [near_out[half], *out_beside[two], *out_late[two]]

    operands = (gates, lhs, out_pieces)
    far, far_mine = project_out(((False, 2), (True, 2)), place, *operands, apart=True)
    far_swapped = exchange(far, 0)
    place = lax.optimization_barrier((place, far_mine))[0]
    (theirs,) = project_out(((False, 1), (False, 3), (False, 0)), place, *operands)
    swapped = exchange(theirs, 0)
    low, high = small_call(far_sum_kernel, [(512, 256)] * 2, 1, far_mine, far_swapped)
    place = lax.optimization_barrier((place, theirs, low))[0]
    low, high = exchange(low, 1), exchange(high, -1)
    (mine,) = project_out(((True, 1), (True, 3)), place, *operands)
    ahead, behind = small_call(near_sum_kernel, [(1024, 256)] * 2, 2, mine, swapped, low, high)
    from_behind, from_ahead = exchange(ahead, 1), exchange(behind, -1)
    place = lax.optimization_barrier((place, ahead))[0]
    (own_block,) = project_out(((True, 0),), place, *operands)
    return rounded_sum(own_block[0], swapped[2], from_behind, from_ahead)


def solution(mesh):
    return jax.shard_map(
        body,
        mesh=mesh,
        in_specs=(
            P("req", None),
            P("req", None),
            P("req"),
            P("req"),
            P(),
            P("req"),
            P(),
            P(),
            P("req", "exp"),
            P("req", None, "exp"),
            P(None, "exp", "req"),
            P("req", None, None),
            P("req", None, "exp"),
            P("req", None, "exp"),
        ),
        out_specs=P("req", "exp"),
        check_vma=False,
    )
```

```python
import functools

import jax
import jax.numpy as jnp
from jax import lax
from jax.experimental import pallas as pl
from jax.experimental.pallas import tpu as pltpu
from jax.sharding import PartitionSpec as P

HD = 128
NE = 8
TOPK = 2
SIDE = 4
BF = jnp.bfloat16
F32 = jnp.float32
NEG = -1e30
adapter_scale = 0.5

ROW_KV, ROW_UP = 512, 640
SHARD_ROWS = 704
OUT_ROWS = 512
ROW_DN, SENT_ROWS = 64, 96
PLACES = []
for _piece, _off in ((0, 0), (1, -1), (2, 1)):
    for _i, _near in enumerate((0, -1, 1, 2)):
        PLACES.append((_piece, _i, _near, _off))
EARLY = list(PLACES)
LATE = [(0, 0, 0, 2), (0, 1, -1, 2), (1, 0, 1, 2), (1, 1, 2, 2)]
PLACES += [(3 + piece, shard, first, second) for piece, shard, first, second in LATE]


def torus(dx, dz):
    return [
        (i, ((i // SIDE + dx) % SIDE) * SIDE + (i % SIDE + dz) % SIDE) for i in range(SIDE * SIDE)
    ]


def send(value, along, step):
    return lax.ppermute(value, "req", torus(step, 0) if along == 0 else torus(0, step))


def first_step(value, along):
    return send(value, along, 1), send(value, along, -1)


def source(group, half, first, second):
    x, z = group // SIDE, group % SIDE
    dx, dz = (first, second) if half == 0 else (second, first)
    return ((x + dx + SIDE) % SIDE) * SIDE + (z + dz + SIDE) % SIDE


def cost(us):
    return pl.CostEstimate(flops=int(us * 1.15e9), bytes_accessed=2**20, transcendentals=0)


ANY = pl.BlockSpec(memory_space=pl.ANY)
WHOLE = pl.BlockSpec(memory_space=pltpu.VMEM)
SCALARS = pl.BlockSpec(memory_space=pltpu.SMEM)


def pack_kernel(index_ref, store_ref, down_ref, out_ref):
    def one(i, carry):
        out_ref[i, 0:ROW_DN, :] = store_ref[index_ref[i]]
        for side in range(2):
            out_ref[i, ROW_DN:SENT_ROWS, side * 256 : side * 256 + 256] = down_ref[
                side * 32 : side * 32 + 32, :
            ]
        return carry

    lax.fori_loop(0, out_ref.shape[0], one, 0)


def pack(index, store, down):
    return pl.pallas_call(
        pack_kernel,
        out_shape=jax.ShapeDtypeStruct((16, SENT_ROWS, 512), BF),
        in_specs=[SCALARS] + [WHOLE] * 2,
        out_specs=WHOLE,
        cost_estimate=cost(3),
        name="pack",
    )(index, store, down)


def pick_down_kernel(info_ref, recv_ref, out_ref, sem):
    for j in range(4):
        slot = info_ref[1 + j]
        owner, inner = slot // 4, slot % 4
        start = pl.multiple_of(ROW_DN + (inner % 2) * 16, 16)
        for side in range(2):

            @pl.when(inner // 2 == side)
            def _(side=side, j=j, owner=owner, start=start):
                pltpu.make_async_copy(
                    recv_ref.at[owner, pl.ds(start, 16), pl.ds(side * 256, 256)],
                    out_ref.at[j],
                    sem.at[j],
                ).start()

    for j in range(4):
        pltpu.make_async_copy(out_ref.at[j], out_ref.at[j], sem.at[j]).wait()


def pick_down(info, recv):
    return pl.pallas_call(
        pick_down_kernel,
        out_shape=jax.ShapeDtypeStruct((4, 16, 256), BF),
        in_specs=[SCALARS, ANY],
        out_specs=WHOLE,
        scratch_shapes=[pltpu.SemaphoreType.DMA((4,))],
        cost_estimate=cost(2),
        name="pick_down",
    )(info, recv)


def products(group, x_ref, routes_ref, pieces, shards, half):
    count = len(pieces) // 2
    x = jnp.concatenate(
        [
            x_ref[:, pl.ds(pl.multiple_of(source(group, half, first, second) * 128, 128), 128)]
            for _, _, first, second in shards
        ],
        axis=1,
    )

    def product(row):
        weight = jnp.concatenate(
            [
                pieces[half * count + piece][pl.ds(shard * SHARD_ROWS + row, 128), :]
                for piece, shard, _, _ in shards
            ],
            axis=0,
        )
        return jnp.dot(x, weight, preferred_element_type=F32)

    chosen = [jnp.zeros((256, 256), F32)] * TOPK
    for i in range(4):
        value = product(i * 128)
        for k in range(TOPK):
            chosen[k] = jnp.where(routes_ref[:, k : k + 1] == half * 4 + i, value, chosen[k])
    return chosen, product(ROW_KV)


def pick_up(info_ref, pieces, shards, up_ref):
    count = len(pieces) // 2
    for half in range(2):
        for piece, shard, first, second in shards:
            owner = source(info_ref[0], half, first, second)
            for j in range(4):
                slot = info_ref[1 + j]

                @pl.when(slot // 4 == owner)
                def _(half=half, piece=piece, shard=shard, j=j, slot=slot):
                    start = pl.multiple_of(shard * SHARD_ROWS + ROW_UP + slot % 4 * 16, 16)
                    up_ref[j, half] = pieces[half * count + piece][pl.ds(start, 16), :]


def early_kernel(info_ref, routes_ref, x_ref, *refs):
    pieces = refs[:6]
    up_ref, sums_ref = refs[6:]
    group = info_ref[0]
    up_ref[...] = jnp.zeros_like(up_ref)
    pick_up(info_ref, pieces, EARLY, up_ref)

    def block(j, carry):
        rows = pl.ds(pl.multiple_of(j * 256, 256), 256)
        x, routes = x_ref.at[rows, :], routes_ref.at[rows, :]
        first, base = products(group, x, routes, pieces, EARLY, 0)
        sums_ref[j, 2] = base
        second, base = products(group, x, routes, pieces, EARLY, 1)
        sums_ref[j, 3] = base
        for k in range(TOPK):
            sums_ref[j, k] = first[k] + second[k]
        return carry

    lax.fori_loop(0, 4, block, 0)


def project_early(info, routes, x, pieces):
    return pl.pallas_call(
        early_kernel,
        out_shape=(
            jax.ShapeDtypeStruct((4, 2, 16, 256), BF),
            jax.ShapeDtypeStruct((4, 4, 256, 256), F32),
        ),
        in_specs=[SCALARS] + [WHOLE] * 8,
        out_specs=(WHOLE, WHOLE),
        compiler_params=pltpu.CompilerParams(vmem_limit_bytes=20 * 2**20),
        cost_estimate=cost(15),
        name="project_early",
    )(info, routes, x, *pieces)


def attend_kernel(info_ref, routes_ref, down_ref, x_ref, up_ref, sums_ref, recv_hbm, *refs):
    pieces = refs[:4]
    out_ref, sums, up, cache, sem = refs[4:]
    group = info_ref[0]
    for j in range(4):
        pltpu.make_async_copy(
            recv_hbm.at[info_ref[5 + j], pl.ds(0, 64), :], cache.at[j], sem.at[j]
        ).start()
    up[...] = up_ref[...]
    pick_up(info_ref, pieces, LATE, up)

    def attend(j, carry):
        pltpu.make_async_copy(cache.at[j], cache.at[j], sem.at[j]).wait()
        rows = pl.ds(pl.multiple_of(j * 256, 256), 256)
        x, routes = x_ref.at[rows, :], routes_ref.at[rows, :]
        for half in range(2):
            chosen, base = products(group, x, routes, pieces, LATE, half)
            sums[2 + half] = sums_ref[j, 2 + half] + base
            for k in range(TOPK):
                before = sums_ref[j, k] if half == 0 else sums[k]
                sums[k] = before + chosen[k]
        down = jnp.concatenate([down_ref[e, j] for e in range(NE)], axis=1)
        low = lax.dot_general(
            x[...], down, (((1,), (1,)), ((), ())), preferred_element_type=F32
        ).astype(BF)
        cached_length = info_ref[9 + j]
        place = lax.broadcasted_iota(jnp.int32, (256, 320), 1)
        query_at = lax.broadcasted_iota(jnp.int32, (256, 320), 0)
        allowed = (place < cached_length) | ((place >= 64) & (place - 64 <= query_at))
        for h in range(2):
            cols = slice(h * HD, (h + 1) * HD)
            extra = jnp.dot(low, up[j, h], preferred_element_type=F32)
            fresh = (sums[2 + h] + adapter_scale * extra).astype(BF)
            keys = jnp.concatenate(
                [cache[j, :, h * 256 : h * 256 + HD], fresh[:, 0:HD]], axis=0
            )
            values = jnp.concatenate(
                [cache[j, :, h * 256 + HD : h * 256 + 2 * HD], fresh[:, HD : 2 * HD]], axis=0
            )
            attended = []
            for k in range(TOPK):
                scores = lax.dot_general(
                    sums[k, :, cols].astype(BF),
                    keys,
                    (((1,), (1,)), ((), ())),
                    preferred_element_type=F32,
                ) * (HD**-0.5)
                scores = jnp.where(allowed, scores, NEG)
                weights = jnp.exp(scores - jnp.max(scores, axis=-1, keepdims=True))
                total = jnp.sum(weights, axis=-1, keepdims=True)
                probability = (weights * (1.0 / total)).astype(BF)
                attended.append(jnp.dot(probability, values, preferred_element_type=F32))
            for e in range(NE):
                chosen = jnp.where(
                    routes[:, 0:1] == e,
                    attended[0],
                    jnp.where(routes[:, 1:2] == e, attended[1], 0.0),
                )
                out_ref[e, rows, cols] = chosen.astype(BF)
        return carry

    lax.fori_loop(0, 4, attend, 0)


def attention(info, routes, down, x, up, sums, recv, pieces):
    return pl.pallas_call(
        attend_kernel,
        out_shape=jax.ShapeDtypeStruct((NE, 1024, 256), BF),
        in_specs=[SCALARS] + [WHOLE] * 5 + [ANY] + [WHOLE] * 4,
        out_specs=WHOLE,
        scratch_shapes=[
            pltpu.VMEM((4, 256, 256), F32),
            pltpu.VMEM((4, 2, 16, 256), BF),
            pltpu.VMEM((4, 64, 512), BF),
            pltpu.SemaphoreType.DMA((4,)),
        ],
        compiler_params=pltpu.CompilerParams(vmem_limit_bytes=20 * 2**20),
        cost_estimate=cost(22),
        name="attention",
    )(info, routes, down, x, up, sums, recv, *pieces)


def project_out_kernel(blocks, place_ref, gates_ref, lhs_ref, *refs):
    pieces = refs[:10]
    *outs, w, sem = refs[10:]
    group, y, core = place_ref[0], place_ref[1], place_ref[2]
    for b, (mine, ahead) in enumerate(blocks):
        wanted_x = (y + ahead) % 4
        side = core if mine else 1 - core
        for half in range(2):
            for piece, shard, first, second in PLACES:
                owner = source(group, half, first, second)

                @pl.when((owner // 4 == wanted_x) & ((owner % 4) // 2 == side))
                def _(b=b, half=half, piece=piece, shard=shard, owner=owner):
                    pltpu.make_async_copy(
                        pieces[half * 5 + piece].at[pl.ds(shard * OUT_ROWS, OUT_ROWS), :],
                        w.at[b, half, owner % 2],
                        sem.at[b],
                    ).start()

    def block(b, out_ref):
        pltpu.make_async_copy(w.at[b], w.at[b], sem.at[b]).wait()

        def tile(i, carry):
            rows = pl.ds(pl.multiple_of(i * 256, 256), 256)
            total = None
            for e in range(NE):
                half, pair, lane = e // 4, (e % 4) // 2, e % 2
                place = (pl.ds(pair * 256, 256), pl.ds(lane * 128, 128))
                weight = jnp.concatenate(
                    [w[b, half, 0, place[0], place[1]], w[b, half, 1, place[0], place[1]]], axis=1
                )
                value = jnp.dot(lhs_ref[e, rows, :], weight, preferred_element_type=F32)
                value = value * gates_ref[rows, e : e + 1]
                total = value if total is None else total + value
            out_ref[rows, :] = total.astype(BF)
            return carry

        lax.fori_loop(0, 4, tile, 0)

    if len(outs) > 1:
        for b, out_ref in enumerate(outs):
            block(b, out_ref)
    else:

        def step(b, carry):
            block(b, outs[0].at[b])
            return carry

        lax.fori_loop(0, len(blocks), step, 0)


def project_out(blocks, place, gates, lhs, pieces, apart=False):
    if apart:
        shapes = [jax.ShapeDtypeStruct((1024, 256), BF)] * len(blocks)
    else:
        shapes = [jax.ShapeDtypeStruct((len(blocks), 1024, 256), BF)]
    return pl.pallas_call(
        functools.partial(project_out_kernel, blocks),
        out_shape=shapes,
        in_specs=[SCALARS, WHOLE, WHOLE] + [ANY] * 10,
        out_specs=[WHOLE] * len(shapes),
        scratch_shapes=[
            pltpu.VMEM((len(blocks), 2, 2, OUT_ROWS, 256), BF),
            pltpu.SemaphoreType.DMA((len(blocks),)),
        ],
        compiler_params=pltpu.CompilerParams(vmem_limit_bytes=8 * 2**20),
        cost_estimate=cost(2.2 * len(blocks)),
        name="project_out_" + str(len(blocks)),
    )(place, gates, lhs, *pieces)


def small_call(kernel, shapes, us, *operands):
    return pl.pallas_call(
        kernel,
        out_shape=[jax.ShapeDtypeStruct(shape, BF) for shape in shapes],
        in_specs=[WHOLE] * len(operands),
        out_specs=[WHOLE] * len(shapes),
        compiler_params=pltpu.CompilerParams(vmem_limit_bytes=8 * 2**20),
        cost_estimate=cost(us),
        name=kernel.__name__,
    )(*operands)


def forward_kernel(*refs):
    for i in range(4):
        source_ref, out_ref = refs[i], refs[4 + i]
        half = out_ref.shape[0]
        out_ref[...] = source_ref[pl.ds(i % 2 * half, half), :]


def forwarded(values):
    half = values[0].shape[0] // 2
    return small_call(forward_kernel, [(half, 256)] * 4, 2, *values)


def onward(values, along):
    low0, high0, low1, high1 = forwarded(values)
    return [
        send(low0, along, 1),
        send(high0, along, -1),
        send(low1, 1 - along, 1),
        send(high1, 1 - along, -1),
    ]


def far_sum_kernel(mine_ref, theirs_ref, low_ref, high_ref):
    for i, out_ref in enumerate((low_ref, high_ref)):
        rows = pl.ds(i * 512, 512)
        out_ref[...] = (mine_ref[rows, :].astype(F32) + theirs_ref[rows, :].astype(F32)).astype(BF)


def near_sum_kernel(mine_ref, theirs_ref, low_ref, high_ref, ahead_ref, behind_ref):
    for i, out_ref in enumerate((ahead_ref, behind_ref)):
        extra_ref = (low_ref, high_ref)[i]
        for half in range(2):
            rows = pl.ds(half * 512, 512)
            total = mine_ref[i, rows, :].astype(F32) + theirs_ref[i, rows, :].astype(F32)
            if half == i:
                total = total + extra_ref[...].astype(F32)
            out_ref[rows, :] = total.astype(BF)


def exchange(value, step):
    if step == 0:
        return lax.ppermute(value, "exp", [(i, i ^ 1) for i in range(8)])
    return lax.ppermute(value, "exp", [(i, (i + 2 * step) % 8) for i in range(8)])


def rounded_sum(*values):
    total = values[0].astype(F32)
    for value in values[1:]:
        total = total + value.astype(F32)
    return total.astype(BF)


def body(
    tokens,
    routes,
    lengths,
    cached_prefix_length,
    prefix_cache_row,
    adapter_per_request,
    adapter_storage_slot,
    router_weight,
    key_value_weight,
    expert_query_weight,
    expert_output_weight,
    adapter_down_maps,
    adapter_up_maps,
    prefix_cache_store,
):
    group = lax.axis_index("req")
    part = lax.axis_index("exp")
    rows_by_group = prefix_cache_row.reshape(16, 4)
    held = (rows_by_group == group).astype(jnp.int32)
    wanted_by = jnp.sum(held * jnp.arange(4, dtype=jnp.int32)[None, :], axis=1)
    down_rows = (
        lax.dynamic_slice_in_dim(adapter_down_maps, part * 256, 256, 1)
        .transpose(0, 2, 1)
        .reshape(64, 256)
    )
    outgoing = pack(wanted_by, prefix_cache_store, down_rows)
    up_rows = adapter_up_maps.reshape(64, 512)

    query_rows = expert_query_weight.transpose(1, 0, 2).reshape(NE * 128, 256)
    out_rows = (
        expert_output_weight.reshape(4, 2, 256, 128).transpose(0, 2, 1, 3).reshape(1024, 256)
    )
    own = [
        jnp.concatenate(
            [
                query_rows[half * 512 : half * 512 + 512],
                key_value_weight[:, half * 256 : half * 256 + 256],
                up_rows[:, half * 256 : half * 256 + 256],
                out_rows[half * 512 : half * 512 + 512],
            ],
            axis=0,
        )
        for half in range(2)
    ]
    adapter_hot = (
        adapter_per_request[:, None]
        == jnp.arange(adapter_storage_slot.shape[0], dtype=jnp.int32)[None, :]
    ).astype(jnp.int32)
    slots = jnp.sum(adapter_hot * adapter_storage_slot[None, :], axis=1)
    own_rows = lax.dynamic_slice_in_dim(prefix_cache_row, group * 4, 4, 0)
    info = jnp.concatenate([group[None].astype(jnp.int32), slots, own_rows, cached_prefix_length])
    place = jnp.stack([group, lax.div(part, 2), lax.rem(part, 2)]).astype(jnp.int32)
    neighbours = [*first_step(own[0], 0), *first_step(own[1], 1)]
    received = lax.all_to_all(outgoing, "req", 0, 0, tiled=True)
    *neighbours, info, place, _ = lax.optimization_barrier((*neighbours, info, place, outgoing))
    passed = onward(neighbours, 0)
    near, near_out = [], []
    for half in range(2):
        before, after = neighbours[2 * half : 2 * half + 2]
        far_low, far_high = passed[2 * half : 2 * half + 2]
        cut = SHARD_ROWS - far_low.shape[0]
        near.append(
            jnp.concatenate(
                [
                    own[half][:SHARD_ROWS],
                    before[:SHARD_ROWS],
                    after[:SHARD_ROWS],
                    far_low,
                    far_high[:cut],
                ],
                axis=0,
            )
        )
        near_out.append(
            jnp.concatenate(
                [
                    own[half][SHARD_ROWS:],
                    before[SHARD_ROWS:],
                    after[SHARD_ROWS:],
                    far_high[cut:],
                ],
                axis=0,
            )
        )

    logits = jnp.dot(tokens, router_weight, preferred_element_type=F32)
    expert = jnp.arange(NE, dtype=jnp.int32)
    route_hot = (routes[:, :, None] == expert[None, None, :]).astype(F32)
    chosen = jnp.sum(route_hot * logits[:, None, :], axis=-1)
    gate_values = jax.nn.sigmoid(chosen - chosen[:, ::-1])
    live = (jnp.arange(256, dtype=jnp.int32)[None, :] < lengths[:, None]).reshape(1024, 1)
    gates = jnp.sum(route_hot * gate_values[:, :, None], axis=1) * live.astype(F32)

    beside = [*first_step(near[0], 1), *first_step(near[1], 0)]
    down_part = pick_down(info, received)
    down_sent = jnp.broadcast_to(down_part[None], (NE, 4, 16, 256))
    down = lax.all_to_all(down_sent, "exp", 0, 0, tiled=True)
    *beside, gates, _ = lax.optimization_barrier((*beside, gates, down_sent))
    late = onward(beside, 1)
    up, sums = project_early(info, routes, tokens, [near[0], *beside[:2], near[1], *beside[2:]])
    *late, near_out[0], near_out[1] = lax.optimization_barrier((*late, *near_out))
    out_beside = [*first_step(near_out[0], 1), *first_step(near_out[1], 0)]
    lhs = attention(info, routes, down, tokens, up, sums, received, late)
    *out_beside, lhs = lax.optimization_barrier((*out_beside, lhs))
    out_late = onward(out_beside, 1)
    out_pieces = []
    for half in range(2):
        two = slice(half * 2, half * 2 + 2)
        out_pieces += [near_out[half], *out_beside[two], *out_late[two]]

    operands = (gates, lhs, out_pieces)
    far, far_mine = project_out(((False, 2), (True, 2)), place, *operands, apart=True)
    far_swapped = exchange(far, 0)
    place = lax.optimization_barrier((place, far_mine))[0]
    (theirs,) = project_out(((False, 1), (False, 3)), place, *operands)
    swapped = exchange(theirs, 0)
    low, high = small_call(far_sum_kernel, [(512, 256)] * 2, 1, far_mine, far_swapped)
    place = lax.optimization_barrier((place, theirs, low))[0]
    low, high = exchange(low, 1), exchange(high, -1)
    (mine,) = project_out(((True, 1), (True, 3)), place, *operands)
    ahead, behind = small_call(near_sum_kernel, [(1024, 256)] * 2, 2, mine, swapped, low, high)
    from_behind, from_ahead = exchange(ahead, 1), exchange(behind, -1)
    place = lax.optimization_barrier((place, ahead))[0]
    (near_block,) = project_out(((False, 0),), place, *operands)
    near_swapped = exchange(near_block, 0)
    place = lax.optimization_barrier((place, near_block))[0]
    (own_block,) = project_out(((True, 0),), place, *operands)
    return rounded_sum(own_block[0], near_swapped[0], from_behind, from_ahead)


def solution(mesh):
    return jax.shard_map(
        body,
        mesh=mesh,
        in_specs=(
            P("req", None),
            P("req", None),
            P("req"),
            P("req"),
            P(),
            P("req"),
            P(),
            P(),
            P("req", "exp"),
            P("req", None, "exp"),
            P(None, "exp", "req"),
            P("req", None, None),
            P("req", None, "exp"),
            P("req", None, "exp"),
        ),
        out_specs=P("req", "exp"),
        check_vma=False,
    )
```

```python
import functools

import jax
import jax.numpy as jnp
from jax import lax
from jax.experimental import pallas as pl
from jax.experimental.pallas import tpu as pltpu
from jax.sharding import PartitionSpec as P

HD = 128
NE = 8
TOPK = 2
SIDE = 4
BF = jnp.bfloat16
F32 = jnp.float32
NEG = -1e30
adapter_scale = 0.5

ROW_KV, ROW_UP = 512, 640
SHARD_ROWS = 704
OUT_ROWS = 512
ROW_DN, SENT_ROWS = 64, 96
PLACES = []
for _piece, _off in ((0, 0), (1, -1), (2, 1)):
    for _i, _near in enumerate((0, -1, 1, 2)):
        PLACES.append((_piece, _i, _near, _off))
EARLY = list(PLACES)
LATE = [(0, 0, 0, 2), (0, 1, -1, 2), (1, 0, 1, 2), (1, 1, 2, 2)]
PLACES += [(3 + piece, shard, first, second) for piece, shard, first, second in LATE]


def torus(dx, dz):
    return [
        (i, ((i // SIDE + dx) % SIDE) * SIDE + (i % SIDE + dz) % SIDE) for i in range(SIDE * SIDE)
    ]


def send(value, along, step):
    return lax.ppermute(value, "req", torus(step, 0) if along == 0 else torus(0, step))


def first_step(value, along):
    return send(value, along, 1), send(value, along, -1)


def source(group, half, first, second):
    x, z = group // SIDE, group % SIDE
    dx, dz = (first, second) if half == 0 else (second, first)
    return ((x + dx + SIDE) % SIDE) * SIDE + (z + dz + SIDE) % SIDE


def cost(us):
    return pl.CostEstimate(flops=int(us * 1.15e9), bytes_accessed=2**20, transcendentals=0)


ANY = pl.BlockSpec(memory_space=pl.ANY)
WHOLE = pl.BlockSpec(memory_space=pltpu.VMEM)
SCALARS = pl.BlockSpec(memory_space=pltpu.SMEM)


def pack_kernel(index_ref, store_ref, down_ref, out_ref):
    def one(i, carry):
        out_ref[i, 0:ROW_DN, :] = store_ref[index_ref[i]]
        for side in range(2):
            out_ref[i, ROW_DN:SENT_ROWS, side * 256 : side * 256 + 256] = down_ref[
                side * 32 : side * 32 + 32, :
            ]
        return carry

    lax.fori_loop(0, out_ref.shape[0], one, 0)


def pack(index, store, down):
    return pl.pallas_call(
        pack_kernel,
        out_shape=jax.ShapeDtypeStruct((16, SENT_ROWS, 512), BF),
        in_specs=[SCALARS] + [WHOLE] * 2,
        out_specs=WHOLE,
        cost_estimate=cost(3),
        name="pack",
    )(index, store, down)


def pick_down_kernel(info_ref, recv_ref, out_ref, sem):
    for j in range(4):
        slot = info_ref[1 + j]
        owner, inner = slot // 4, slot % 4
        start = pl.multiple_of(ROW_DN + (inner % 2) * 16, 16)
        for side in range(2):

            @pl.when(inner // 2 == side)
            def _(side=side, j=j, owner=owner, start=start):
                pltpu.make_async_copy(
                    recv_ref.at[owner, pl.ds(start, 16), pl.ds(side * 256, 256)],
                    out_ref.at[j],
                    sem.at[j],
                ).start()

    for j in range(4):
        pltpu.make_async_copy(out_ref.at[j], out_ref.at[j], sem.at[j]).wait()


def pick_down(info, recv):
    return pl.pallas_call(
        pick_down_kernel,
        out_shape=jax.ShapeDtypeStruct((4, 16, 256), BF),
        in_specs=[SCALARS, ANY],
        out_specs=WHOLE,
        scratch_shapes=[pltpu.SemaphoreType.DMA((4,))],
        cost_estimate=cost(2),
        name="pick_down",
    )(info, recv)


def products(group, x_ref, routes_ref, pieces, shards, half):
    count = len(pieces) // 2
    x = jnp.concatenate(
        [
            x_ref[:, pl.ds(pl.multiple_of(source(group, half, first, second) * 128, 128), 128)]
            for _, _, first, second in shards
        ],
        axis=1,
    )

    def product(row):
        weight = jnp.concatenate(
            [
                pieces[half * count + piece][pl.ds(shard * SHARD_ROWS + row, 128), :]
                for piece, shard, _, _ in shards
            ],
            axis=0,
        )
        return jnp.dot(x, weight, preferred_element_type=F32)

    chosen = [jnp.zeros((256, 256), F32)] * TOPK
    for i in range(4):
        value = product(i * 128)
        for k in range(TOPK):
            chosen[k] = jnp.where(routes_ref[:, k : k + 1] == half * 4 + i, value, chosen[k])
    return chosen, product(ROW_KV)


def pick_up(info_ref, pieces, shards, up_ref):
    count = len(pieces) // 2
    for half in range(2):
        for piece, shard, first, second in shards:
            owner = source(info_ref[0], half, first, second)
            for j in range(4):
                slot = info_ref[1 + j]

                @pl.when(slot // 4 == owner)
                def _(half=half, piece=piece, shard=shard, j=j, slot=slot):
                    start = pl.multiple_of(shard * SHARD_ROWS + ROW_UP + slot % 4 * 16, 16)
                    up_ref[j, half] = pieces[half * count + piece][pl.ds(start, 16), :]


def early_kernel(info_ref, routes_ref, x_ref, *refs):
    pieces = refs[:6]
    up_ref, sums_ref = refs[6:]
    group = info_ref[0]
    up_ref[...] = jnp.zeros_like(up_ref)
    pick_up(info_ref, pieces, EARLY, up_ref)

    def block(j, carry):
        rows = pl.ds(pl.multiple_of(j * 256, 256), 256)
        x, routes = x_ref.at[rows, :], routes_ref.at[rows, :]
        first, base = products(group, x, routes, pieces, EARLY, 0)
        sums_ref[j, 2] = base
        second, base = products(group, x, routes, pieces, EARLY, 1)
        sums_ref[j, 3] = base
        for k in range(TOPK):
            sums_ref[j, k] = first[k] + second[k]
        return carry

    lax.fori_loop(0, 4, block, 0)


def project_early(info, routes, x, pieces):
    return pl.pallas_call(
        early_kernel,
        out_shape=(
            jax.ShapeDtypeStruct((4, 2, 16, 256), BF),
            jax.ShapeDtypeStruct((4, 4, 256, 256), F32),
        ),
        in_specs=[SCALARS] + [WHOLE] * 8,
        out_specs=(WHOLE, WHOLE),
        compiler_params=pltpu.CompilerParams(vmem_limit_bytes=20 * 2**20),
        cost_estimate=cost(15),
        name="project_early",
    )(info, routes, x, *pieces)


def attend_kernel(info_ref, routes_ref, down_ref, x_ref, up_ref, sums_ref, recv_hbm, *refs):
    pieces = refs[:4]
    out_ref, sums, up, cache, sem = refs[4:]
    group = info_ref[0]
    for j in range(4):
        pltpu.make_async_copy(
            recv_hbm.at[info_ref[5 + j], pl.ds(0, 64), :], cache.at[j], sem.at[j]
        ).start()
    up[...] = up_ref[...]
    pick_up(info_ref, pieces, LATE, up)

    def attend(j, carry):
        pltpu.make_async_copy(cache.at[j], cache.at[j], sem.at[j]).wait()
        rows = pl.ds(pl.multiple_of(j * 256, 256), 256)
        x, routes = x_ref.at[rows, :], routes_ref.at[rows, :]
        for half in range(2):
            chosen, base = products(group, x, routes, pieces, LATE, half)
            sums[2 + half] = sums_ref[j, 2 + half] + base
            for k in range(TOPK):
                before = sums_ref[j, k] if half == 0 else sums[k]
                sums[k] = before + chosen[k]
        down = jnp.concatenate([down_ref[e, j] for e in range(NE)], axis=1)
        low = lax.dot_general(
            x[...], down, (((1,), (1,)), ((), ())), preferred_element_type=F32
        ).astype(BF)
        cached_length = info_ref[9 + j]
        place = lax.broadcasted_iota(jnp.int32, (256, 320), 1)
        query_at = lax.broadcasted_iota(jnp.int32, (256, 320), 0)
        allowed = (place < cached_length) | ((place >= 64) & (place - 64 <= query_at))
        for h in range(2):
            cols = slice(h * HD, (h + 1) * HD)
            extra = jnp.dot(low, up[j, h], preferred_element_type=F32)
            fresh = (sums[2 + h] + adapter_scale * extra).astype(BF)
            keys = jnp.concatenate(
                [cache[j, :, h * 256 : h * 256 + HD], fresh[:, 0:HD]], axis=0
            )
            values = jnp.concatenate(
                [cache[j, :, h * 256 + HD : h * 256 + 2 * HD], fresh[:, HD : 2 * HD]], axis=0
            )
            attended = []
            for k in range(TOPK):
                scores = lax.dot_general(
                    sums[k, :, cols].astype(BF),
                    keys,
                    (((1,), (1,)), ((), ())),
                    preferred_element_type=F32,
                ) * (HD**-0.5)
                scores = jnp.where(allowed, scores, NEG)
                weights = jnp.exp(scores - jnp.max(scores, axis=-1, keepdims=True))
                total = jnp.sum(weights, axis=-1, keepdims=True)
                probability = (weights * (1.0 / total)).astype(BF)
                attended.append(jnp.dot(probability, values, preferred_element_type=F32))
            for e in range(NE):
                chosen = jnp.where(
                    routes[:, 0:1] == e,
                    attended[0],
                    jnp.where(routes[:, 1:2] == e, attended[1], 0.0),
                )
                out_ref[e, rows, cols] = chosen.astype(BF)
        return carry

    lax.fori_loop(0, 4, attend, 0)


def attention(info, routes, down, x, up, sums, recv, pieces):
    return pl.pallas_call(
        attend_kernel,
        out_shape=jax.ShapeDtypeStruct((NE, 1024, 256), BF),
        in_specs=[SCALARS] + [WHOLE] * 5 + [ANY] + [WHOLE] * 4,
        out_specs=WHOLE,
        scratch_shapes=[
            pltpu.VMEM((4, 256, 256), F32),
            pltpu.VMEM((4, 2, 16, 256), BF),
            pltpu.VMEM((4, 64, 512), BF),
            pltpu.SemaphoreType.DMA((4,)),
        ],
        compiler_params=pltpu.CompilerParams(vmem_limit_bytes=20 * 2**20),
        cost_estimate=cost(22),
        name="attention",
    )(info, routes, down, x, up, sums, recv, *pieces)


def project_out_kernel(blocks, place_ref, gates_ref, lhs_ref, *refs):
    pieces = refs[:10]
    *outs, w, sem = refs[10:]
    group, y, core = place_ref[0], place_ref[1], place_ref[2]
    for b, (mine, ahead) in enumerate(blocks):
        wanted_x = (y + ahead) % 4
        side = core if mine else 1 - core
        for half in range(2):
            for piece, shard, first, second in PLACES:
                owner = source(group, half, first, second)

                @pl.when((owner // 4 == wanted_x) & ((owner % 4) // 2 == side))
                def _(b=b, half=half, piece=piece, shard=shard, owner=owner):
                    pltpu.make_async_copy(
                        pieces[half * 5 + piece].at[pl.ds(shard * OUT_ROWS, OUT_ROWS), :],
                        w.at[b, half, owner % 2],
                        sem.at[b],
                    ).start()

    def block(b, carry):
        pltpu.make_async_copy(w.at[b], w.at[b], sem.at[b]).wait()

        def tile(i, inner):
            rows = pl.ds(pl.multiple_of(i * 256, 256), 256)
            total = None
            for e in range(NE):
                half, pair, lane = e // 4, (e % 4) // 2, e % 2
                place = (pl.ds(pair * 256, 256), pl.ds(lane * 128, 128))
                weight = jnp.concatenate(
                    [w[b, half, 0, place[0], place[1]], w[b, half, 1, place[0], place[1]]], axis=1
                )
                value = jnp.dot(lhs_ref[e, rows, :], weight, preferred_element_type=F32)
                value = value * gates_ref[rows, e : e + 1]
                total = value if total is None else total + value
            total = total.astype(BF)
            if len(outs) == 1:
                outs[0][b, rows, :] = total
            else:
                for at, out_ref in enumerate(outs):

                    @pl.when(b == at)
                    def _(out_ref=out_ref):
                        out_ref[rows, :] = total

            return inner

        return lax.fori_loop(0, 4, tile, carry)

    lax.fori_loop(0, len(blocks), block, 0)


def project_out(blocks, place, gates, lhs, pieces, apart=False):
    if apart:
        shapes = [jax.ShapeDtypeStruct((1024, 256), BF)] * len(blocks)
    else:
        shapes = [jax.ShapeDtypeStruct((len(blocks), 1024, 256), BF)]
    return pl.pallas_call(
        functools.partial(project_out_kernel, blocks),
        out_shape=shapes,
        in_specs=[SCALARS, WHOLE, WHOLE] + [ANY] * 10,
        out_specs=[WHOLE] * len(shapes),
        scratch_shapes=[
            pltpu.VMEM((len(blocks), 2, 2, OUT_ROWS, 256), BF),
            pltpu.SemaphoreType.DMA((len(blocks),)),
        ],
        compiler_params=pltpu.CompilerParams(vmem_limit_bytes=8 * 2**20),
        cost_estimate=cost(2.2 * len(blocks)),
        name="project_out_" + str(len(blocks)),
    )(place, gates, lhs, *pieces)


def small_call(kernel, shapes, us, *operands):
    return pl.pallas_call(
        kernel,
        out_shape=[jax.ShapeDtypeStruct(shape, BF) for shape in shapes],
        in_specs=[WHOLE] * len(operands),
        out_specs=[WHOLE] * len(shapes),
        compiler_params=pltpu.CompilerParams(vmem_limit_bytes=8 * 2**20),
        cost_estimate=cost(us),
        name=kernel.__name__,
    )(*operands)


def forward_kernel(*refs):
    for i in range(4):
        source_ref, out_ref = refs[i], refs[4 + i]
        half = out_ref.shape[0]
        out_ref[...] = source_ref[pl.ds(i % 2 * half, half), :]


def forwarded(values):
    half = values[0].shape[0] // 2
    return small_call(forward_kernel, [(half, 256)] * 4, 2, *values)


def onward(values, along):
    low0, high0, low1, high1 = forwarded(values)
    return [
        send(low0, along, 1),
        send(high0, along, -1),
        send(low1, 1 - along, 1),
        send(high1, 1 - along, -1),
    ]


def far_sum_kernel(mine_ref, theirs_ref, low_ref, high_ref):
    for i, out_ref in enumerate((low_ref, high_ref)):
        rows = pl.ds(i * 512, 512)
        out_ref[...] = (mine_ref[rows, :].astype(F32) + theirs_ref[rows, :].astype(F32)).astype(BF)


def near_sum_kernel(mine_ref, theirs_ref, low_ref, high_ref, ahead_ref, behind_ref):
    for i, out_ref in enumerate((ahead_ref, behind_ref)):
        extra_ref = (low_ref, high_ref)[i]
        for half in range(2):
            rows = pl.ds(half * 512, 512)
            total = mine_ref[i, rows, :].astype(F32) + theirs_ref[i, rows, :].astype(F32)
            if half == i:
                total = total + extra_ref[...].astype(F32)
            out_ref[rows, :] = total.astype(BF)


def exchange(value, step):
    if step == 0:
        return lax.ppermute(value, "exp", [(i, i ^ 1) for i in range(8)])
    return lax.ppermute(value, "exp", [(i, (i + 2 * step) % 8) for i in range(8)])


def rounded_sum(*values):
    total = values[0].astype(F32)
    for value in values[1:]:
        total = total + value.astype(F32)
    return total.astype(BF)


def body(
    tokens,
    routes,
    lengths,
    cached_prefix_length,
    prefix_cache_row,
    adapter_per_request,
    adapter_storage_slot,
    router_weight,
    key_value_weight,
    expert_query_weight,
    expert_output_weight,
    adapter_down_maps,
    adapter_up_maps,
    prefix_cache_store,
):
    group = lax.axis_index("req")
    part = lax.axis_index("exp")
    rows_by_group = prefix_cache_row.reshape(16, 4)
    held = (rows_by_group == group).astype(jnp.int32)
    wanted_by = jnp.sum(held * jnp.arange(4, dtype=jnp.int32)[None, :], axis=1)
    down_rows = (
        lax.dynamic_slice_in_dim(adapter_down_maps, part * 256, 256, 1)
        .transpose(0, 2, 1)
        .reshape(64, 256)
    )
    outgoing = pack(wanted_by, prefix_cache_store, down_rows)
    up_rows = adapter_up_maps.reshape(64, 512)

    query_rows = expert_query_weight.transpose(1, 0, 2).reshape(NE * 128, 256)
    out_rows = (
        expert_output_weight.reshape(4, 2, 256, 128).transpose(0, 2, 1, 3).reshape(1024, 256)
    )
    own = [
        jnp.concatenate(
            [
                query_rows[half * 512 : half * 512 + 512],
                key_value_weight[:, half * 256 : half * 256 + 256],
                up_rows[:, half * 256 : half * 256 + 256],
                out_rows[half * 512 : half * 512 + 512],
            ],
            axis=0,
        )
        for half in range(2)
    ]
    adapter_hot = (
        adapter_per_request[:, None]
        == jnp.arange(adapter_storage_slot.shape[0], dtype=jnp.int32)[None, :]
    ).astype(jnp.int32)
    slots = jnp.sum(adapter_hot * adapter_storage_slot[None, :], axis=1)
    own_rows = lax.dynamic_slice_in_dim(prefix_cache_row, group * 4, 4, 0)
    info = jnp.concatenate([group[None].astype(jnp.int32), slots, own_rows, cached_prefix_length])
    place = jnp.stack([group, lax.div(part, 2), lax.rem(part, 2)]).astype(jnp.int32)
    neighbours = [*first_step(own[0], 0), *first_step(own[1], 1)]
    received = lax.all_to_all(outgoing, "req", 0, 0, tiled=True)
    *neighbours, info, place, _ = lax.optimization_barrier((*neighbours, info, place, outgoing))
    passed = onward(neighbours, 0)
    near, near_out = [], []
    for half in range(2):
        before, after = neighbours[2 * half : 2 * half + 2]
        far_low, far_high = passed[2 * half : 2 * half + 2]
        cut = SHARD_ROWS - far_low.shape[0]
        near.append(
            jnp.concatenate(
                [
                    own[half][:SHARD_ROWS],
                    before[:SHARD_ROWS],
                    after[:SHARD_ROWS],
                    far_low,
                    far_high[:cut],
                ],
                axis=0,
            )
        )
        near_out.append(
            jnp.concatenate(
                [
                    own[half][SHARD_ROWS:],
                    before[SHARD_ROWS:],
                    after[SHARD_ROWS:],
                    far_high[cut:],
                ],
                axis=0,
            )
        )

    logits = jnp.dot(tokens, router_weight, preferred_element_type=F32)
    expert = jnp.arange(NE, dtype=jnp.int32)
    route_hot = (routes[:, :, None] == expert[None, None, :]).astype(F32)
    chosen = jnp.sum(route_hot * logits[:, None, :], axis=-1)
    gate_values = jax.nn.sigmoid(chosen - chosen[:, ::-1])
    live = (jnp.arange(256, dtype=jnp.int32)[None, :] < lengths[:, None]).reshape(1024, 1)
    gates = jnp.sum(route_hot * gate_values[:, :, None], axis=1) * live.astype(F32)

    beside = [*first_step(near[0], 1), *first_step(near[1], 0)]
    down_part = pick_down(info, received)
    down = lax.all_to_all(
        jnp.broadcast_to(down_part[None], (NE, 4, 16, 256)), "exp", 0, 0, tiled=True
    )
    *beside, down, gates = lax.optimization_barrier((*beside, down, gates))
    late = onward(beside, 1)
    up, sums = project_early(info, routes, tokens, [near[0], *beside[:2], near[1], *beside[2:]])
    *late, near_out[0], near_out[1] = lax.optimization_barrier((*late, *near_out))
    out_beside = [*first_step(near_out[0], 1), *first_step(near_out[1], 0)]
    lhs = attention(info, routes, down, tokens, up, sums, received, late)
    *out_beside, lhs = lax.optimization_barrier((*out_beside, lhs))
    out_late = onward(out_beside, 1)
    out_pieces = []
    for half in range(2):
        two = slice(half * 2, half * 2 + 2)
        out_pieces += [near_out[half], *out_beside[two], *out_late[two]]

    operands = (gates, lhs, out_pieces)
    far, far_mine, near_theirs = project_out(
        ((False, 2), (True, 2), (False, 0)), place, *operands, apart=True
    )
    far_swapped = exchange(far, 0)
    place = lax.optimization_barrier((place, far_mine))[0]
    (theirs,) = project_out(((False, 1), (False, 3)), place, *operands)
    swapped = exchange(theirs, 0)
    near_swapped = exchange(near_theirs, 0)
    low, high = small_call(far_sum_kernel, [(512, 256)] * 2, 1, far_mine, far_swapped)
    place = lax.optimization_barrier((place, theirs, low))[0]
    low, high = exchange(low, 1), exchange(high, -1)
    (mine,) = project_out(((True, 1), (True, 3)), place, *operands)
    ahead, behind = small_call(near_sum_kernel, [(1024, 256)] * 2, 2, mine, swapped, low, high)
    from_behind, from_ahead = exchange(ahead, 1), exchange(behind, -1)
    place = lax.optimization_barrier((place, ahead))[0]
    (own_block,) = project_out(((True, 0),), place, *operands)
    return rounded_sum(own_block[0], near_swapped, from_behind, from_ahead)


def solution(mesh):
    return jax.shard_map(
        body,
        mesh=mesh,
        in_specs=(
            P("req", None),
            P("req", None),
            P("req"),
            P("req"),
            P(),
            P("req"),
            P(),
            P(),
            P("req", "exp"),
            P("req", None, "exp"),
            P(None, "exp", "req"),
            P("req", None, None),
            P("req", None, "exp"),
            P("req", None, "exp"),
        ),
        out_specs=P("req", "exp"),
        check_vma=False,
    )
```

```python
import functools

import jax
import jax.numpy as jnp
from jax import lax
from jax.experimental import pallas as pl
from jax.experimental.pallas import tpu as pltpu
from jax.sharding import PartitionSpec as P

HD = 128
NE = 8
TOPK = 2
SIDE = 4
BF = jnp.bfloat16
F32 = jnp.float32
NEG = -1e30
adapter_scale = 0.5

ROW_KV, ROW_UP = 512, 640
SHARD_ROWS = 704
OUT_ROWS = 512
ROW_DN, SENT_ROWS = 64, 96
PLACES = []
for _piece, _off in ((0, 0), (1, -1), (2, 1)):
    for _i, _near in enumerate((0, -1, 1, 2)):
        PLACES.append((_piece, _i, _near, _off))
EARLY = list(PLACES)
LATE = [(0, 0, 0, 2), (0, 1, -1, 2), (1, 0, 1, 2), (1, 1, 2, 2)]
PLACES += [(3 + piece, shard, first, second) for piece, shard, first, second in LATE]


def torus(dx, dz):
    return [
        (i, ((i // SIDE + dx) % SIDE) * SIDE + (i % SIDE + dz) % SIDE) for i in range(SIDE * SIDE)
    ]


def send(value, along, step):
    return lax.ppermute(value, "req", torus(step, 0) if along == 0 else torus(0, step))


def first_step(value, along):
    return send(value, along, 1), send(value, along, -1)


def source(group, half, first, second):
    x, z = group // SIDE, group % SIDE
    dx, dz = (first, second) if half == 0 else (second, first)
    return ((x + dx + SIDE) % SIDE) * SIDE + (z + dz + SIDE) % SIDE


def cost(us):
    return pl.CostEstimate(flops=int(us * 1.15e9), bytes_accessed=2**20, transcendentals=0)


ANY = pl.BlockSpec(memory_space=pl.ANY)
WHOLE = pl.BlockSpec(memory_space=pltpu.VMEM)
SCALARS = pl.BlockSpec(memory_space=pltpu.SMEM)


def pack_kernel(index_ref, store_ref, down_ref, out_ref):
    def one(i, carry):
        out_ref[i, 0:ROW_DN, :] = store_ref[index_ref[i]]
        for side in range(2):
            out_ref[i, ROW_DN:SENT_ROWS, side * 256 : side * 256 + 256] = down_ref[
                side * 32 : side * 32 + 32, :
            ]
        return carry

    lax.fori_loop(0, out_ref.shape[0], one, 0)


def pack(index, store, down):
    return pl.pallas_call(
        pack_kernel,
        out_shape=jax.ShapeDtypeStruct((16, SENT_ROWS, 512), BF),
        in_specs=[SCALARS] + [WHOLE] * 2,
        out_specs=WHOLE,
        cost_estimate=cost(3),
        name="pack",
    )(index, store, down)


def pick_down_kernel(info_ref, recv_ref, out_ref, sem):
    for j in range(4):
        slot = info_ref[1 + j]
        owner, inner = slot // 4, slot % 4
        start = pl.multiple_of(ROW_DN + (inner % 2) * 16, 16)
        for side in range(2):

            @pl.when(inner // 2 == side)
            def _(side=side, j=j, owner=owner, start=start):
                pltpu.make_async_copy(
                    recv_ref.at[owner, pl.ds(start, 16), pl.ds(side * 256, 256)],
                    out_ref.at[j],
                    sem.at[j],
                ).start()

    for j in range(4):
        pltpu.make_async_copy(out_ref.at[j], out_ref.at[j], sem.at[j]).wait()


def pick_down(info, recv):
    return pl.pallas_call(
        pick_down_kernel,
        out_shape=jax.ShapeDtypeStruct((4, 16, 256), BF),
        in_specs=[SCALARS, ANY],
        out_specs=WHOLE,
        scratch_shapes=[pltpu.SemaphoreType.DMA((4,))],
        cost_estimate=cost(2),
        name="pick_down",
    )(info, recv)


def products(group, x_ref, routes_ref, pieces, shards, half):
    count = len(pieces) // 2
    x = jnp.concatenate(
        [
            x_ref[:, pl.ds(pl.multiple_of(source(group, half, first, second) * 128, 128), 128)]
            for _, _, first, second in shards
        ],
        axis=1,
    )

    def product(row):
        weight = jnp.concatenate(
            [
                pieces[half * count + piece][pl.ds(shard * SHARD_ROWS + row, 128), :]
                for piece, shard, _, _ in shards
            ],
            axis=0,
        )
        return jnp.dot(x, weight, preferred_element_type=F32)

    chosen = [jnp.zeros((256, 256), F32)] * TOPK
    for i in range(4):
        value = product(i * 128)
        for k in range(TOPK):
            chosen[k] = jnp.where(routes_ref[:, k : k + 1] == half * 4 + i, value, chosen[k])
    return chosen, product(ROW_KV)


def pick_up(info_ref, pieces, shards, up_ref):
    count = len(pieces) // 2
    for half in range(2):
        for piece, shard, first, second in shards:
            owner = source(info_ref[0], half, first, second)
            for j in range(4):
                slot = info_ref[1 + j]

                @pl.when(slot // 4 == owner)
                def _(half=half, piece=piece, shard=shard, j=j, slot=slot):
                    start = pl.multiple_of(shard * SHARD_ROWS + ROW_UP + slot % 4 * 16, 16)
                    up_ref[j, half] = pieces[half * count + piece][pl.ds(start, 16), :]


def early_kernel(info_ref, routes_ref, x_ref, *refs):
    pieces = refs[:6]
    up_ref, sums_ref = refs[6:]
    group = info_ref[0]
    up_ref[...] = jnp.zeros_like(up_ref)
    pick_up(info_ref, pieces, EARLY, up_ref)

    def block(j, carry):
        rows = pl.ds(pl.multiple_of(j * 256, 256), 256)
        x, routes = x_ref.at[rows, :], routes_ref.at[rows, :]
        first, base = products(group, x, routes, pieces, EARLY, 0)
        sums_ref[j, 2] = base
        second, base = products(group, x, routes, pieces, EARLY, 1)
        sums_ref[j, 3] = base
        for k in range(TOPK):
            sums_ref[j, k] = first[k] + second[k]
        return carry

    lax.fori_loop(0, 4, block, 0)


def project_early(info, routes, x, pieces):
    return pl.pallas_call(
        early_kernel,
        out_shape=(
            jax.ShapeDtypeStruct((4, 2, 16, 256), BF),
            jax.ShapeDtypeStruct((4, 4, 256, 256), F32),
        ),
        in_specs=[SCALARS] + [WHOLE] * 8,
        out_specs=(WHOLE, WHOLE),
        compiler_params=pltpu.CompilerParams(vmem_limit_bytes=20 * 2**20),
        cost_estimate=cost(15),
        name="project_early",
    )(info, routes, x, *pieces)


def attend_kernel(info_ref, routes_ref, down_ref, x_ref, up_ref, sums_ref, recv_hbm, *refs):
    pieces = refs[:4]
    out_ref, sums, up, cache, sem = refs[4:]
    group = info_ref[0]
    for j in range(4):
        pltpu.make_async_copy(
            recv_hbm.at[info_ref[5 + j], pl.ds(0, 64), :], cache.at[j], sem.at[j]
        ).start()
    up[...] = up_ref[...]
    pick_up(info_ref, pieces, LATE, up)

    def attend(j, carry):
        pltpu.make_async_copy(cache.at[j], cache.at[j], sem.at[j]).wait()
        rows = pl.ds(pl.multiple_of(j * 256, 256), 256)
        x, routes = x_ref.at[rows, :], routes_ref.at[rows, :]
        for half in range(2):
            chosen, base = products(group, x, routes, pieces, LATE, half)
            sums[2 + half] = sums_ref[j, 2 + half] + base
            for k in range(TOPK):
                before = sums_ref[j, k] if half == 0 else sums[k]
                sums[k] = before + chosen[k]
        down = jnp.concatenate([down_ref[e, j] for e in range(NE)], axis=1)
        low = lax.dot_general(
            x[...], down, (((1,), (1,)), ((), ())), preferred_element_type=F32
        ).astype(BF)
        cached_length = info_ref[9 + j]
        place = lax.broadcasted_iota(jnp.int32, (256, 320), 1)
        query_at = lax.broadcasted_iota(jnp.int32, (256, 320), 0)
        allowed = (place < cached_length) | ((place >= 64) & (place - 64 <= query_at))
        for h in range(2):
            cols = slice(h * HD, (h + 1) * HD)
            extra = jnp.dot(low, up[j, h], preferred_element_type=F32)
            fresh = (sums[2 + h] + adapter_scale * extra).astype(BF)
            keys = jnp.concatenate(
                [cache[j, :, h * 256 : h * 256 + HD], fresh[:, 0:HD]], axis=0
            )
            values = jnp.concatenate(
                [cache[j, :, h * 256 + HD : h * 256 + 2 * HD], fresh[:, HD : 2 * HD]], axis=0
            )
            attended = []
            for k in range(TOPK):
                scores = lax.dot_general(
                    sums[k, :, cols].astype(BF),
                    keys,
                    (((1,), (1,)), ((), ())),
                    preferred_element_type=F32,
                ) * (HD**-0.5)
                scores = jnp.where(allowed, scores, NEG)
                weights = jnp.exp(scores - jnp.max(scores, axis=-1, keepdims=True))
                total = jnp.sum(weights, axis=-1, keepdims=True)
                probability = (weights * (1.0 / total)).astype(BF)
                attended.append(jnp.dot(probability, values, preferred_element_type=F32))
            for e in range(NE):
                chosen = jnp.where(
                    routes[:, 0:1] == e,
                    attended[0],
                    jnp.where(routes[:, 1:2] == e, attended[1], 0.0),
                )
                out_ref[e, rows, cols] = chosen.astype(BF)
        return carry

    lax.fori_loop(0, 4, attend, 0)


def attention(info, routes, down, x, up, sums, recv, pieces):
    return pl.pallas_call(
        attend_kernel,
        out_shape=jax.ShapeDtypeStruct((NE, 1024, 256), BF),
        in_specs=[SCALARS] + [WHOLE] * 5 + [ANY] + [WHOLE] * 4,
        out_specs=WHOLE,
        scratch_shapes=[
            pltpu.VMEM((4, 256, 256), F32),
            pltpu.VMEM((4, 2, 16, 256), BF),
            pltpu.VMEM((4, 64, 512), BF),
            pltpu.SemaphoreType.DMA((4,)),
        ],
        compiler_params=pltpu.CompilerParams(vmem_limit_bytes=20 * 2**20),
        cost_estimate=cost(22),
        name="attention",
    )(info, routes, down, x, up, sums, recv, *pieces)


def project_out_kernel(blocks, place_ref, gates_ref, lhs_ref, *refs):
    pieces = refs[:10]
    *outs, w, sem = refs[10:]
    group, y, core = place_ref[0], place_ref[1], place_ref[2]
    for b, (mine, ahead) in enumerate(blocks):
        wanted_x = (y + ahead) % 4
        side = core if mine else 1 - core
        for half in range(2):
            for piece, shard, first, second in PLACES:
                owner = source(group, half, first, second)

                @pl.when((owner // 4 == wanted_x) & ((owner % 4) // 2 == side))
                def _(b=b, half=half, piece=piece, shard=shard, owner=owner):
                    pltpu.make_async_copy(
                        pieces[half * 5 + piece].at[pl.ds(shard * OUT_ROWS, OUT_ROWS), :],
                        w.at[b, half, owner % 2],
                        sem.at[b],
                    ).start()

    def block(b, carry):
        pltpu.make_async_copy(w.at[b], w.at[b], sem.at[b]).wait()

        def tile(i, inner):
            rows = pl.ds(pl.multiple_of(i * 256, 256), 256)
            total = None
            for e in range(NE):
                half, pair, lane = e // 4, (e % 4) // 2, e % 2
                place = (pl.ds(pair * 256, 256), pl.ds(lane * 128, 128))
                weight = jnp.concatenate(
                    [w[b, half, 0, place[0], place[1]], w[b, half, 1, place[0], place[1]]], axis=1
                )
                value = jnp.dot(lhs_ref[e, rows, :], weight, preferred_element_type=F32)
                value = value * gates_ref[rows, e : e + 1]
                total = value if total is None else total + value
            total = total.astype(BF)
            if len(outs) == 1:
                outs[0][b, rows, :] = total
            else:
                for at, out_ref in enumerate(outs):

                    @pl.when(b == at)
                    def _(out_ref=out_ref):
                        out_ref[rows, :] = total

            return inner

        return lax.fori_loop(0, 4, tile, carry)

    lax.fori_loop(0, len(blocks), block, 0)


def project_out(blocks, place, gates, lhs, pieces, apart=False):
    if apart:
        shapes = [jax.ShapeDtypeStruct((1024, 256), BF)] * len(blocks)
    else:
        shapes = [jax.ShapeDtypeStruct((len(blocks), 1024, 256), BF)]
    return pl.pallas_call(
        functools.partial(project_out_kernel, blocks),
        out_shape=shapes,
        in_specs=[SCALARS, WHOLE, WHOLE] + [ANY] * 10,
        out_specs=[WHOLE] * len(shapes),
        scratch_shapes=[
            pltpu.VMEM((len(blocks), 2, 2, OUT_ROWS, 256), BF),
            pltpu.SemaphoreType.DMA((len(blocks),)),
        ],
        compiler_params=pltpu.CompilerParams(vmem_limit_bytes=8 * 2**20),
        cost_estimate=cost(2.2 * len(blocks)),
        name="project_out_" + str(len(blocks)),
    )(place, gates, lhs, *pieces)


def small_call(kernel, shapes, us, *operands):
    return pl.pallas_call(
        kernel,
        out_shape=[jax.ShapeDtypeStruct(shape, BF) for shape in shapes],
        in_specs=[WHOLE] * len(operands),
        out_specs=[WHOLE] * len(shapes),
        compiler_params=pltpu.CompilerParams(vmem_limit_bytes=8 * 2**20),
        cost_estimate=cost(us),
        name=kernel.__name__,
    )(*operands)


def forward_kernel(*refs):
    half = refs[4].shape[0]
    steps = 8 if half % 128 == 0 else 2
    chunk = half // steps

    def copy(step, carry):
        start = pl.multiple_of(step * chunk, chunk)
        for i in range(4):
            refs[4 + i][pl.ds(start, chunk), :] = refs[i][pl.ds(i % 2 * half + start, chunk), :]
        return carry

    lax.fori_loop(0, steps, copy, 0)


def forwarded(values):
    half = values[0].shape[0] // 2
    return small_call(forward_kernel, [(half, 256)] * 4, 2, *values)


def onward(values, along):
    low0, high0, low1, high1 = forwarded(values)
    return [
        send(low0, along, 1),
        send(high0, along, -1),
        send(low1, 1 - along, 1),
        send(high1, 1 - along, -1),
    ]


def far_sum_kernel(mine_ref, theirs_ref, low_ref, high_ref):
    for i, out_ref in enumerate((low_ref, high_ref)):
        rows = pl.ds(i * 512, 512)
        out_ref[...] = (mine_ref[rows, :].astype(F32) + theirs_ref[rows, :].astype(F32)).astype(BF)


def near_sum_kernel(mine_ref, theirs_ref, low_ref, high_ref, ahead_ref, behind_ref):
    for i, out_ref in enumerate((ahead_ref, behind_ref)):
        extra_ref = (low_ref, high_ref)[i]
        for half in range(2):
            rows = pl.ds(half * 512, 512)
            total = mine_ref[i, rows, :].astype(F32) + theirs_ref[i, rows, :].astype(F32)
            if half == i:
                total = total + extra_ref[...].astype(F32)
            out_ref[rows, :] = total.astype(BF)


def exchange(value, step):
    if step == 0:
        return lax.ppermute(value, "exp", [(i, i ^ 1) for i in range(8)])
    return lax.ppermute(value, "exp", [(i, (i + 2 * step) % 8) for i in range(8)])


def rounded_sum(*values):
    total = values[0].astype(F32)
    for value in values[1:]:
        total = total + value.astype(F32)
    return total.astype(BF)


def body(
    tokens,
    routes,
    lengths,
    cached_prefix_length,
    prefix_cache_row,
    adapter_per_request,
    adapter_storage_slot,
    router_weight,
    key_value_weight,
    expert_query_weight,
    expert_output_weight,
    adapter_down_maps,
    adapter_up_maps,
    prefix_cache_store,
):
    group = lax.axis_index("req")
    part = lax.axis_index("exp")
    rows_by_group = prefix_cache_row.reshape(16, 4)
    held = (rows_by_group == group).astype(jnp.int32)
    wanted_by = jnp.sum(held * jnp.arange(4, dtype=jnp.int32)[None, :], axis=1)
    down_rows = (
        lax.dynamic_slice_in_dim(adapter_down_maps, part * 256, 256, 1)
        .transpose(0, 2, 1)
        .reshape(64, 256)
    )
    outgoing = pack(wanted_by, prefix_cache_store, down_rows)
    up_rows = adapter_up_maps.reshape(64, 512)

    query_rows = expert_query_weight.transpose(1, 0, 2).reshape(NE * 128, 256)
    out_rows = (
        expert_output_weight.reshape(4, 2, 256, 128).transpose(0, 2, 1, 3).reshape(1024, 256)
    )
    own = [
        jnp.concatenate(
            [
                query_rows[half * 512 : half * 512 + 512],
                key_value_weight[:, half * 256 : half * 256 + 256],
                up_rows[:, half * 256 : half * 256 + 256],
                out_rows[half * 512 : half * 512 + 512],
            ],
            axis=0,
        )
        for half in range(2)
    ]
    adapter_hot = (
        adapter_per_request[:, None]
        == jnp.arange(adapter_storage_slot.shape[0], dtype=jnp.int32)[None, :]
    ).astype(jnp.int32)
    slots = jnp.sum(adapter_hot * adapter_storage_slot[None, :], axis=1)
    own_rows = lax.dynamic_slice_in_dim(prefix_cache_row, group * 4, 4, 0)
    info = jnp.concatenate([group[None].astype(jnp.int32), slots, own_rows, cached_prefix_length])
    place = jnp.stack([group, lax.div(part, 2), lax.rem(part, 2)]).astype(jnp.int32)
    neighbours = [*first_step(own[0], 0), *first_step(own[1], 1)]
    received = lax.all_to_all(outgoing, "req", 0, 0, tiled=True)
    *neighbours, info, place, _ = lax.optimization_barrier((*neighbours, info, place, outgoing))
    passed = onward(neighbours, 0)
    near, near_out = [], []
    for half in range(2):
        before, after = neighbours[2 * half : 2 * half + 2]
        far_low, far_high = passed[2 * half : 2 * half + 2]
        cut = SHARD_ROWS - far_low.shape[0]
        near.append(
            jnp.concatenate(
                [
                    own[half][:SHARD_ROWS],
                    before[:SHARD_ROWS],
                    after[:SHARD_ROWS],
                    far_low,
                    far_high[:cut],
                ],
                axis=0,
            )
        )
        near_out.append(
            jnp.concatenate(
                [
                    own[half][SHARD_ROWS:],
                    before[SHARD_ROWS:],
                    after[SHARD_ROWS:],
                    far_high[cut:],
                ],
                axis=0,
            )
        )

    logits = jnp.dot(tokens, router_weight, preferred_element_type=F32)
    expert = jnp.arange(NE, dtype=jnp.int32)
    route_hot = (routes[:, :, None] == expert[None, None, :]).astype(F32)
    chosen = jnp.sum(route_hot * logits[:, None, :], axis=-1)
    gate_values = jax.nn.sigmoid(chosen - chosen[:, ::-1])
    live = (jnp.arange(256, dtype=jnp.int32)[None, :] < lengths[:, None]).reshape(1024, 1)
    gates = jnp.sum(route_hot * gate_values[:, :, None], axis=1) * live.astype(F32)

    beside = [*first_step(near[0], 1), *first_step(near[1], 0)]
    down_part = pick_down(info, received)
    down = lax.all_to_all(
        jnp.broadcast_to(down_part[None], (NE, 4, 16, 256)), "exp", 0, 0, tiled=True
    )
    *beside, down, gates = lax.optimization_barrier((*beside, down, gates))
    late = onward(beside, 1)
    up, sums = project_early(info, routes, tokens, [near[0], *beside[:2], near[1], *beside[2:]])
    *late, near_out[0], near_out[1] = lax.optimization_barrier((*late, *near_out))
    out_beside = [*first_step(near_out[0], 1), *first_step(near_out[1], 0)]
    lhs = attention(info, routes, down, tokens, up, sums, received, late)
    *out_beside, lhs = lax.optimization_barrier((*out_beside, lhs))
    out_late = onward(out_beside, 1)
    out_pieces = []
    for half in range(2):
        two = slice(half * 2, half * 2 + 2)
        out_pieces += [near_out[half], *out_beside[two], *out_late[two]]

    operands = (gates, lhs, out_pieces)
    far, far_mine, near_theirs = project_out(
        ((False, 2), (True, 2), (False, 0)), place, *operands, apart=True
    )
    far_swapped = exchange(far, 0)
    place = lax.optimization_barrier((place, far_mine))[0]
    (theirs,) = project_out(((False, 1), (False, 3)), place, *operands)
    swapped = exchange(theirs, 0)
    near_swapped = exchange(near_theirs, 0)
    low, high = small_call(far_sum_kernel, [(512, 256)] * 2, 1, far_mine, far_swapped)
    place = lax.optimization_barrier((place, theirs, low))[0]
    low, high = exchange(low, 1), exchange(high, -1)
    (mine,) = project_out(((True, 1), (True, 3)), place, *operands)
    ahead, behind = small_call(near_sum_kernel, [(1024, 256)] * 2, 2, mine, swapped, low, high)
    from_behind, from_ahead = exchange(ahead, 1), exchange(behind, -1)
    place = lax.optimization_barrier((place, ahead))[0]
    (own_block,) = project_out(((True, 0),), place, *operands)
    return rounded_sum(own_block[0], near_swapped, from_behind, from_ahead)


def solution(mesh):
    return jax.shard_map(
        body,
        mesh=mesh,
        in_specs=(
            P("req", None),
            P("req", None),
            P("req"),
            P("req"),
            P(),
            P("req"),
            P(),
            P(),
            P("req", "exp"),
            P("req", None, "exp"),
            P(None, "exp", "req"),
            P("req", None, None),
            P("req", None, "exp"),
            P("req", None, "exp"),
        ),
        out_specs=P("req", "exp"),
        check_vma=False,
    )
```

```python
import functools

import jax
import jax.numpy as jnp
from jax import lax
from jax.experimental import pallas as pl
from jax.experimental.pallas import tpu as pltpu
from jax.sharding import PartitionSpec as P

HD = 128
NE = 8
TOPK = 2
SIDE = 4
BF = jnp.bfloat16
F32 = jnp.float32
NEG = -1e30
adapter_scale = 0.5

ROW_KV, ROW_UP = 512, 640
SHARD_ROWS = 704
OUT_ROWS = 512
ROW_DN, SENT_ROWS = 64, 96
PLACES = []
for _piece, _off in ((0, 0), (1, -1), (2, 1)):
    for _i, _near in enumerate((0, -1, 1, 2)):
        PLACES.append((_piece, _i, _near, _off))
EARLY = list(PLACES)
LATE = [(0, 0, 0, 2), (0, 1, -1, 2), (1, 0, 1, 2), (1, 1, 2, 2)]
PLACES += [(3 + piece, shard, first, second) for piece, shard, first, second in LATE]


def torus(dx, dz):
    return [
        (i, ((i // SIDE + dx) % SIDE) * SIDE + (i % SIDE + dz) % SIDE) for i in range(SIDE * SIDE)
    ]


def send(value, along, step):
    return lax.ppermute(value, "req", torus(step, 0) if along == 0 else torus(0, step))


def first_step(value, along):
    return send(value, along, 1), send(value, along, -1)


def source(group, half, first, second):
    x, z = group // SIDE, group % SIDE
    dx, dz = (first, second) if half == 0 else (second, first)
    return ((x + dx + SIDE) % SIDE) * SIDE + (z + dz + SIDE) % SIDE


def cost(us):
    return pl.CostEstimate(flops=int(us * 1.15e9), bytes_accessed=2**20, transcendentals=0)


ANY = pl.BlockSpec(memory_space=pl.ANY)
WHOLE = pl.BlockSpec(memory_space=pltpu.VMEM)
SCALARS = pl.BlockSpec(memory_space=pltpu.SMEM)


def pack_kernel(index_ref, store_ref, down_ref, out_ref):
    def one(i, carry):
        out_ref[i, 0:ROW_DN, :] = store_ref[index_ref[i]]
        for side in range(2):
            out_ref[i, ROW_DN:SENT_ROWS, side * 256 : side * 256 + 256] = down_ref[
                side * 32 : side * 32 + 32, :
            ]
        return carry

    lax.fori_loop(0, out_ref.shape[0], one, 0)


def pack(index, store, down):
    return pl.pallas_call(
        pack_kernel,
        out_shape=jax.ShapeDtypeStruct((16, SENT_ROWS, 512), BF),
        in_specs=[SCALARS] + [WHOLE] * 2,
        out_specs=WHOLE,
        cost_estimate=cost(3),
        name="pack",
    )(index, store, down)


def pick_down_kernel(info_ref, recv_ref, out_ref, sem):
    for j in range(4):
        slot = info_ref[1 + j]
        owner, inner = slot // 4, slot % 4
        start = pl.multiple_of(ROW_DN + (inner % 2) * 16, 16)
        for side in range(2):

            @pl.when(inner // 2 == side)
            def _(side=side, j=j, owner=owner, start=start):
                pltpu.make_async_copy(
                    recv_ref.at[owner, pl.ds(start, 16), pl.ds(side * 256, 256)],
                    out_ref.at[j],
                    sem.at[j],
                ).start()

    for j in range(4):
        pltpu.make_async_copy(out_ref.at[j], out_ref.at[j], sem.at[j]).wait()


def pick_down(info, recv):
    return pl.pallas_call(
        pick_down_kernel,
        out_shape=jax.ShapeDtypeStruct((4, 16, 256), BF),
        in_specs=[SCALARS, ANY],
        out_specs=WHOLE,
        scratch_shapes=[pltpu.SemaphoreType.DMA((4,))],
        cost_estimate=cost(2),
        name="pick_down",
    )(info, recv)


def products(group, x_ref, routes_ref, pieces, shards, half):
    count = len(pieces) // 2
    x = jnp.concatenate(
        [
            x_ref[:, pl.ds(pl.multiple_of(source(group, half, first, second) * 128, 128), 128)]
            for _, _, first, second in shards
        ],
        axis=1,
    )

    def product(row):
        weight = jnp.concatenate(
            [
                pieces[half * count + piece][pl.ds(shard * SHARD_ROWS + row, 128), :]
                for piece, shard, _, _ in shards
            ],
            axis=0,
        )
        return jnp.dot(x, weight, preferred_element_type=F32)

    chosen = [jnp.zeros((256, 256), F32)] * TOPK
    for i in range(4):
        value = product(i * 128)
        for k in range(TOPK):
            chosen[k] = jnp.where(routes_ref[:, k : k + 1] == half * 4 + i, value, chosen[k])
    return chosen, product(ROW_KV)


def pick_up(info_ref, pieces, shards, up_ref):
    count = len(pieces) // 2
    for half in range(2):
        for piece, shard, first, second in shards:
            owner = source(info_ref[0], half, first, second)
            for j in range(4):
                slot = info_ref[1 + j]

                @pl.when(slot // 4 == owner)
                def _(half=half, piece=piece, shard=shard, j=j, slot=slot):
                    start = pl.multiple_of(shard * SHARD_ROWS + ROW_UP + slot % 4 * 16, 16)
                    up_ref[j, half] = pieces[half * count + piece][pl.ds(start, 16), :]


def early_kernel(info_ref, routes_ref, x_ref, *refs):
    pieces = refs[:6]
    up_ref, sums_ref = refs[6:]
    group = info_ref[0]
    up_ref[...] = jnp.zeros_like(up_ref)
    pick_up(info_ref, pieces, EARLY, up_ref)

    def block(j, carry):
        rows = pl.ds(pl.multiple_of(j * 256, 256), 256)
        x, routes = x_ref.at[rows, :], routes_ref.at[rows, :]
        first, base = products(group, x, routes, pieces, EARLY, 0)
        sums_ref[j, 2] = base
        second, base = products(group, x, routes, pieces, EARLY, 1)
        sums_ref[j, 3] = base
        for k in range(TOPK):
            sums_ref[j, k] = first[k] + second[k]
        return carry

    lax.fori_loop(0, 4, block, 0)


def project_early(info, routes, x, pieces):
    return pl.pallas_call(
        early_kernel,
        out_shape=(
            jax.ShapeDtypeStruct((4, 2, 16, 256), BF),
            jax.ShapeDtypeStruct((4, 4, 256, 256), F32),
        ),
        in_specs=[SCALARS] + [WHOLE] * 8,
        out_specs=(WHOLE, WHOLE),
        compiler_params=pltpu.CompilerParams(vmem_limit_bytes=20 * 2**20),
        cost_estimate=cost(15),
        name="project_early",
    )(info, routes, x, *pieces)


def attend_kernel(info_ref, routes_ref, down_ref, x_ref, up_ref, sums_ref, recv_hbm, *refs):
    pieces = refs[:4]
    out_ref, sums, up, cache, sem = refs[4:]
    group = info_ref[0]
    for j in range(4):
        pltpu.make_async_copy(
            recv_hbm.at[info_ref[5 + j], pl.ds(0, 64), :], cache.at[j], sem.at[j]
        ).start()
    up[...] = up_ref[...]
    pick_up(info_ref, pieces, LATE, up)

    def attend(j, carry):
        pltpu.make_async_copy(cache.at[j], cache.at[j], sem.at[j]).wait()
        rows = pl.ds(pl.multiple_of(j * 256, 256), 256)
        x, routes = x_ref.at[rows, :], routes_ref.at[rows, :]
        for half in range(2):
            chosen, base = products(group, x, routes, pieces, LATE, half)
            sums[2 + half] = sums_ref[j, 2 + half] + base
            for k in range(TOPK):
                before = sums_ref[j, k] if half == 0 else sums[k]
                sums[k] = before + chosen[k]
        down = jnp.concatenate([down_ref[e, j] for e in range(NE)], axis=1)
        low = lax.dot_general(
            x[...], down, (((1,), (1,)), ((), ())), preferred_element_type=F32
        ).astype(BF)
        cached_length = info_ref[9 + j]
        place = lax.broadcasted_iota(jnp.int32, (256, 320), 1)
        query_at = lax.broadcasted_iota(jnp.int32, (256, 320), 0)
        allowed = (place < cached_length) | ((place >= 64) & (place - 64 <= query_at))
        for h in range(2):
            cols = slice(h * HD, (h + 1) * HD)
            extra = jnp.dot(low, up[j, h], preferred_element_type=F32)
            fresh = (sums[2 + h] + adapter_scale * extra).astype(BF)
            keys = jnp.concatenate(
                [cache[j, :, h * 256 : h * 256 + HD], fresh[:, 0:HD]], axis=0
            )
            values = jnp.concatenate(
                [cache[j, :, h * 256 + HD : h * 256 + 2 * HD], fresh[:, HD : 2 * HD]], axis=0
            )
            attended = []
            for k in range(TOPK):
                scores = lax.dot_general(
                    sums[k, :, cols].astype(BF),
                    keys,
                    (((1,), (1,)), ((), ())),
                    preferred_element_type=F32,
                ) * (HD**-0.5)
                scores = jnp.where(allowed, scores, NEG)
                weights = jnp.exp(scores - jnp.max(scores, axis=-1, keepdims=True))
                total = jnp.sum(weights, axis=-1, keepdims=True)
                probability = (weights * (1.0 / total)).astype(BF)
                attended.append(jnp.dot(probability, values, preferred_element_type=F32))
            for e in range(NE):
                chosen = jnp.where(
                    routes[:, 0:1] == e,
                    attended[0],
                    jnp.where(routes[:, 1:2] == e, attended[1], 0.0),
                )
                out_ref[e, rows, cols] = chosen.astype(BF)
        return carry

    lax.fori_loop(0, 4, attend, 0)


def attention(info, routes, down, x, up, sums, recv, pieces):
    return pl.pallas_call(
        attend_kernel,
        out_shape=jax.ShapeDtypeStruct((NE, 1024, 256), BF),
        in_specs=[SCALARS] + [WHOLE] * 5 + [ANY] + [WHOLE] * 4,
        out_specs=WHOLE,
        scratch_shapes=[
            pltpu.VMEM((4, 256, 256), F32),
            pltpu.VMEM((4, 2, 16, 256), BF),
            pltpu.VMEM((4, 64, 512), BF),
            pltpu.SemaphoreType.DMA((4,)),
        ],
        compiler_params=pltpu.CompilerParams(vmem_limit_bytes=20 * 2**20),
        cost_estimate=cost(22),
        name="attention",
    )(info, routes, down, x, up, sums, recv, *pieces)


def project_out_kernel(blocks, place_ref, gates_ref, lhs_ref, *refs):
    pieces = refs[:10]
    *outs, w, sem = refs[10:]
    group, y, core = place_ref[0], place_ref[1], place_ref[2]
    for b, (mine, ahead) in enumerate(blocks):
        wanted_x = (y + ahead) % 4
        side = core if mine else 1 - core
        for half in range(2):
            for piece, shard, first, second in PLACES:
                owner = source(group, half, first, second)

                @pl.when((owner // 4 == wanted_x) & ((owner % 4) // 2 == side))
                def _(b=b, half=half, piece=piece, shard=shard, owner=owner):
                    pltpu.make_async_copy(
                        pieces[half * 5 + piece].at[pl.ds(shard * OUT_ROWS, OUT_ROWS), :],
                        w.at[b, half, owner % 2],
                        sem.at[b],
                    ).start()

    def block(b, carry):
        pltpu.make_async_copy(w.at[b], w.at[b], sem.at[b]).wait()

        def tile(i, inner):
            rows = pl.ds(pl.multiple_of(i * 256, 256), 256)
            total = None
            for e in range(NE):
                half, pair, lane = e // 4, (e % 4) // 2, e % 2
                place = (pl.ds(pair * 256, 256), pl.ds(lane * 128, 128))
                weight = jnp.concatenate(
                    [w[b, half, 0, place[0], place[1]], w[b, half, 1, place[0], place[1]]], axis=1
                )
                value = jnp.dot(lhs_ref[e, rows, :], weight, preferred_element_type=F32)
                value = value * gates_ref[rows, e : e + 1]
                total = value if total is None else total + value
            total = total.astype(BF)
            if len(outs) == 1:
                outs[0][b, rows, :] = total
            else:
                for at, out_ref in enumerate(outs):

                    @pl.when(b == at)
                    def _(out_ref=out_ref):
                        out_ref[rows, :] = total

            return inner

        return lax.fori_loop(0, 4, tile, carry)

    lax.fori_loop(0, len(blocks), block, 0)


def project_out(blocks, place, gates, lhs, pieces, apart=False):
    if apart:
        shapes = [jax.ShapeDtypeStruct((1024, 256), BF)] * len(blocks)
    else:
        shapes = [jax.ShapeDtypeStruct((len(blocks), 1024, 256), BF)]
    return pl.pallas_call(
        functools.partial(project_out_kernel, blocks),
        out_shape=shapes,
        in_specs=[SCALARS, WHOLE, WHOLE] + [ANY] * 10,
        out_specs=[WHOLE] * len(shapes),
        scratch_shapes=[
            pltpu.VMEM((len(blocks), 2, 2, OUT_ROWS, 256), BF),
            pltpu.SemaphoreType.DMA((len(blocks),)),
        ],
        compiler_params=pltpu.CompilerParams(vmem_limit_bytes=8 * 2**20),
        cost_estimate=cost(2.2 * len(blocks)),
        name="project_out_" + str(len(blocks)),
    )(place, gates, lhs, *pieces)


def small_call(kernel, shapes, us, *operands):
    return pl.pallas_call(
        kernel,
        out_shape=[jax.ShapeDtypeStruct(shape, BF) for shape in shapes],
        in_specs=[WHOLE] * len(operands),
        out_specs=[WHOLE] * len(shapes),
        compiler_params=pltpu.CompilerParams(vmem_limit_bytes=8 * 2**20),
        cost_estimate=cost(us),
        name=kernel.__name__,
    )(*operands)


def forward_kernel(*refs):
    half = refs[4].shape[0]
    if half > 1024:

        def together(sem):
            copies = [
                pltpu.make_async_copy(
                    refs[i].at[pl.ds(i % 2 * half, half), :], refs[4 + i], sem.at[i]
                )
                for i in range(4)
            ]
            for one in copies:
                one.start()
            for one in copies:
                one.wait()

        pl.run_scoped(together, pltpu.SemaphoreType.DMA((4,)))
        return
    steps = 8 if half % 128 == 0 else 2
    chunk = half // steps

    def copy(step, carry):
        start = pl.multiple_of(step * chunk, chunk)
        for i in range(4):
            refs[4 + i][pl.ds(start, chunk), :] = refs[i][pl.ds(i % 2 * half + start, chunk), :]
        return carry

    lax.fori_loop(0, steps, copy, 0)


def forwarded(values):
    half = values[0].shape[0] // 2
    return small_call(forward_kernel, [(half, 256)] * 4, 2, *values)


def onward(values, along):
    low0, high0, low1, high1 = forwarded(values)
    return [
        send(low0, along, 1),
        send(high0, along, -1),
        send(low1, 1 - along, 1),
        send(high1, 1 - along, -1),
    ]


def far_sum_kernel(mine_ref, theirs_ref, low_ref, high_ref):
    for i, out_ref in enumerate((low_ref, high_ref)):
        rows = pl.ds(i * 512, 512)
        out_ref[...] = (mine_ref[rows, :].astype(F32) + theirs_ref[rows, :].astype(F32)).astype(BF)


def near_sum_kernel(mine_ref, theirs_ref, low_ref, high_ref, ahead_ref, behind_ref):
    for i, out_ref in enumerate((ahead_ref, behind_ref)):
        extra_ref = (low_ref, high_ref)[i]
        for half in range(2):
            rows = pl.ds(half * 512, 512)
            total = mine_ref[i, rows, :].astype(F32) + theirs_ref[i, rows, :].astype(F32)
            if half == i:
                total = total + extra_ref[...].astype(F32)
            out_ref[rows, :] = total.astype(BF)


def exchange(value, step):
    if step == 0:
        return lax.ppermute(value, "exp", [(i, i ^ 1) for i in range(8)])
    return lax.ppermute(value, "exp", [(i, (i + 2 * step) % 8) for i in range(8)])


def rounded_sum(*values):
    total = values[0].astype(F32)
    for value in values[1:]:
        total = total + value.astype(F32)
    return total.astype(BF)


def body(
    tokens,
    routes,
    lengths,
    cached_prefix_length,
    prefix_cache_row,
    adapter_per_request,
    adapter_storage_slot,
    router_weight,
    key_value_weight,
    expert_query_weight,
    expert_output_weight,
    adapter_down_maps,
    adapter_up_maps,
    prefix_cache_store,
):
    group = lax.axis_index("req")
    part = lax.axis_index("exp")
    rows_by_group = prefix_cache_row.reshape(16, 4)
    held = (rows_by_group == group).astype(jnp.int32)
    wanted_by = jnp.sum(held * jnp.arange(4, dtype=jnp.int32)[None, :], axis=1)
    down_rows = (
        lax.dynamic_slice_in_dim(adapter_down_maps, part * 256, 256, 1)
        .transpose(0, 2, 1)
        .reshape(64, 256)
    )
    outgoing = pack(wanted_by, prefix_cache_store, down_rows)
    up_rows = adapter_up_maps.reshape(64, 512)

    query_rows = expert_query_weight.transpose(1, 0, 2).reshape(NE * 128, 256)
    out_rows = (
        expert_output_weight.reshape(4, 2, 256, 128).transpose(0, 2, 1, 3).reshape(1024, 256)
    )
    own = [
        jnp.concatenate(
            [
                query_rows[half * 512 : half * 512 + 512],
                key_value_weight[:, half * 256 : half * 256 + 256],
                up_rows[:, half * 256 : half * 256 + 256],
                out_rows[half * 512 : half * 512 + 512],
            ],
            axis=0,
        )
        for half in range(2)
    ]
    adapter_hot = (
        adapter_per_request[:, None]
        == jnp.arange(adapter_storage_slot.shape[0], dtype=jnp.int32)[None, :]
    ).astype(jnp.int32)
    slots = jnp.sum(adapter_hot * adapter_storage_slot[None, :], axis=1)
    own_rows = lax.dynamic_slice_in_dim(prefix_cache_row, group * 4, 4, 0)
    info = jnp.concatenate([group[None].astype(jnp.int32), slots, own_rows, cached_prefix_length])
    place = jnp.stack([group, lax.div(part, 2), lax.rem(part, 2)]).astype(jnp.int32)
    neighbours = [*first_step(own[0], 0), *first_step(own[1], 1)]
    received = lax.all_to_all(outgoing, "req", 0, 0, tiled=True)
    *neighbours, info, place, _ = lax.optimization_barrier((*neighbours, info, place, outgoing))
    passed = onward(neighbours, 0)
    near, near_out = [], []
    for half in range(2):
        before, after = neighbours[2 * half : 2 * half + 2]
        far_low, far_high = passed[2 * half : 2 * half + 2]
        cut = SHARD_ROWS - far_low.shape[0]
        near.append(
            jnp.concatenate(
                [
                    own[half][:SHARD_ROWS],
                    before[:SHARD_ROWS],
                    after[:SHARD_ROWS],
                    far_low,
                    far_high[:cut],
                ],
                axis=0,
            )
        )
        near_out.append(
            jnp.concatenate(
                [
                    own[half][SHARD_ROWS:],
                    before[SHARD_ROWS:],
                    after[SHARD_ROWS:],
                    far_high[cut:],
                ],
                axis=0,
            )
        )

    logits = jnp.dot(tokens, router_weight, preferred_element_type=F32)
    expert = jnp.arange(NE, dtype=jnp.int32)
    route_hot = (routes[:, :, None] == expert[None, None, :]).astype(F32)
    chosen = jnp.sum(route_hot * logits[:, None, :], axis=-1)
    gate_values = jax.nn.sigmoid(chosen - chosen[:, ::-1])
    live = (jnp.arange(256, dtype=jnp.int32)[None, :] < lengths[:, None]).reshape(1024, 1)
    gates = jnp.sum(route_hot * gate_values[:, :, None], axis=1) * live.astype(F32)

    beside = [*first_step(near[0], 1), *first_step(near[1], 0)]
    down_part = pick_down(info, received)
    down = lax.all_to_all(
        jnp.broadcast_to(down_part[None], (NE, 4, 16, 256)), "exp", 0, 0, tiled=True
    )
    *beside, down, gates = lax.optimization_barrier((*beside, down, gates))
    late = onward(beside, 1)
    up, sums = project_early(info, routes, tokens, [near[0], *beside[:2], near[1], *beside[2:]])
    *late, near_out[0], near_out[1] = lax.optimization_barrier((*late, *near_out))
    out_beside = [*first_step(near_out[0], 1), *first_step(near_out[1], 0)]
    lhs = attention(info, routes, down, tokens, up, sums, received, late)
    *out_beside, lhs = lax.optimization_barrier((*out_beside, lhs))
    out_late = onward(out_beside, 1)
    out_pieces = []
    for half in range(2):
        two = slice(half * 2, half * 2 + 2)
        out_pieces += [near_out[half], *out_beside[two], *out_late[two]]

    operands = (gates, lhs, out_pieces)
    far, far_mine, near_theirs = project_out(
        ((False, 2), (True, 2), (False, 0)), place, *operands, apart=True
    )
    far_swapped = exchange(far, 0)
    place = lax.optimization_barrier((place, far_mine))[0]
    (theirs,) = project_out(((False, 1), (False, 3)), place, *operands)
    swapped = exchange(theirs, 0)
    near_swapped = exchange(near_theirs, 0)
    low, high = small_call(far_sum_kernel, [(512, 256)] * 2, 1, far_mine, far_swapped)
    place = lax.optimization_barrier((place, theirs, low))[0]
    low, high = exchange(low, 1), exchange(high, -1)
    (mine,) = project_out(((True, 1), (True, 3)), place, *operands)
    ahead, behind = small_call(near_sum_kernel, [(1024, 256)] * 2, 2, mine, swapped, low, high)
    from_behind, from_ahead = exchange(ahead, 1), exchange(behind, -1)
    place = lax.optimization_barrier((place, ahead))[0]
    (own_block,) = project_out(((True, 0),), place, *operands)
    return rounded_sum(own_block[0], near_swapped, from_behind, from_ahead)


def solution(mesh):
    return jax.shard_map(
        body,
        mesh=mesh,
        in_specs=(
            P("req", None),
            P("req", None),
            P("req"),
            P("req"),
            P(),
            P("req"),
            P(),
            P(),
            P("req", "exp"),
            P("req", None, "exp"),
            P(None, "exp", "req"),
            P("req", None, None),
            P("req", None, "exp"),
            P("req", None, "exp"),
        ),
        out_specs=P("req", "exp"),
        check_vma=False,
    )
```
